32 devices in a mesh: batch: 16 (over z, y, x), tensor: 2 (over core).
Axes of the slice: x: 2, y: 2, z: 4, core: 2. Of those that a mesh axis runs over, the one named last changes fastest.
Arguments:
- features: bfloat16 [16, 1024, 1024], P('batch', 'tensor'), may hold values from -6 to 6
- lengths: int32 [16], P('batch'), may hold values from 256 to 1024, as said below
- norm_gains: bfloat16 [5, 1024], replicated, may hold values from 0.5 to 1.5
- norm_shifts: bfloat16 [5, 1024], replicated, may hold values from -3 to 3
- first_up: bfloat16 [1024, 4096], P(None, 'tensor'), may hold values from -0.1875 to 0.1875
- first_down: bfloat16 [4096, 1024], P('tensor'), may hold values from -0.1875 to 0.1875
- attention_in: bfloat16 [3, 1024, 1024], P(None, None, 'tensor'), may hold values from -0.1875 to 0.1875
- position_proj: bfloat16 [1024, 1024], P(None, 'tensor'), may hold values from -0.1875 to 0.1875
- position_bias: bfloat16 [2, 8, 128], P(None, 'tensor'), may hold values from -3 to 3
- attention_out: bfloat16 [1024, 1024], P('tensor'), may hold values from -0.75 to 0.75
- pointwise_in: bfloat16 [1024, 2, 1024], P(None, None, 'tensor'), may hold values from -0.1875 to 0.1875
- depthwise: bfloat16 [5, 1024], P(None, 'tensor'), may hold values from -2.5 to 2.5
- batch_gain: bfloat16 [1024], P('tensor'), may hold values from 0.5 to 1.5
- batch_shift: bfloat16 [1024], P('tensor'), may hold values from -3 to 3
- pointwise_out: bfloat16 [1024, 1024], P('tensor'), may hold values from -0.25 to 0.25
- second_up: bfloat16 [1024, 4096], P(None, 'tensor'), may hold values from -0.1875 to 0.1875
- second_down: bfloat16 [4096, 1024], P('tensor'), may hold values from -0.1875 to 0.1875
- cotangent: bfloat16 [16, 1024, 1024], P('batch', 'tensor'), may hold values from -6 to 6
Outputs:
- output: bfloat16 [16, 1024, 1024], P('batch', 'tensor')
- input_grad: float32 [16, 1024, 1024], P('batch', 'tensor')
- grad_norm_gains: float32 [5, 1024], replicated
- grad_norm_shifts: float32 [5, 1024], replicated
- grad_first_up: float32 [1024, 4096], P('batch', 'tensor')
- grad_first_down: float32 [4096, 1024], P('tensor', 'batch')
- grad_attention_in: float32 [3, 1024, 1024], P(None, 'batch', 'tensor')
- grad_position_proj: float32 [1024, 1024], P('batch', 'tensor')
- grad_position_bias: float32 [2, 8, 128], P(None, 'tensor')
- grad_attention_out: float32 [1024, 1024], P('tensor', 'batch')
- grad_pointwise_in: float32 [1024, 2, 1024], P('batch', None, 'tensor')
- grad_depthwise: float32 [5, 1024], P(None, 'tensor')
- grad_batch_gain: float32 [1024], P('tensor')
- grad_batch_shift: float32 [1024], P('tensor')
- grad_pointwise_out: float32 [1024, 1024], P('tensor', 'batch')
- grad_second_up: float32 [1024, 4096], P('batch', 'tensor')
- grad_second_down: float32 [4096, 1024], P('tensor', 'batch')
The draws below stay inside these ranges and needn't reach their ends.
Inputs may be any that keep to these rules, and one draw needn't show every extreme that they name: Frames from lengths[r] on are padding; in every draw some slot is full, holding 1024 frames, and some slot holds 256 frames.
All inputs are finite; a program needn't handle non-finite values.
Results may differ from the reference program's by a relative error of at most 0.03.
Values may be sent and summed in bfloat16 or wider, within the bound.
A program may use at most 320 MiB of HBM per device.

```python
import math
import jax
import jax.numpy as jnp
from jax import lax

D = 1024
HEADS = 8
HEAD = 128
FF = 4096
KERNEL = 5
LEN = 1024
ROWS = 16


def draw_lengths(key, part):
    first_key = jax.random.fold_in(key, 11)
    second_key = jax.random.fold_in(key, 12)
    common = jax.random.randint(first_key, (ROWS,), LEN // 4, LEN // 2 + 1)
    rare = jax.random.randint(second_key, (ROWS,), 0, 8)
    picked = jnp.where(rare == 0, LEN, common)
    picked = picked.at[ROWS - 1].set(LEN // 4)
    return picked.at[0].set(LEN).astype(jnp.int32)


def levels(own_key, dims, cuts, low, high):
    def one(position, parts):
        heights = jax.random.uniform(jax.random.fold_in(jax.random.fold_in(own_key, 6), position), (parts,), jnp.float32, low / len(cuts), high / len(cuts))
        return jnp.repeat(jnp.exp(heights), dims[position] // parts).reshape((-1,) + (1,) * (len(dims) - position - 1))

    factor_of = one(*cuts[0])
    for cut in cuts[1:]:
        factor_of = factor_of * one(*cut)
    return factor_of


def normal_values(rng, extent, width, bound, split=(), dtype=jnp.bfloat16):
    drawn = jax.random.normal(rng, extent, jnp.float32) * width
    if len(split) > 0:
        drawn = levels(rng, extent, split, -0.22, 0.18) * drawn
    return jnp.clip(drawn, min=-bound, max=bound).astype(dtype)


def setup_inputs(seed: int = 0) -> dict:
    key_list = jax.random.split(jax.random.key(seed), 19)
    return {
        "features": normal_values(key_list[0], (ROWS, LEN, D), 1.0, 6.0, ((0, 16), (1, 2))),
        "lengths": draw_lengths(jax.random.fold_in(key_list[18], 71), 0),
        "norm_gains": jnp.clip(1.0 + 0.1 * jax.random.normal(key_list[2], (5, D), jnp.float32), 0.5, 1.5).astype(jnp.bfloat16),
        "norm_shifts": normal_values(key_list[3], (5, D), 0.2, 3.0),
        "first_up": normal_values(key_list[4], (D, FF), D ** -0.5, 0.1875, ((1, 2),)),
        "first_down": normal_values(key_list[5], (FF, D), (FF // 4) ** -0.5, 0.1875, ((0, 2),)),
        "attention_in": normal_values(key_list[6], (3, D, D), D ** -0.5, 0.1875, ((2, 2),)),
        "position_proj": normal_values(key_list[7], (D, D), D ** -0.5, 0.1875, ((1, 2),)),
        "position_bias": normal_values(key_list[8], (2, HEADS, HEAD), 0.5, 3.0, ((1, 2),)),
        "attention_out": normal_values(key_list[9], (D, D), (D // 16) ** -0.5, 0.75, ((0, 2),)),
        "pointwise_in": normal_values(key_list[10], (D, 2, D), D ** -0.5, 0.1875, ((2, 2),)),
        "depthwise": normal_values(key_list[11], (KERNEL, D), KERNEL ** -0.5, 2.5, ((1, 2),)),
        "batch_gain": jnp.clip(1.0 + 0.1 * jax.random.normal(key_list[12], (D,), jnp.float32), 0.5, 1.5).astype(jnp.bfloat16),
        "batch_shift": normal_values(key_list[13], (D,), 0.2, 3.0, ((0, 2),)),
        "pointwise_out": normal_values(key_list[14], (D, D), (D // 2) ** -0.5, 0.25, ((0, 2),)),
        "second_up": normal_values(key_list[15], (D, FF), D ** -0.5, 0.1875, ((1, 2),)),
        "second_down": normal_values(key_list[16], (FF, D), (FF // 4) ** -0.5, 0.1875, ((0, 2),)),
        "cotangent": normal_values(key_list[17], (ROWS, LEN, D), 1.0, 6.0, ((0, 16), (1, 2))),
    }


@jax.custom_vjp
def low(v):
    return lax.optimization_barrier(v.astype(jnp.bfloat16)).astype(jnp.float32)

@jax.custom_vjp
def low_back(v):
    return v

def low_keep(v):
    return (low(v), None)

def low_pass(kept, grad):
    return (grad,)

def back_keep(v):
    return (v, None)

def back_low(kept, grad):
    return (low(grad),)
low.defvjp(low_keep, low_pass)
low_back.defvjp(back_keep, back_low)
eps_norm = 1e-05
eps_batch = 1e-05

def product(left, right):
    return jnp.dot(left, right, precision=lax.Precision.HIGHEST)

def layer_norm(values, norm_gain, norm_shift):
    center = values - lax.optimization_barrier(jnp.mean(values, axis=-1, keepdims=True))
    spread_sq = lax.optimization_barrier(jnp.mean(center * center, axis=-1, keepdims=True))
    return center * lax.rsqrt(spread_sq + eps_norm) * norm_gain + norm_shift

def swish(values):
    return values * jax.nn.sigmoid(values)

def relative_table(slot_frames, model_width):
    offsets = (slot_frames - 1 - jnp.arange(2 * slot_frames - 1)).astype(jnp.float32)
    column = jnp.arange(model_width // 2).astype(jnp.float32)
    freqs = jnp.exp(column * (-2.0 * math.log(10000.0) / model_width))
    angles = offsets[:, None] * freqs[None, :]
    return jnp.stack([jnp.sin(angles), jnp.cos(angles)], axis=-1).reshape(2 * slot_frames - 1, model_width)

def skew(wide, slot_frames):
    head_count, block_size, window_len = wide.shape
    flat_wide = wide.reshape(head_count, block_size * window_len)
    flat_wide = lax.slice_in_dim(flat_wide, block_size - 1, block_size - 1 + block_size * (window_len - 1), axis=1)
    return flat_wide.reshape(head_count, block_size, window_len - 1)[:, :, :slot_frames]

def attend_block(block_content, block_position, slot_keys, slot_values, table, block_start, length):
    block_size = block_content.shape[0]
    slot_frames = slot_keys.shape[0]
    window = lax.dynamic_slice_in_dim(table, (slot_frames - block_size - block_start).astype(jnp.int32), block_size + slot_frames - 1, 0)
    content = jnp.einsum('bhe,khe->hbk', block_content, slot_keys, precision=lax.Precision.HIGHEST)
    wide = jnp.einsum('bhe,whe->hbw', block_position, window, precision=lax.Precision.HIGHEST)
    raw = low_back(content + skew(wide, slot_frames))
    live_keys = jnp.arange(slot_frames) < length
    scores = jnp.where(live_keys[None, None, :], raw * block_content.shape[2] ** (-0.5), -jnp.inf)
    probs_soft = jax.nn.softmax(scores, axis=-1)
    return jnp.einsum('hbk,khe->bhe', low(probs_soft), slot_values, precision=lax.Precision.HIGHEST)

def attend_slot(pieces, table):
    slot_content, slot_position, slot_keys, slot_values, length = pieces
    slot_frames, head_count, head_size = slot_keys.shape
    block_size = min(512, slot_frames)
    block_count = slot_frames // block_size
    starts = (jnp.arange(block_count) * block_size).astype(jnp.int32)

    def one_block(block_args):
        return attend_block(block_args[0], block_args[1], slot_keys, slot_values, table, block_args[2], length)
    shaped = (block_count, block_size, head_count, head_size)
    blocks_out = lax.map(jax.checkpoint(one_block), (slot_content.reshape(shaped), slot_position.reshape(shaped), starts))
    return blocks_out.reshape(slot_frames, head_count, head_size)

def feed(flat_in, norm_gain, norm_shift, weight_up, weight_down):
    act_in = low(layer_norm(flat_in, norm_gain, norm_shift))
    pre_act = low_back(product(act_in, weight_up))
    return low_back(product(low(swish(pre_act)), weight_down))

def attention(flat_in, norm_gain, norm_shift, proj_heads, proj_table, bias_heads, proj_back, lengths, slot_count, slot_frames):
    model_width = flat_in.shape[1]
    head_count, head_size = (bias_heads.shape[1], bias_heads.shape[2])
    act_in = low(layer_norm(flat_in, norm_gain, norm_shift))
    query = low_back(product(act_in, proj_heads[0]))
    key_all = low(low_back(product(act_in, proj_heads[1])))
    value_all = low(low_back(product(act_in, proj_heads[2])))
    query_content = low(query + bias_heads[0].reshape(model_width))
    query_position = low(query + bias_heads[1].reshape(model_width))
    table = low(low_back(product(low(relative_table(slot_frames, model_width)), proj_table)))
    table = table.reshape(2 * slot_frames - 1, head_count, head_size)
    shaped = (slot_count, slot_frames, head_count, head_size)

    def slot_fn(pieces):
        return attend_slot(pieces, table)
    context = lax.map(jax.checkpoint(slot_fn), (query_content.reshape(shaped), query_position.reshape(shaped), key_all.reshape(shaped), value_all.reshape(shaped), lengths))
    context = low(low_back(context.reshape(slot_count * slot_frames, model_width)))
    return low_back(product(context, proj_back))

def convolution(flat_in, norm_gain, norm_shift, point_in, conv_taps, norm_scale, norm_offset, point_out, live_mask, slot_count, slot_frames):
    act_in = low(layer_norm(flat_in, norm_gain, norm_shift))
    value_half = low_back(product(act_in, point_in[:, 0, :]))
    gate_half = low_back(product(act_in, point_in[:, 1, :]))
    gated = value_half * jax.nn.sigmoid(gate_half) * live_mask
    channels = gated.shape[1]
    tap_count = conv_taps.shape[0]
    half_taps = tap_count // 2
    padded = jnp.pad(gated.reshape(slot_count, slot_frames, channels), ((0, 0), (half_taps, half_taps), (0, 0)))
    mixed_conv = padded[:, 0:slot_frames, :] * conv_taps[0]
    for tap_index in range(1, tap_count):
        mixed_conv = mixed_conv + padded[:, tap_index:tap_index + slot_frames, :] * conv_taps[tap_index]
    mixed_conv = mixed_conv.reshape(slot_count * slot_frames, channels)
    frame_count = jnp.sum(live_mask)
    batch_mean = lax.optimization_barrier(jnp.sum(mixed_conv * live_mask, axis=0)) / frame_count
    batch_square = lax.optimization_barrier(jnp.sum(mixed_conv * mixed_conv * live_mask, axis=0)) / frame_count
    inv_std = lax.rsqrt(batch_square - batch_mean * batch_mean + eps_batch)
    normed = (mixed_conv - batch_mean) * inv_std * norm_scale + norm_offset
    return low_back(product(low(swish(normed)), point_out))

def reference(features, lengths, norm_gains, norm_shifts, first_up, first_down, attention_in, position_proj, position_bias, attention_out, pointwise_in, depthwise, batch_gain, batch_shift, pointwise_out, second_up, second_down, cotangent):
    slot_count, slot_frames, model_width = features.shape
    frames = slot_count * slot_frames
    live_mask = (jnp.arange(slot_frames)[None, :] < lengths[:, None]).astype(jnp.float32).reshape(frames, 1)

    def forward(flat_in, gain_rows, shift_rows, up_first, down_first, proj_heads, proj_table, bias_heads, proj_back, point_in, conv_taps, norm_scale, norm_offset, point_out, up_second, down_second):
        hidden_one = flat_in + 0.5 * feed(flat_in, gain_rows[0], shift_rows[0], up_first, down_first)
        hidden_two = hidden_one + attention(hidden_one, gain_rows[1], shift_rows[1], proj_heads, proj_table, bias_heads, proj_back, lengths, slot_count, slot_frames)
        hidden_three = hidden_two + convolution(hidden_two, gain_rows[2], shift_rows[2], point_in, conv_taps, norm_scale, norm_offset, point_out, live_mask, slot_count, slot_frames)
        hidden_four = hidden_three + 0.5 * feed(hidden_three, gain_rows[3], shift_rows[3], up_second, down_second)
        return layer_norm(hidden_four, gain_rows[4], shift_rows[4]) * live_mask
    primals = (features.reshape(frames, model_width).astype(jnp.float32), norm_gains.astype(jnp.float32), norm_shifts.astype(jnp.float32), first_up.astype(jnp.float32), first_down.astype(jnp.float32), attention_in.astype(jnp.float32), position_proj.astype(jnp.float32), position_bias.astype(jnp.float32), attention_out.astype(jnp.float32), pointwise_in.astype(jnp.float32), depthwise.astype(jnp.float32), batch_gain.astype(jnp.float32), batch_shift.astype(jnp.float32), pointwise_out.astype(jnp.float32), second_up.astype(jnp.float32), second_down.astype(jnp.float32))
    result, pullback = jax.vjp(forward, *primals)
    grads = pullback(cotangent.reshape(frames, model_width).astype(jnp.float32))
    return (result.reshape(slot_count, slot_frames, model_width).astype(jnp.bfloat16), grads[0].reshape(slot_count, slot_frames, model_width), grads[1], grads[2], grads[3], grads[4], grads[5], grads[6], grads[7], grads[8], grads[9], grads[10], grads[11], grads[12], grads[13], grads[14], grads[15])
```

```python
import functools
import math

import jax
import jax.numpy as jnp
import numpy as np
from jax import lax
from jax.experimental import pallas as pl
from jax.experimental.pallas import tpu as pltpu
from jax.sharding import PartitionSpec as P

eps_norm = 1e-05
eps_batch = 1e-05


def contract_rows(left, right):
    return lax.dot_general(
        left, right, (((0,), (0,)), ((), ())), preferred_element_type=jnp.float32
    )


def times_transposed(left, right):
    return lax.dot_general(
        left, right, (((1,), (1,)), ((), ())), preferred_element_type=jnp.float32
    )


def norm_forward(values, norm_gain, norm_shift):
    center = values - jnp.mean(values, axis=-1, keepdims=True)
    inv_std = lax.rsqrt(jnp.mean(center * center, axis=-1, keepdims=True) + eps_norm)
    scaled = center * inv_std
    return (scaled * norm_gain + norm_shift, scaled, inv_std)


def norm_backward(grad_out, scaled, inv_std, norm_gain):
    grad_scaled = grad_out * norm_gain
    grad_in = inv_std * (
        grad_scaled
        - jnp.mean(grad_scaled, axis=-1, keepdims=True)
        - scaled * jnp.mean(grad_scaled * scaled, axis=-1, keepdims=True)
    )
    return (grad_in, jnp.sum(grad_out * scaled, axis=(0, 1)), jnp.sum(grad_out, axis=(0, 1)))


def widen(normed):
    return lax.all_gather(normed.astype(jnp.bfloat16), "tensor", axis=1, tiled=True)


def narrow(partial_out):
    return lax.psum_scatter(
        partial_out.astype(jnp.bfloat16), "tensor", scatter_dimension=1, tiled=True
    ).astype(jnp.float32)


def widen_grad(grad_half):
    return lax.all_gather(grad_half.astype(jnp.bfloat16), "tensor", axis=1, tiled=True)


def narrow_grad(partial_grad):
    return lax.psum_scatter(
        partial_grad.astype(jnp.bfloat16), "tensor", scatter_dimension=1, tiled=True
    ).astype(jnp.float32)


def scatter_batch(grad, dimension):
    return lax.psum_scatter(
        grad.astype(jnp.bfloat16), "batch", scatter_dimension=dimension, tiled=True
    ).astype(jnp.float32)


def relative_table(slot_frames, model_width):
    step = min(32, slot_frames)
    column = np.arange(model_width)
    freqs = np.exp((column // 2) * (-2.0 * math.log(10000.0) / model_width))
    coarse = (slot_frames - 1 - step * np.arange(2 * slot_frames // step))[:, None] * freqs + (column % 2) * (
        np.pi / 2
    )
    fine = np.arange(step)[:, None] * freqs
    parts = [jnp.asarray(part, jnp.float32) for part in (np.sin(coarse), np.cos(coarse), np.cos(fine), np.sin(fine))]
    table = parts[0][:, None, :] * parts[2][None] - parts[1][:, None, :] * parts[3][None]
    return table.reshape(2 * slot_frames, model_width).astype(jnp.bfloat16)


def dot_nn(a, b):
    return lax.dot_general(a, b, (((1,), (0,)), ((), ())), preferred_element_type=jnp.float32)
def dot_nt(a, b):
    return lax.dot_general(a, b, (((1,), (1,)), ((), ())), preferred_element_type=jnp.float32)
def dot_tn(a, b):
    return lax.dot_general(a, b, (((0,), (0,)), ((), ())), preferred_element_type=jnp.float32)

def flip_rows(x):
    order = 7 - lax.broadcasted_iota(jnp.int32, (8, x.shape[1]), 0)
    return jnp.concatenate(
        [jnp.take_along_axis(x[at : at + 8], order, axis=0) for at in range(x.shape[0] - 8, -8, -8)], axis=0)

def attend_kernel(frames, block, lengths, content, position, keys, values, table, context, probs):
    wide_len = frames + block
    start = pl.multiple_of(frames - block - pl.program_id(1) * block, block)
    window = table[pl.ds(start, wide_len), :]
    wide = dot_nt(position[...], window)
    skewed = pltpu.roll(wide, frames + 1, 1, stride=1, stride_axis=0)[:, :frames]
    raw = (dot_nt(content[...], keys[...]) + skewed) * (content.shape[1] ** -0.5)
    live = lax.broadcasted_iota(jnp.int32, (1, frames), 1) < lengths[0]
    scores = jnp.where(live, raw, -jnp.inf)
    weight = jnp.exp(scores - jnp.max(scores, axis=1, keepdims=True))
    soft = (weight / jnp.sum(weight, axis=1, keepdims=True)).astype(jnp.bfloat16)
    probs[0] = soft
    context[...] = dot_nn(soft, values[...]).astype(jnp.bfloat16)

def attend(lengths, content, position, keys, values, table, head, block):
    frames, width = content.shape
    heads = width // head
    rows = pl.BlockSpec((block, head), lambda h, i, *_: (i, h))
    whole = pl.BlockSpec((frames, head), lambda h, i, *_: (0, h))
    return pl.pallas_call(
        functools.partial(attend_kernel, frames, block),
        out_shape=(jax.ShapeDtypeStruct((frames, width), jnp.bfloat16), jax.ShapeDtypeStruct((heads, frames, frames), jnp.bfloat16)),
        grid_spec=pltpu.PrefetchScalarGridSpec(
            num_scalar_prefetch=1, grid=(heads, frames // block),
            in_specs=[rows, rows, whole, whole, pl.BlockSpec((2 * frames, head), lambda h, i, *_: (0, h))],
            out_specs=[rows, pl.BlockSpec((1, block, frames), lambda h, i, *_: (h, i, 0))]),
        name="attend",
    )(lengths, content, position, keys, values, table)

def attend_back_kernel(frames, block, probs, grad_context, content, position, keys, values, table, grad_query, grad_keys, grad_values, grad_table, grad_bias, key_sum, value_sum, table_sum):
    wide_len = frames + block
    step = pl.program_id(1)
    start = pl.multiple_of(frames - block - step * block, block)
    @pl.when(step == 0)
    def _():
        key_sum[...] = jnp.zeros_like(key_sum)
        value_sum[...] = jnp.zeros_like(value_sum)
        table_sum[...] = jnp.zeros_like(table_sum)
        grad_bias[...] = jnp.zeros_like(grad_bias)
    soft = probs[0]
    grad_out = grad_context[...]
    grad_probs = dot_nt(grad_out, values[...])
    wide_soft = soft.astype(jnp.float32)
    delta = jnp.sum(wide_soft * grad_probs, axis=1, keepdims=True)
    grad_raw = wide_soft * (grad_probs - delta) * (content.shape[1] ** -0.5)
    padded = jnp.concatenate([flip_rows(grad_raw), jnp.zeros((block, block), jnp.float32)], axis=1)
    grad_wide = pltpu.roll(padded, 0, 1, stride=1, stride_axis=0).astype(jnp.bfloat16)
    grad_raw = grad_raw.astype(jnp.bfloat16)
    from_content = dot_nn(grad_raw, keys[...])
    from_position = dot_nn(grad_wide, table[pl.ds(start, wide_len), :])
    from_position = flip_rows(from_position)
    grad_query[...] = (from_content + from_position).astype(jnp.bfloat16)
    grad_bias[0:1, :] += jnp.sum(from_content, axis=0, keepdims=True)
    grad_bias[1:2, :] += jnp.sum(from_position, axis=0, keepdims=True)
    key_sum[...] += dot_tn(content[...], grad_raw)
    value_sum[...] += dot_tn(grad_out, soft)
    table_sum[:, pl.ds(start, wide_len)] += dot_tn(flip_rows(position[...].astype(jnp.float32)).astype(jnp.bfloat16), grad_wide)
    @pl.when(step == pl.num_programs(1) - 1)
    def _():
        grad_keys[...] = key_sum[...].T.astype(jnp.bfloat16)
        grad_values[...] = value_sum[...].T.astype(jnp.bfloat16)
        grad_table[...] = table_sum[...].T.astype(jnp.bfloat16)

def attend_back(probs, grad_context, content, position, keys, values, table, head, block):
    frames, width = content.shape
    heads = width // head
    rows = pl.BlockSpec((block, head), lambda h, i: (i, h))
    whole = pl.BlockSpec((frames, head), lambda h, i: (0, h))
    both = pl.BlockSpec((2 * frames, head), lambda h, i: (0, h))
    out = functools.partial(jax.ShapeDtypeStruct, dtype=jnp.bfloat16)
    return pl.pallas_call(
        functools.partial(attend_back_kernel, frames, block),
        out_shape=(out((frames, width)), out((frames, width)), out((frames, width)), out((2 * frames, width)), jax.ShapeDtypeStruct((8, width), jnp.float32)),
        grid=(heads, frames // block),
        in_specs=[pl.BlockSpec((1, block, frames), lambda h, i: (h, i, 0)), rows, rows, rows, whole, whole, both],
        out_specs=[rows, whole, whole, both, pl.BlockSpec((8, head), lambda h, i: (0, h))],
        scratch_shapes=[pltpu.VMEM((head, frames), jnp.float32), pltpu.VMEM((head, frames), jnp.float32), pltpu.VMEM((head, 2 * frames), jnp.float32)],
        name="attend_back",
    )(probs, grad_context, content, position, keys, values, table)


def ffn_forward(residual, norm_gain, norm_shift, weight_up, weight_down):
    normed, scaled, inv_std = norm_forward(residual, norm_gain, norm_shift)
    gathered = widen(normed)
    slot_count, slot_frames, model_width = gathered.shape
    flat_act = gathered.reshape(slot_count * slot_frames, model_width)
    pre_act = jnp.dot(flat_act, weight_up, preferred_element_type=jnp.float32)
    hidden = (pre_act * jax.nn.sigmoid(pre_act)).astype(jnp.bfloat16)
    partial_out = jnp.dot(hidden, weight_down, preferred_element_type=jnp.float32).reshape(
        slot_count, slot_frames, model_width
    )
    return (narrow(partial_out), (scaled, inv_std, flat_act, pre_act, hidden))


def ffn_backward(grad_after, saved, norm_gain, weight_up, weight_down):
    scaled, inv_std, flat_act, pre_act, hidden = saved
    grad_round = widen_grad(grad_after)
    slot_count, slot_frames, model_width = grad_round.shape
    grad_flat = grad_round.reshape(slot_count * slot_frames, model_width)
    grad_down = contract_rows(hidden, grad_flat)
    grad_hidden = times_transposed(grad_flat, weight_down)
    gate_sig = jax.nn.sigmoid(pre_act)
    grad_pre = (grad_hidden * gate_sig * (1.0 + pre_act * (1.0 - gate_sig))).astype(jnp.bfloat16)
    grad_up = contract_rows(flat_act, grad_pre)
    grad_act = times_transposed(grad_pre, weight_up).reshape(slot_count, slot_frames, model_width)
    grad_resid, grad_gain, grad_shift = norm_backward(
        narrow_grad(grad_act), scaled, inv_std, norm_gain
    )
    return (grad_resid, grad_gain, grad_shift, grad_up, grad_down)


def attn_forward(
    residual,
    norm_gain,
    norm_shift,
    attention_in,
    position_proj,
    position_bias,
    attention_out,
    lengths,
):
    normed, scaled, inv_std = norm_forward(residual, norm_gain, norm_shift)
    gathered = widen(normed)
    slot_count, slot_frames, model_width = gathered.shape
    flat_act = gathered.reshape(slot_count * slot_frames, model_width)
    head_count, head_size = (position_bias.shape[1], position_bias.shape[2])
    local_width = head_count * head_size
    projected = jnp.einsum(
        "fd,sdc->sfc", flat_act, attention_in, preferred_element_type=jnp.float32
    )
    biases = position_bias.astype(jnp.float32).reshape(2, 1, local_width)
    query_content = (projected[0] + biases[0]).astype(jnp.bfloat16)
    query_position = (projected[0] + biases[1]).astype(jnp.bfloat16)
    key_all = projected[1].astype(jnp.bfloat16)
    value_all = projected[2].astype(jnp.bfloat16)
    table_in = relative_table(slot_frames, model_width)
    table = jnp.dot(table_in, position_proj, preferred_element_type=jnp.float32).astype(jnp.bfloat16)
    context, probs = attend(
        lengths, query_content, query_position, key_all, value_all, table, head_size, min(256, slot_frames)
    )
    partial_out = jnp.dot(context, attention_out, preferred_element_type=jnp.float32).reshape(
        slot_count, slot_frames, model_width
    )
    saved = (
        scaled,
        inv_std,
        flat_act,
        query_content,
        query_position,
        key_all,
        value_all,
        table_in,
        table,
        context,
        probs,
    )
    return (narrow(partial_out), saved)


def attn_backward(grad_after, saved, norm_gain, attention_in, attention_out, head_count, head_size):
    (
        scaled,
        inv_std,
        flat_act,
        query_content,
        query_position,
        key_all,
        value_all,
        table_in,
        table,
        context,
        probs,
    ) = saved
    grad_round = widen_grad(grad_after)
    slot_count, slot_frames, model_width = grad_round.shape
    frames = slot_count * slot_frames
    grad_flat = grad_round.reshape(frames, model_width)
    grad_back_proj = contract_rows(context, grad_flat)
    grad_context = times_transposed(grad_flat, attention_out).astype(jnp.bfloat16)
    grad_query, grad_keys, grad_values, grad_table, grad_bias = attend_back(
        probs,
        grad_context,
        query_content,
        query_position,
        key_all,
        value_all,
        table,
        head_size,
        min(256, slot_frames),
    )
    grad_bias = grad_bias[:2].reshape(2, head_count, head_size)
    grad_proj = (grad_query, grad_keys, grad_values)
    grad_in_proj = jnp.stack([contract_rows(flat_act, part) for part in grad_proj])
    grad_act = sum(times_transposed(part, attention_in[at]) for at, part in enumerate(grad_proj)).reshape(
        slot_count, slot_frames, model_width
    )
    grad_table_proj = contract_rows(table_in, grad_table)
    grad_resid, grad_gain, grad_shift = norm_backward(
        narrow_grad(grad_act), scaled, inv_std, norm_gain
    )
    return (
        grad_resid,
        grad_gain,
        grad_shift,
        grad_in_proj,
        grad_table_proj,
        grad_bias,
        grad_back_proj,
    )


def conv_forward(
    residual,
    norm_gain,
    norm_shift,
    pointwise_in,
    depthwise,
    batch_gain,
    batch_shift,
    pointwise_out,
    lengths,
    live_full,
):
    normed, scaled, inv_std = norm_forward(residual, norm_gain, norm_shift)
    gathered = widen(normed)
    slot_count, slot_frames, model_width = gathered.shape
    flat_act = gathered.reshape(slot_count * slot_frames, model_width)
    both_halves = jnp.einsum(
        "fd,dsc->sfc", flat_act, pointwise_in, preferred_element_type=jnp.float32
    )
    gate_sig = jax.nn.sigmoid(both_halves[1])
    gated = both_halves[0] * gate_sig * live_full
    channels = gated.shape[1]
    kernel = depthwise.astype(jnp.float32)
    tap_count = kernel.shape[0]
    half_taps = tap_count // 2
    padded = jnp.pad(
        gated.reshape(slot_count, slot_frames, channels), ((0, 0), (half_taps, half_taps), (0, 0))
    )
    mixed_conv = padded[:, 0:slot_frames, :] * kernel[0]
    for tap_index in range(1, tap_count):
        mixed_conv = (
            mixed_conv + padded[:, tap_index : tap_index + slot_frames, :] * kernel[tap_index]
        )
    mixed_conv = mixed_conv.reshape(slot_count * slot_frames, channels)
    totals = lax.psum(
        (
            jnp.sum(mixed_conv * live_full, axis=0),
            jnp.sum(mixed_conv * mixed_conv * live_full, axis=0),
            jnp.sum(lengths).astype(jnp.float32),
        ),
        "batch",
    )
    frame_count = totals[2]
    batch_mean = totals[0] / frame_count
    batch_inv = lax.rsqrt(totals[1] / frame_count - batch_mean * batch_mean + eps_batch)
    centered = (mixed_conv - batch_mean) * batch_inv
    normed_batch = centered * batch_gain.astype(jnp.float32) + batch_shift.astype(jnp.float32)
    batch_sig = jax.nn.sigmoid(normed_batch)
    swished = (normed_batch * batch_sig).astype(jnp.bfloat16)
    partial_out = jnp.dot(swished, pointwise_out, preferred_element_type=jnp.float32).reshape(
        slot_count, slot_frames, model_width
    )
    saved = (
        scaled,
        inv_std,
        flat_act,
        both_halves,
        gate_sig,
        padded,
        centered,
        batch_inv,
        frame_count,
        normed_batch,
        batch_sig,
        swished,
    )
    return (narrow(partial_out), saved)


def conv_backward(
    grad_after, saved, norm_gain, pointwise_in, depthwise, batch_gain, pointwise_out, live_full
):
    (
        scaled,
        inv_std,
        flat_act,
        both_halves,
        gate_sig,
        padded,
        centered,
        batch_inv,
        frame_count,
        normed_batch,
        batch_sig,
        swished,
    ) = saved
    grad_round = widen_grad(grad_after)
    slot_count, slot_frames, model_width = grad_round.shape
    grad_flat = grad_round.reshape(slot_count * slot_frames, model_width)
    grad_point_out = contract_rows(swished, grad_flat)
    grad_swished = times_transposed(grad_flat, pointwise_out)
    grad_normed = grad_swished * batch_sig * (1.0 + normed_batch * (1.0 - batch_sig))
    sums = lax.psum(
        (jnp.sum(grad_normed, axis=0), jnp.sum(grad_normed * centered, axis=0)), "batch"
    )
    gamma = batch_gain.astype(jnp.float32)
    grad_mixed = batch_inv * (
        grad_normed * gamma
        - live_full * (gamma * sums[0] + centered * gamma * sums[1]) / frame_count
    )
    channels = grad_mixed.shape[1]
    kernel = depthwise.astype(jnp.float32)
    tap_count = kernel.shape[0]
    half_taps = tap_count // 2
    grad_mixed3 = grad_mixed.reshape(slot_count, slot_frames, channels)
    grad_kernel = jnp.stack(
        [
            jnp.sum(grad_mixed3 * padded[:, tap_index : tap_index + slot_frames, :], axis=(0, 1))
            for tap_index in range(tap_count)
        ]
    )
    spread = jnp.pad(grad_mixed3, ((0, 0), (half_taps, half_taps), (0, 0)))
    grad_gated = spread[:, 2 * half_taps : 2 * half_taps + slot_frames, :] * kernel[0]
    for tap_index in range(1, tap_count):
        begin = 2 * half_taps - tap_index
        grad_gated = grad_gated + spread[:, begin : begin + slot_frames, :] * kernel[tap_index]
    grad_gated = grad_gated.reshape(slot_count * slot_frames, channels) * live_full
    grad_halves = jnp.stack(
        [grad_gated * gate_sig, grad_gated * both_halves[0] * gate_sig * (1.0 - gate_sig)]
    ).astype(jnp.bfloat16)
    grad_point_in = jnp.einsum(
        "fd,sfc->dsc", flat_act, grad_halves, preferred_element_type=jnp.float32
    )
    grad_act = jnp.einsum(
        "sfc,dsc->fd", grad_halves, pointwise_in, preferred_element_type=jnp.float32
    ).reshape(slot_count, slot_frames, model_width)
    grad_resid, grad_gain, grad_shift = norm_backward(
        narrow_grad(grad_act), scaled, inv_std, norm_gain
    )
    return (grad_resid, grad_gain, grad_shift, grad_point_in, grad_point_out, grad_kernel, sums)


def per_device(
    features,
    lengths,
    norm_gains,
    norm_shifts,
    first_up,
    first_down,
    attention_in,
    position_proj,
    position_bias,
    attention_out,
    pointwise_in,
    depthwise,
    batch_gain,
    batch_shift,
    pointwise_out,
    second_up,
    second_down,
    cotangent,
):
    slot_count, half_frames, model_width = features.shape
    slot_frames = half_frames * lax.axis_size("tensor")
    positions = (
        lax.broadcasted_iota(jnp.int32, (slot_count, half_frames), 1)
        + lax.axis_index("tensor") * half_frames
    )
    live_half = (positions < lengths[:, None]).astype(jnp.float32)[:, :, None]
    full_positions = lax.broadcasted_iota(jnp.int32, (slot_count, slot_frames), 1)
    live_full = (
        (full_positions < lengths[:, None]).astype(jnp.float32).reshape(slot_count * slot_frames, 1)
    )
    gain_rows = norm_gains.astype(jnp.float32)
    shift_rows = norm_shifts.astype(jnp.float32)
    stream_zero = features.astype(jnp.float32)
    branch_one, saved_one = ffn_forward(
        stream_zero, gain_rows[0], shift_rows[0], first_up, first_down
    )
    stream_one = stream_zero + 0.5 * branch_one
    branch_two, saved_two = attn_forward(
        stream_one,
        gain_rows[1],
        shift_rows[1],
        attention_in,
        position_proj,
        position_bias,
        attention_out,
        lengths,
    )
    stream_two = stream_one + branch_two
    branch_three, saved_three = conv_forward(
        stream_two,
        gain_rows[2],
        shift_rows[2],
        pointwise_in,
        depthwise,
        batch_gain,
        batch_shift,
        pointwise_out,
        lengths,
        live_full,
    )
    stream_three = stream_two + branch_three
    branch_four, saved_four = ffn_forward(
        stream_three, gain_rows[3], shift_rows[3], second_up, second_down
    )
    stream_four = stream_three + 0.5 * branch_four
    final_norm, scaled_final, inv_final = norm_forward(stream_four, gain_rows[4], shift_rows[4])
    output = (final_norm * live_half).astype(jnp.bfloat16)
    grad_final = cotangent.astype(jnp.float32) * live_half
    grad_stream, gain_five, shift_five = norm_backward(
        grad_final, scaled_final, inv_final, gain_rows[4]
    )
    grad_branch, gain_four, shift_four, up_two, down_two = ffn_backward(
        0.5 * grad_stream, saved_four, gain_rows[3], second_up, second_down
    )
    grad_stream = grad_stream + grad_branch
    grad_branch, gain_three, shift_three, point_in_grad, point_out_grad, kernel_grad, batch_sums = (
        conv_backward(
            grad_stream,
            saved_three,
            gain_rows[2],
            pointwise_in,
            depthwise,
            batch_gain,
            pointwise_out,
            live_full,
        )
    )
    grad_stream = grad_stream + grad_branch
    grad_branch, gain_two, shift_two, heads_grad, table_grad, bias_grad, back_grad = attn_backward(
        grad_stream,
        saved_two,
        gain_rows[1],
        attention_in,
        attention_out,
        position_bias.shape[1],
        position_bias.shape[2],
    )
    grad_stream = grad_stream + grad_branch
    grad_branch, gain_one, shift_one, up_one, down_one = ffn_backward(
        0.5 * grad_stream, saved_one, gain_rows[0], first_up, first_down
    )
    (
        up_one,
        down_one,
        heads_grad,
        table_grad,
        back_grad,
        point_in_grad,
        point_out_grad,
        up_two,
        down_two,
    ) = (
        scatter_batch(up_one, 0),
        scatter_batch(down_one, 1),
        scatter_batch(heads_grad, 1),
        scatter_batch(table_grad, 0),
        scatter_batch(back_grad, 1),
        scatter_batch(point_in_grad, 0),
        scatter_batch(point_out_grad, 1),
        scatter_batch(up_two, 0),
        scatter_batch(down_two, 1),
    )
    grad_stream = grad_stream + grad_branch
    gain_grads = jnp.stack([gain_one, gain_two, gain_three, gain_four, gain_five])
    shift_grads = jnp.stack([shift_one, shift_two, shift_three, shift_four, shift_five])
    gain_grads, shift_grads = lax.psum((gain_grads, shift_grads), ("batch", "tensor"))
    bias_grad, kernel_grad = lax.psum((bias_grad, kernel_grad), "batch")
    return (
        output,
        grad_stream,
        gain_grads,
        shift_grads,
        up_one,
        down_one,
        heads_grad,
        table_grad,
        bias_grad,
        back_grad,
        point_in_grad,
        kernel_grad,
        batch_sums[1],
        batch_sums[0],
        point_out_grad,
        up_two,
        down_two,
    )


def solution(mesh):
    in_specs = (
        P("batch", "tensor", None),
        P("batch"),
        P(),
        P(),
        P(None, "tensor"),
        P("tensor", None),
        P(None, None, "tensor"),
        P(None, "tensor"),
        P(None, "tensor", None),
        P("tensor", None),
        P(None, None, "tensor"),
        P(None, "tensor"),
        P("tensor"),
        P("tensor"),
        P("tensor", None),
        P(None, "tensor"),
        P("tensor", None),
        P("batch", "tensor", None),
    )
    out_specs = (
        P("batch", "tensor", None),
        P("batch", "tensor", None),
        P(),
        P(),
        P("batch", "tensor"),
        P("tensor", "batch"),
        P(None, "batch", "tensor"),
        P("batch", "tensor"),
        P(None, "tensor", None),
        P("tensor", "batch"),
        P("batch", None, "tensor"),
        P(None, "tensor"),
        P("tensor"),
        P("tensor"),
        P("tensor", "batch"),
        P("batch", "tensor"),
        P("tensor", "batch"),
    )
    return jax.shard_map(
        per_device, mesh=mesh, in_specs=in_specs, out_specs=out_specs, check_vma=False
    )
```

```python
import functools
import math

import jax
import jax.numpy as jnp
import numpy as np
from jax import lax
from jax.experimental import pallas as pl
from jax.experimental.pallas import tpu as pltpu
from jax.sharding import PartitionSpec as P

eps_norm = 1e-05
eps_batch = 1e-05


def contract_rows(left, right):
    return lax.dot_general(
        left, right, (((0,), (0,)), ((), ())), preferred_element_type=jnp.float32
    )


def times_transposed(left, right):
    return lax.dot_general(
        left, right, (((1,), (1,)), ((), ())), preferred_element_type=jnp.float32
    )


def norm_forward(values, norm_gain, norm_shift):
    center = values - jnp.mean(values, axis=-1, keepdims=True)
    inv_std = lax.rsqrt(jnp.mean(center * center, axis=-1, keepdims=True) + eps_norm)
    scaled = center * inv_std
    return (scaled * norm_gain + norm_shift, scaled, inv_std)


def norm_backward(grad_out, scaled, inv_std, norm_gain):
    grad_scaled = grad_out * norm_gain
    grad_in = inv_std * (
        grad_scaled
        - jnp.mean(grad_scaled, axis=-1, keepdims=True)
        - scaled * jnp.mean(grad_scaled * scaled, axis=-1, keepdims=True)
    )
    return (grad_in, jnp.sum(grad_out * scaled, axis=0), jnp.sum(grad_out, axis=0))


def swap(half):
    return lax.ppermute(half, "tensor", [(0, 1), (1, 0)])


def in_order(own, peer):
    first = lax.axis_index("tensor") == 0
    return jnp.concatenate([jnp.where(first, own, peer), jnp.where(first, peer, own)], axis=0)


def split_own(whole):
    half = whole.shape[0] // 2
    side = lax.axis_index("tensor")
    return (
        lax.dynamic_slice_in_dim(whole, side * half, half, 0),
        lax.dynamic_slice_in_dim(whole, (1 - side) * half, half, 0),
    )


def narrow(own, peer):
    return own + swap(peer.astype(jnp.bfloat16)).astype(jnp.float32)


def exchange(values, axis):
    size = lax.axis_size(axis)
    reach = 1
    while reach < size:
        radix = 4 if size % (reach * 4) == 0 else 2
        got = [
            lax.ppermute(values, axis, [(at, at ^ (reach * other)) for at in range(size)])
            for other in range(1, radix)
        ]
        values = sum(got, values)
        reach *= radix
    return values


def pick(term, bit, axis):
    return lax.dynamic_index_in_dim(term, bit, axis, keepdims=False)


def total(terms):
    return sum((term.astype(jnp.float32) for term in terms[1:]), terms[0].astype(jnp.float32))


def halve(grad, order):
    size = lax.axis_size("batch")
    index = lax.axis_index("batch")
    rows, columns = grad.shape
    left = list(range(size.bit_length() - 1))[::-1]
    terms = [grad.reshape((2,) * len(left) + (rows // size, columns))]
    for bit in order:
        axis = left.index(bit)
        mine = (index // 2**bit) % 2
        outgoing = total([pick(term, 1 - mine, axis) for term in terms]).astype(jnp.bfloat16)
        got = lax.ppermute(outgoing, "batch", [(at, at ^ 2**bit) for at in range(size)])
        terms = [pick(term, mine, axis) for term in terms] + [got]
        left.remove(bit)
    return total(terms)


def scatter_batch(grad, kind):
    bits = list(range(lax.axis_size("batch").bit_length() - 1))
    orders = {"x": bits, "y": [1, 0] + bits[2:], "z": bits[2:] + bits[:2]}
    return halve(grad.astype(jnp.bfloat16), orders[kind])


def scatter_mixed(grad, kind):
    cut = grad.shape[1] * 3 // 4
    grad = grad.astype(jnp.bfloat16)
    return jnp.concatenate([scatter_batch(grad[:, :cut], kind), scatter_batch(grad[:, cut:], "z")], axis=1)


def relative_table(slot_frames, model_width):
    step = min(32, slot_frames)
    column = np.arange(model_width)
    freqs = np.exp((column // 2) * (-2.0 * math.log(10000.0) / model_width))
    coarse = (slot_frames - 1 - step * np.arange(2 * slot_frames // step))[:, None] * freqs + (column % 2) * (
        np.pi / 2
    )
    fine = np.arange(step)[:, None] * freqs
    parts = [jnp.asarray(part, jnp.float32) for part in (np.sin(coarse), np.cos(coarse), np.cos(fine), np.sin(fine))]
    table = parts[0][:, None, :] * parts[2][None] - parts[1][:, None, :] * parts[3][None]
    return table.reshape(2 * slot_frames, model_width).astype(jnp.bfloat16)


def dot_nn(a, b):
    return lax.dot_general(a, b, (((1,), (0,)), ((), ())), preferred_element_type=jnp.float32)
def dot_nt(a, b):
    return lax.dot_general(a, b, (((1,), (1,)), ((), ())), preferred_element_type=jnp.float32)
def dot_tn(a, b):
    return lax.dot_general(a, b, (((0,), (0,)), ((), ())), preferred_element_type=jnp.float32)

def flip_rows(x):
    order = 7 - lax.broadcasted_iota(jnp.int32, (8, x.shape[1]), 0)
    return jnp.concatenate(
        [jnp.take_along_axis(x[at : at + 8], order, axis=0) for at in range(x.shape[0] - 8, -8, -8)], axis=0)

def attend_kernel(frames, block, lengths, content, position, keys, values, table, context, probs):
    wide_len = frames + block
    start = pl.multiple_of(frames - block - pl.program_id(1) * block, block)
    window = table[pl.ds(start, wide_len), :]
    wide = dot_nt(position[...], window)
    skewed = pltpu.roll(wide, frames + 1, 1, stride=1, stride_axis=0)[:, :frames]
    raw = (dot_nt(content[...], keys[...]) + skewed) * (content.shape[1] ** -0.5)
    live = lax.broadcasted_iota(jnp.int32, (1, frames), 1) < lengths[0]
    scores = jnp.where(live, raw, -jnp.inf)
    weight = jnp.exp(scores - jnp.max(scores, axis=1, keepdims=True))
    soft = (weight / jnp.sum(weight, axis=1, keepdims=True)).astype(jnp.bfloat16)
    probs[0] = soft
    context[...] = dot_nn(soft, values[...]).astype(jnp.bfloat16)

def attend(lengths, content, position, keys, values, table, head, block):
    frames, width = content.shape
    heads = width // head
    rows = pl.BlockSpec((block, head), lambda h, i, *_: (i, h))
    whole = pl.BlockSpec((frames, head), lambda h, i, *_: (0, h))
    return pl.pallas_call(
        functools.partial(attend_kernel, frames, block),
        out_shape=(jax.ShapeDtypeStruct((frames, width), jnp.bfloat16), jax.ShapeDtypeStruct((heads, frames, frames), jnp.bfloat16)),
        grid_spec=pltpu.PrefetchScalarGridSpec(
            num_scalar_prefetch=1, grid=(heads, frames // block),
            in_specs=[rows, rows, whole, whole, pl.BlockSpec((2 * frames, head), lambda h, i, *_: (0, h))],
            out_specs=[rows, pl.BlockSpec((1, block, frames), lambda h, i, *_: (h, i, 0))]),
        name="attend",
    )(lengths, content, position, keys, values, table)

def attend_back_kernel(frames, block, probs, grad_context, content, position, keys, values, table, grad_query, grad_keys, grad_values, grad_table, grad_bias, key_sum, value_sum, table_sum):
    wide_len = frames + block
    step = pl.program_id(1)
    start = pl.multiple_of(frames - block - step * block, block)
    @pl.when(step == 0)
    def _():
        key_sum[...] = jnp.zeros_like(key_sum)
        value_sum[...] = jnp.zeros_like(value_sum)
        table_sum[...] = jnp.zeros_like(table_sum)
        grad_bias[...] = jnp.zeros_like(grad_bias)
    soft = probs[0]
    grad_out = grad_context[...]
    grad_probs = dot_nt(grad_out, values[...])
    wide_soft = soft.astype(jnp.float32)
    delta = jnp.sum(wide_soft * grad_probs, axis=1, keepdims=True)
    grad_raw = wide_soft * (grad_probs - delta) * (content.shape[1] ** -0.5)
    padded = jnp.concatenate([flip_rows(grad_raw), jnp.zeros((block, block), jnp.float32)], axis=1)
    grad_wide = pltpu.roll(padded, 0, 1, stride=1, stride_axis=0).astype(jnp.bfloat16)
    grad_raw = grad_raw.astype(jnp.bfloat16)
    from_content = dot_nn(grad_raw, keys[...])
    from_position = dot_nn(grad_wide, table[pl.ds(start, wide_len), :])
    from_position = flip_rows(from_position)
    grad_query[...] = (from_content + from_position).astype(jnp.bfloat16)
    grad_bias[0:1, :] += jnp.sum(from_content, axis=0, keepdims=True)
    grad_bias[1:2, :] += jnp.sum(from_position, axis=0, keepdims=True)
    key_sum[...] += dot_tn(content[...], grad_raw)
    value_sum[...] += dot_tn(grad_out, soft)
    table_sum[:, pl.ds(start, wide_len)] += dot_tn(flip_rows(position[...].astype(jnp.float32)).astype(jnp.bfloat16), grad_wide)
    @pl.when(step == pl.num_programs(1) - 1)
    def _():
        grad_keys[...] = key_sum[...].T.astype(jnp.bfloat16)
        grad_values[...] = value_sum[...].T.astype(jnp.bfloat16)
        grad_table[...] = table_sum[...].T.astype(jnp.bfloat16)

def attend_back(probs, grad_context, content, position, keys, values, table, head, block):
    frames, width = content.shape
    heads = width // head
    rows = pl.BlockSpec((block, head), lambda h, i: (i, h))
    whole = pl.BlockSpec((frames, head), lambda h, i: (0, h))
    both = pl.BlockSpec((2 * frames, head), lambda h, i: (0, h))
    out = functools.partial(jax.ShapeDtypeStruct, dtype=jnp.bfloat16)
    return pl.pallas_call(
        functools.partial(attend_back_kernel, frames, block),
        out_shape=(out((frames, width)), out((frames, width)), out((frames, width)), out((2 * frames, width)), jax.ShapeDtypeStruct((8, width), jnp.float32)),
        grid=(heads, frames // block),
        in_specs=[pl.BlockSpec((1, block, frames), lambda h, i: (h, i, 0)), rows, rows, rows, whole, whole, both],
        out_specs=[rows, whole, whole, both, pl.BlockSpec((8, head), lambda h, i: (0, h))],
        scratch_shapes=[pltpu.VMEM((head, frames), jnp.float32), pltpu.VMEM((head, frames), jnp.float32), pltpu.VMEM((head, 2 * frames), jnp.float32)],
        name="attend_back",
    )(probs, grad_context, content, position, keys, values, table)


def ffn_forward(residual, norm_gain, norm_shift, weight_up, weight_down):
    normed, scaled, inv_std = norm_forward(residual, norm_gain, norm_shift)
    act_own = normed.astype(jnp.bfloat16)
    act_peer = swap(act_own)

    def hidden_of(act):
        pre_act = jnp.dot(act, weight_up, preferred_element_type=jnp.float32)
        gate_sig = jax.nn.sigmoid(pre_act)
        slope = gate_sig * (1.0 + pre_act * (1.0 - gate_sig))
        return ((pre_act * gate_sig).astype(jnp.bfloat16), slope.astype(jnp.bfloat16))

    hidden_own, slope_own = hidden_of(act_own)
    hidden_peer, slope_peer = hidden_of(act_peer)
    out_peer = jnp.dot(hidden_peer, weight_down, preferred_element_type=jnp.float32)
    out_own = jnp.dot(hidden_own, weight_down, preferred_element_type=jnp.float32)
    saved = (scaled, inv_std, act_own, act_peer, hidden_own, hidden_peer, slope_own, slope_peer)
    return (narrow(out_own, out_peer), saved)


def ffn_backward(grad_after, saved, norm_gain, weight_up, weight_down):
    scaled, inv_std, act_own, act_peer, hidden_own, hidden_peer, slope_own, slope_peer = saved
    grad_own = grad_after.astype(jnp.bfloat16)
    grad_peer = swap(grad_own)
    pre_own = (times_transposed(grad_own, weight_down) * slope_own.astype(jnp.float32)).astype(jnp.bfloat16)
    pre_peer = (times_transposed(grad_peer, weight_down) * slope_peer.astype(jnp.float32)).astype(jnp.bfloat16)
    back_peer = times_transposed(pre_peer, weight_up)
    back_own = times_transposed(pre_own, weight_up)
    grad_down = contract_rows(grad_own, hidden_own) + contract_rows(grad_peer, hidden_peer)
    grad_up = contract_rows(act_own, pre_own) + contract_rows(act_peer, pre_peer)
    grad_resid, grad_gain, grad_shift = norm_backward(
        narrow(back_own, back_peer), scaled, inv_std, norm_gain
    )
    return (grad_resid, grad_gain, grad_shift, scatter_mixed(grad_up, "x"), scatter_mixed(grad_down, "y").T)


def attn_forward(
    residual,
    norm_gain,
    norm_shift,
    attention_in,
    position_proj,
    position_bias,
    attention_out,
    lengths,
):
    normed, scaled, inv_std = norm_forward(residual, norm_gain, norm_shift)
    own = normed.astype(jnp.bfloat16)
    flat_act = in_order(own, swap(own))
    slot_frames, model_width = flat_act.shape
    head_count, head_size = (position_bias.shape[1], position_bias.shape[2])
    local_width = head_count * head_size
    projected = [
        jnp.dot(flat_act, attention_in[at], preferred_element_type=jnp.float32) for at in range(3)
    ]
    biases = position_bias.astype(jnp.float32).reshape(2, 1, local_width)
    query_content = (projected[0] + biases[0]).astype(jnp.bfloat16)
    query_position = (projected[0] + biases[1]).astype(jnp.bfloat16)
    key_all = projected[1].astype(jnp.bfloat16)
    value_all = projected[2].astype(jnp.bfloat16)
    table_in = relative_table(slot_frames, model_width)
    table = jnp.dot(table_in, position_proj, preferred_element_type=jnp.float32).astype(jnp.bfloat16)
    context, probs = attend(
        lengths, query_content, query_position, key_all, value_all, table, head_size, min(256, slot_frames)
    )
    context_own, context_peer = split_own(context)
    out_peer = jnp.dot(context_peer, attention_out, preferred_element_type=jnp.float32)
    out_own = jnp.dot(context_own, attention_out, preferred_element_type=jnp.float32)
    saved = (
        scaled,
        inv_std,
        flat_act,
        query_content,
        query_position,
        key_all,
        value_all,
        table_in,
        table,
        context,
        probs,
    )
    return (narrow(out_own, out_peer), saved)


def attn_backward(grad_after, saved, norm_gain, attention_in, attention_out, head_count, head_size):
    (
        scaled,
        inv_std,
        flat_act,
        query_content,
        query_position,
        key_all,
        value_all,
        table_in,
        table,
        context,
        probs,
    ) = saved
    grad_own = grad_after.astype(jnp.bfloat16)
    grad_flat = in_order(grad_own, swap(grad_own))
    slot_frames = grad_flat.shape[0]
    grad_back_proj = contract_rows(grad_flat, context)
    grad_context = times_transposed(grad_flat, attention_out).astype(jnp.bfloat16)
    grad_query, grad_keys, grad_values, grad_table, grad_bias = attend_back(
        probs,
        grad_context,
        query_content,
        query_position,
        key_all,
        value_all,
        table,
        head_size,
        min(256, slot_frames),
    )
    grad_bias = grad_bias[:2].reshape(2, head_count, head_size)
    grad_proj = (grad_query, grad_keys, grad_values)
    halves = [split_own(part) for part in grad_proj]
    back_own, back_peer = (
        sum(times_transposed(half[side], attention_in[at]) for at, half in enumerate(halves))
        for side in (0, 1)
    )
    grad_in_proj = jnp.concatenate([contract_rows(flat_act, part) for part in grad_proj], axis=1)
    grad_in_proj = scatter_batch(grad_in_proj, "y")
    grad_in_proj = jnp.stack(jnp.split(grad_in_proj, 3, axis=1))
    grad_table_proj = contract_rows(table_in, grad_table)
    grad_resid, grad_gain, grad_shift = norm_backward(
        narrow(back_own, back_peer), scaled, inv_std, norm_gain
    )
    return (
        grad_resid,
        grad_gain,
        grad_shift,
        grad_in_proj,
        scatter_batch(grad_table_proj, "z"),
        grad_bias,
        scatter_batch(grad_back_proj, "z").T,
    )


def conv_forward(
    residual,
    norm_gain,
    norm_shift,
    pointwise_in,
    depthwise,
    batch_gain,
    batch_shift,
    pointwise_out,
    frame_count,
    live_full,
):
    normed, scaled, inv_std = norm_forward(residual, norm_gain, norm_shift)
    own = normed.astype(jnp.bfloat16)
    flat_act = in_order(own, swap(own))
    slot_frames = flat_act.shape[0]
    both_halves = [
        jnp.dot(flat_act, pointwise_in[:, at], preferred_element_type=jnp.float32) for at in range(2)
    ]
    gate_sig = jax.nn.sigmoid(both_halves[1])
    gated = both_halves[0] * gate_sig * live_full
    channels = gated.shape[1]
    kernel = depthwise.astype(jnp.float32)
    tap_count = kernel.shape[0]
    half_taps = tap_count // 2
    padded = jnp.pad(gated, ((half_taps, half_taps), (0, 0)))
    mixed_conv = padded[0:slot_frames] * kernel[0]
    for tap_index in range(1, tap_count):
        mixed_conv = mixed_conv + padded[tap_index : tap_index + slot_frames] * kernel[tap_index]
    totals = exchange(
        jnp.stack([jnp.sum(mixed_conv * live_full, axis=0), jnp.sum(mixed_conv * mixed_conv * live_full, axis=0)]),
        "batch",
    )
    batch_mean = totals[0] / frame_count
    batch_inv = lax.rsqrt(totals[1] / frame_count - batch_mean * batch_mean + eps_batch)
    centered = (mixed_conv - batch_mean) * batch_inv
    normed_batch = centered * batch_gain.astype(jnp.float32) + batch_shift.astype(jnp.float32)
    batch_sig = jax.nn.sigmoid(normed_batch)
    swished = (normed_batch * batch_sig).astype(jnp.bfloat16)
    swished_own, swished_peer = split_own(swished)
    out_peer = jnp.dot(swished_peer, pointwise_out, preferred_element_type=jnp.float32)
    out_own = jnp.dot(swished_own, pointwise_out, preferred_element_type=jnp.float32)
    saved = (
        scaled,
        inv_std,
        flat_act,
        both_halves,
        gate_sig,
        padded,
        centered,
        batch_inv,
        frame_count,
        normed_batch,
        batch_sig,
        swished,
    )
    return (narrow(out_own, out_peer), saved)


def conv_backward(
    grad_after, saved, norm_gain, pointwise_in, depthwise, batch_gain, pointwise_out, live_full
):
    (
        scaled,
        inv_std,
        flat_act,
        both_halves,
        gate_sig,
        padded,
        centered,
        batch_inv,
        frame_count,
        normed_batch,
        batch_sig,
        swished,
    ) = saved
    grad_own = grad_after.astype(jnp.bfloat16)
    grad_flat = in_order(grad_own, swap(grad_own))
    slot_frames = grad_flat.shape[0]
    grad_point_out = scatter_batch(contract_rows(grad_flat, swished), "x").T
    grad_swished = times_transposed(grad_flat, pointwise_out)
    grad_normed = grad_swished * batch_sig * (1.0 + normed_batch * (1.0 - batch_sig))
    sums = exchange(
        jnp.stack([jnp.sum(grad_normed, axis=0), jnp.sum(grad_normed * centered, axis=0)]), "batch"
    )
    gamma = batch_gain.astype(jnp.float32)
    grad_mixed = batch_inv * (
        grad_normed * gamma
        - live_full * (gamma * sums[0] + centered * gamma * sums[1]) / frame_count
    )
    channels = grad_mixed.shape[1]
    kernel = depthwise.astype(jnp.float32)
    tap_count = kernel.shape[0]
    half_taps = tap_count // 2
    grad_kernel = jnp.stack(
        [
            jnp.sum(grad_mixed * padded[tap_index : tap_index + slot_frames], axis=0)
            for tap_index in range(tap_count)
        ]
    )
    spread = jnp.pad(grad_mixed, ((half_taps, half_taps), (0, 0)))
    grad_gated = spread[2 * half_taps : 2 * half_taps + slot_frames] * kernel[0]
    for tap_index in range(1, tap_count):
        begin = 2 * half_taps - tap_index
        grad_gated = grad_gated + spread[begin : begin + slot_frames] * kernel[tap_index]
    grad_gated = grad_gated * live_full
    grad_halves = [
        (grad_gated * gate_sig).astype(jnp.bfloat16),
        (grad_gated * both_halves[0] * gate_sig * (1.0 - gate_sig)).astype(jnp.bfloat16),
    ]
    grad_point_in = jnp.concatenate([contract_rows(flat_act, part) for part in grad_halves], axis=1)
    grad_point_in = scatter_batch(grad_point_in, "x")
    grad_point_in = grad_point_in.reshape(grad_point_in.shape[0], 2, channels)
    halves = [split_own(part) for part in grad_halves]
    back_own, back_peer = (
        sum(times_transposed(half[side], pointwise_in[:, at]) for at, half in enumerate(halves))
        for side in (0, 1)
    )
    grad_resid, grad_gain, grad_shift = norm_backward(
        narrow(back_own, back_peer), scaled, inv_std, norm_gain
    )
    return (grad_resid, grad_gain, grad_shift, grad_point_in, grad_point_out, grad_kernel, sums)


def per_device(
    features,
    lengths,
    norm_gains,
    norm_shifts,
    first_up,
    first_down,
    attention_in,
    position_proj,
    position_bias,
    attention_out,
    pointwise_in,
    depthwise,
    batch_gain,
    batch_shift,
    pointwise_out,
    second_up,
    second_down,
    cotangent,
):
    slot_count, half_frames, model_width = features.shape
    slot_frames = half_frames * lax.axis_size("tensor")
    positions = lax.broadcasted_iota(jnp.int32, (half_frames, 1), 0) + lax.axis_index("tensor") * half_frames
    live_half = (positions < lengths[0]).astype(jnp.float32)
    full_positions = lax.broadcasted_iota(jnp.int32, (slot_frames, 1), 0)
    live_full = (full_positions < lengths[0]).astype(jnp.float32)
    frame_count = exchange(jnp.broadcast_to(lengths.astype(jnp.float32), (8, 128)), "batch")[0, 0]
    gain_rows = norm_gains.astype(jnp.float32)
    shift_rows = norm_shifts.astype(jnp.float32)
    stream_zero = features[0].astype(jnp.float32)
    branch_one, saved_one = ffn_forward(
        stream_zero, gain_rows[0], shift_rows[0], first_up, first_down
    )
    stream_one = stream_zero + 0.5 * branch_one
    branch_two, saved_two = attn_forward(
        stream_one,
        gain_rows[1],
        shift_rows[1],
        attention_in,
        position_proj,
        position_bias,
        attention_out,
        lengths,
    )
    stream_two = stream_one + branch_two
    branch_three, saved_three = conv_forward(
        stream_two,
        gain_rows[2],
        shift_rows[2],
        pointwise_in,
        depthwise,
        batch_gain,
        batch_shift,
        pointwise_out,
        frame_count,
        live_full,
    )
    stream_three = stream_two + branch_three
    branch_four, saved_four = ffn_forward(
        stream_three, gain_rows[3], shift_rows[3], second_up, second_down
    )
    stream_four = stream_three + 0.5 * branch_four
    final_norm, scaled_final, inv_final = norm_forward(stream_four, gain_rows[4], shift_rows[4])
    output = (final_norm * live_half).astype(jnp.bfloat16)
    grad_final = cotangent[0].astype(jnp.float32) * live_half
    grad_stream, gain_five, shift_five = norm_backward(
        grad_final, scaled_final, inv_final, gain_rows[4]
    )
    grad_branch, gain_four, shift_four, up_two, down_two = ffn_backward(
        0.5 * grad_stream, saved_four, gain_rows[3], second_up, second_down
    )
    grad_stream = grad_stream + grad_branch
    grad_branch, gain_three, shift_three, point_in_grad, point_out_grad, kernel_grad, batch_sums = (
        conv_backward(
            grad_stream,
            saved_three,
            gain_rows[2],
            pointwise_in,
            depthwise,
            batch_gain,
            pointwise_out,
            live_full,
        )
    )
    grad_stream = grad_stream + grad_branch
    grad_branch, gain_two, shift_two, heads_grad, table_grad, bias_grad, back_grad = attn_backward(
        grad_stream,
        saved_two,
        gain_rows[1],
        attention_in,
        attention_out,
        position_bias.shape[1],
        position_bias.shape[2],
    )
    grad_stream = grad_stream + grad_branch
    grad_branch, gain_one, shift_one, up_one, down_one = ffn_backward(
        0.5 * grad_stream, saved_one, gain_rows[0], first_up, first_down
    )
    grad_stream = grad_stream + grad_branch
    early = exchange(
        exchange(jnp.stack([gain_two, gain_three, gain_four, gain_five, shift_two, shift_three, shift_four, shift_five]), "batch"),
        "tensor",
    )
    late = exchange(exchange(jnp.stack([gain_one, shift_one]), "batch"), "tensor")
    gain_grads = jnp.concatenate([late[:1], early[:4]])
    shift_grads = jnp.concatenate([late[1:], early[4:]])
    channels = kernel_grad.shape[1]
    head_grads = exchange(jnp.concatenate([kernel_grad, bias_grad.reshape(2, channels)]), "batch")
    kernel_grad = head_grads[:-2]
    bias_grad = head_grads[-2:].reshape(bias_grad.shape)
    return (
        output[None],
        grad_stream[None],
        gain_grads,
        shift_grads,
        up_one,
        down_one,
        heads_grad,
        table_grad,
        bias_grad,
        back_grad,
        point_in_grad,
        kernel_grad,
        batch_sums[1],
        batch_sums[0],
        point_out_grad,
        up_two,
        down_two,
    )


def solution(mesh):
    in_specs = (
        P("batch", "tensor", None),
        P("batch"),
        P(),
        P(),
        P(None, "tensor"),
        P("tensor", None),
        P(None, None, "tensor"),
        P(None, "tensor"),
        P(None, "tensor", None),
        P("tensor", None),
        P(None, None, "tensor"),
        P(None, "tensor"),
        P("tensor"),
        P("tensor"),
        P("tensor", None),
        P(None, "tensor"),
        P("tensor", None),
        P("batch", "tensor", None),
    )
    out_specs = (
        P("batch", "tensor", None),
        P("batch", "tensor", None),
        P(),
        P(),
        P("batch", "tensor"),
        P("tensor", "batch"),
        P(None, "batch", "tensor"),
        P("batch", "tensor"),
        P(None, "tensor", None),
        P("tensor", "batch"),
        P("batch", None, "tensor"),
        P(None, "tensor"),
        P("tensor"),
        P("tensor"),
        P("tensor", "batch"),
        P("batch", "tensor"),
        P("tensor", "batch"),
    )
    return jax.shard_map(
        per_device, mesh=mesh, in_specs=in_specs, out_specs=out_specs, check_vma=False
    )
```

```python
import functools
import math

import jax
import jax.numpy as jnp
import numpy as np
from jax import lax
from jax.experimental import pallas as pl
from jax.experimental.pallas import tpu as pltpu
from jax.sharding import PartitionSpec as P

eps_norm = 1e-05
eps_batch = 1e-05


def contract_rows(left, right):
    return lax.dot_general(
        left, right, (((0,), (0,)), ((), ())), preferred_element_type=jnp.float32
    )


def times_transposed(left, right):
    return lax.dot_general(
        left, right, (((1,), (1,)), ((), ())), preferred_element_type=jnp.float32
    )


def norm_forward(values, norm_gain, norm_shift):
    center = values - jnp.mean(values, axis=-1, keepdims=True)
    inv_std = lax.rsqrt(jnp.mean(center * center, axis=-1, keepdims=True) + eps_norm)
    scaled = center * inv_std
    return (scaled * norm_gain + norm_shift, scaled, inv_std)


def norm_backward(grad_out, scaled, inv_std, norm_gain):
    grad_scaled = grad_out * norm_gain
    grad_in = inv_std * (
        grad_scaled
        - jnp.mean(grad_scaled, axis=-1, keepdims=True)
        - scaled * jnp.mean(grad_scaled * scaled, axis=-1, keepdims=True)
    )
    return (grad_in, jnp.sum(grad_out * scaled, axis=0), jnp.sum(grad_out, axis=0))


def swap(half):
    return lax.ppermute(half, "tensor", [(0, 1), (1, 0)])


def in_order(own, peer):
    first = lax.axis_index("tensor") == 0
    return jnp.concatenate([jnp.where(first, own, peer), jnp.where(first, peer, own)], axis=0)


def split_own(whole):
    half = whole.shape[0] // 2
    side = lax.axis_index("tensor")
    return (
        lax.dynamic_slice_in_dim(whole, side * half, half, 0),
        lax.dynamic_slice_in_dim(whole, (1 - side) * half, half, 0),
    )


def narrow(own, peer):
    return own + swap(peer.astype(jnp.bfloat16)).astype(jnp.float32)


def after(value, tie):
    return lax.optimization_barrier((value, tie))[0]


def exchange(values, axis, fillers=()):
    size = lax.axis_size(axis)
    fillers, filled = list(fillers), []
    reach = 1
    while reach < size:
        radix = 4 if size % (reach * 4) == 0 else 2
        got = [
            lax.ppermute(values, axis, [(at, at ^ (reach * other)) for at in range(size)])
            for other in range(1, radix)
        ]
        if fillers:
            *got, work = lax.optimization_barrier((*got, fillers.pop(0)(values)))
            filled.append(work)
        values = sum(got, values)
        reach *= radix
    for filler in fillers:
        filled.append(filler(values))
    return values, filled


def scatter_batch(grad):
    return lax.psum_scatter(
        grad.astype(jnp.bfloat16), "batch", scatter_dimension=0, tiled=True
    ).astype(jnp.float32)


chunk_width = 512


def reduce_plan(size, chunk_count):
    bits = list(range(size.bit_length() - 1))
    kinds = (bits, [1, 0] + bits[2:], bits[2:] + bits[:2])
    few = max(1, round(chunk_count * 2 / 9))
    orders = []
    for at in range(chunk_count):
        orders.append(kinds[2] if at % 4 == 3 and sum(o is kinds[2] for o in orders) < few else None)
    plain = [at for at in range(chunk_count) if orders[at] is None]
    for turn, at in enumerate(plain):
        orders[at] = kinds[turn % 2]
    free, arrivals, events = {}, [], []

    def issue(chunk, stage, now):
        bit = orders[chunk][stage]
        link = min(bit, 2)
        cost = 2.0 ** -(stage + 1) * (2 if bit >= 3 else 1)
        free[link] = max(free.get(link, 0.0), now) + cost
        arrivals.append((free[link] + 0.05, chunk, stage))

    def issue_small(stage, now):
        link = min(stage, 2) if stage < len(bits) else 3
        free[link] = max(free.get(link, 0.0), now) + 0.03
        arrivals.append((free[link] + 0.1, -1, stage))

    issue_small(0, 0.0)
    for chunk in range(chunk_count):
        issue(chunk, 0, 0.0)
    while arrivals:
        arrivals.sort()
        now, chunk, stage = arrivals.pop(0)
        events.append((chunk, stage + 1))
        if chunk < 0 and stage < len(bits):
            issue_small(stage + 1, now)
        elif chunk >= 0 and stage + 1 < len(bits):
            issue(chunk, stage + 1, now)
    return orders, events


def reduce_kernel(size, places, pair_rows, *refs):
    stages = size.bit_length() - 1
    orders, events = reduce_plan(size, len(places))
    count = max(at for at, _ in places) + 1
    grads, small, out, small_out = refs[:count], refs[count], refs[count + 1], refs[count + 2]
    refs = refs[count + 3 :]
    landed = refs[:stages]
    leaving = (None,) + tuple(refs[stages : 2 * stages - 1])
    small_sum, small_landed, sent, arrived, small_sent, small_arrived = refs[2 * stages - 1 :]
    rows = out.shape[0]
    me = lax.axis_index("batch")
    mine = [lax.rem(me // 2**bit, 2) for bit in range(stages)]

    def shard(block):
        return sum(2**bit * lax.rem(mine[bit] + (block >> bit) % 2, 2) for bit in range(stages))

    barrier = pltpu.get_barrier_semaphore()
    for bit in range(stages):
        pl.semaphore_signal(barrier, inc=1, device_id={"batch": shard(2**bit)}, device_id_type=pl.DeviceIdType.MESH)
    peer = {"tensor": 1 - lax.axis_index("tensor")}
    pl.semaphore_signal(barrier, inc=1, device_id=peer, device_id_type=pl.DeviceIdType.MESH)
    pl.semaphore_wait(barrier, stages + 1)

    def blocks(chunk, stage):
        order = orders[chunk]
        return [
            block
            for block in range(size)
            if (block >> order[stage]) % 2 and not any((block >> bit) % 2 for bit in order[:stage])
        ]

    def copy(chunk, stage, source, target):
        return pltpu.make_async_remote_copy(
            src_ref=source,
            dst_ref=target,
            send_sem=sent.at[chunk, stage],
            recv_sem=arrived.at[chunk, stage],
            device_id={"batch": shard(2 ** orders[chunk][stage])},
            device_id_type=pl.DeviceIdType.MESH,
        )

    def columns(chunk):
        return pl.ds(places[chunk][1], chunk_width)

    def summed(chunk, block, stage, tile):
        total = grads[places[chunk][0]][shard(block), tile, columns(chunk)].astype(jnp.float32)
        for past in range(stage):
            at = blocks(chunk, past).index(block | (1 << orders[chunk][past]))
            total = total + landed[past][chunk, at, tile, :].astype(jnp.float32)
        return total

    def whole(chunk, stage):
        return copy(chunk, stage, landed[stage].at[chunk], landed[stage].at[chunk])

    def small_copy(stage):
        rows = pl.ds(0, small.shape[0] if stage < stages else pair_rows)
        return pltpu.make_async_remote_copy(
            src_ref=(small if stage == 0 else small_sum.at[stage]).at[rows],
            dst_ref=small_landed.at[stage, rows],
            send_sem=small_sent.at[stage],
            recv_sem=small_arrived.at[stage],
            device_id={"batch": shard(2**stage)} if stage < stages else peer,
            device_id_type=pl.DeviceIdType.MESH,
        )

    small_copy(0).start()
    for chunk in range(len(places)):
        for at, block in enumerate(blocks(chunk, 0)):
            copy(
                chunk, 0, grads[places[chunk][0]].at[shard(block), :, columns(chunk)], landed[0].at[chunk, at]
            ).start()

    step = min(16, rows)
    for chunk, stage in events:
        if chunk < 0:
            small_copy(stage - 1).wait_recv()
            held = small[...] if stage == 1 else small_sum[stage - 1]
            if stage <= stages:
                small_sum[stage] = held + small_landed[stage - 1]
                small_copy(stage).start()
            else:
                small_out[:pair_rows, :] = held[:pair_rows] + small_landed[stages, :pair_rows, :]
                small_out[pair_rows:, :] = held[pair_rows:]
            continue
        whole(chunk, stage - 1).wait_recv()

        def work(tile_index, carry, chunk=chunk, stage=stage):
            tile = pl.ds(pl.multiple_of(tile_index * step, step), step)
            if stage < stages:
                for at, block in enumerate(blocks(chunk, stage)):
                    leaving[stage][chunk, at, tile, :] = summed(chunk, block, stage, tile).astype(jnp.bfloat16)
            else:
                out[tile, pl.ds(chunk * chunk_width, chunk_width)] = summed(chunk, 0, stage, tile)
            return carry

        lax.fori_loop(0, rows // step, work, 0)
        if stage < stages:
            copy(chunk, stage, leaving[stage].at[chunk], landed[stage].at[chunk]).start()
    for stage in range(stages + 1):
        small_copy(stage).wait_send()
    for chunk in range(len(places)):
        for stage in range(stages):
            whole(chunk, stage).wait_send()


def reduce_rows(grads, small, pair_rows):
    size = lax.axis_size("batch")
    stages = size.bit_length() - 1
    rows = grads[0].shape[0] // size
    places = [(at, begin) for at, grad in enumerate(grads) for begin in range(0, grad.shape[1], chunk_width)]
    chunks = len(places)
    total_width = chunks * chunk_width
    halves = [pltpu.VMEM((chunks, size >> (stage + 1), rows, chunk_width), jnp.bfloat16) for stage in range(stages)]
    vmem = pl.BlockSpec(memory_space=pltpu.VMEM)
    return pl.pallas_call(
        functools.partial(reduce_kernel, size, places, pair_rows),
        out_shape=(jax.ShapeDtypeStruct((rows, total_width), jnp.float32), jax.ShapeDtypeStruct(small.shape, jnp.float32)),
        in_specs=[vmem] * (len(grads) + 1),
        out_specs=(vmem, vmem),
        scratch_shapes=halves
        + halves[1:]
        + [pltpu.VMEM((stages + 1,) + small.shape, jnp.float32)] * 2
        + [pltpu.SemaphoreType.DMA((chunks, stages))] * 2
        + [pltpu.SemaphoreType.DMA((stages + 1,))] * 2,
        compiler_params=pltpu.CompilerParams(
            collective_id=1, has_side_effects=True, vmem_limit_bytes=60 * 1024 * 1024
        ),
        name="reduce_rows",
    )(*[grad.reshape(size, rows, grad.shape[1]) for grad in grads], small)


def finish_sums(grads, small, pair_rows):
    if grads[0].shape[0] // lax.axis_size("batch") % 16 == 0 and not any(grad.shape[1] % chunk_width for grad in grads):
        return reduce_rows(grads, small, pair_rows)
    small, _ = exchange(small, "batch")
    paired, _ = exchange(small[:pair_rows], "tensor")
    return scatter_batch(jnp.concatenate(grads, axis=1)), jnp.concatenate([paired, small[pair_rows:]])


def relative_table(slot_frames, model_width):
    step = min(32, slot_frames)
    column = np.arange(model_width)
    freqs = np.exp((column // 2) * (-2.0 * math.log(10000.0) / model_width))
    coarse = (slot_frames - 1 - step * np.arange(2 * slot_frames // step))[:, None] * freqs + (column % 2) * (
        np.pi / 2
    )
    fine = np.arange(step)[:, None] * freqs
    parts = [jnp.asarray(part, jnp.float32) for part in (np.sin(coarse), np.cos(coarse), np.cos(fine), np.sin(fine))]
    table = parts[0][:, None, :] * parts[2][None] - parts[1][:, None, :] * parts[3][None]
    return table.reshape(2 * slot_frames, model_width).astype(jnp.bfloat16)


def dot_nn(a, b):
    return lax.dot_general(a, b, (((1,), (0,)), ((), ())), preferred_element_type=jnp.float32)
def dot_nt(a, b):
    return lax.dot_general(a, b, (((1,), (1,)), ((), ())), preferred_element_type=jnp.float32)
def dot_tn(a, b):
    return lax.dot_general(a, b, (((0,), (0,)), ((), ())), preferred_element_type=jnp.float32)

def flip_rows(x):
    order = 7 - lax.broadcasted_iota(jnp.int32, (8, x.shape[1]), 0)
    return jnp.concatenate(
        [jnp.take_along_axis(x[at : at + 8], order, axis=0) for at in range(x.shape[0] - 8, -8, -8)], axis=0)

def attend_kernel(frames, block, lengths, content, position, keys, values, table, context, probs):
    wide_len = frames + block
    start = pl.multiple_of(frames - block - pl.program_id(1) * block, block)
    window = table[pl.ds(start, wide_len), :]
    wide = dot_nt(position[...], window)
    skewed = pltpu.roll(wide, frames + 1, 1, stride=1, stride_axis=0)[:, :frames]
    raw = (dot_nt(content[...], keys[...]) + skewed) * (content.shape[1] ** -0.5)
    live = lax.broadcasted_iota(jnp.int32, (1, frames), 1) < lengths[0]
    scores = jnp.where(live, raw, -jnp.inf)
    weight = jnp.exp(scores - jnp.max(scores, axis=1, keepdims=True))
    soft = (weight / jnp.sum(weight, axis=1, keepdims=True)).astype(jnp.bfloat16)
    probs[0] = soft
    context[...] = dot_nn(soft, values[...]).astype(jnp.bfloat16)

def attend(lengths, content, position, keys, values, table, head, block):
    frames, width = content.shape
    heads = width // head
    rows = pl.BlockSpec((block, head), lambda h, i, *_: (i, h))
    whole = pl.BlockSpec((frames, head), lambda h, i, *_: (0, h))
    return pl.pallas_call(
        functools.partial(attend_kernel, frames, block),
        out_shape=(jax.ShapeDtypeStruct((frames, width), jnp.bfloat16), jax.ShapeDtypeStruct((heads, frames, frames), jnp.bfloat16)),
        grid_spec=pltpu.PrefetchScalarGridSpec(
            num_scalar_prefetch=1, grid=(heads, frames // block),
            in_specs=[rows, rows, whole, whole, pl.BlockSpec((2 * frames, head), lambda h, i, *_: (0, h))],
            out_specs=[rows, pl.BlockSpec((1, block, frames), lambda h, i, *_: (h, i, 0))]),
        name="attend",
    )(lengths, content, position, keys, values, table)

def attend_back_kernel(frames, block, probs, grad_context, content, position, keys, values, table, grad_query, grad_keys, grad_values, grad_table, grad_bias, key_sum, value_sum, table_sum):
    wide_len = frames + block
    step = pl.program_id(1)
    start = pl.multiple_of(frames - block - step * block, block)
    @pl.when(step == 0)
    def _():
        key_sum[...] = jnp.zeros_like(key_sum)
        value_sum[...] = jnp.zeros_like(value_sum)
        table_sum[...] = jnp.zeros_like(table_sum)
        grad_bias[...] = jnp.zeros_like(grad_bias)
    soft = probs[0]
    grad_out = grad_context[...]
    grad_probs = dot_nt(grad_out, values[...])
    wide_soft = soft.astype(jnp.float32)
    delta = jnp.sum(wide_soft * grad_probs, axis=1, keepdims=True)
    grad_raw = wide_soft * (grad_probs - delta) * (content.shape[1] ** -0.5)
    padded = jnp.concatenate([flip_rows(grad_raw), jnp.zeros((block, block), jnp.float32)], axis=1)
    grad_wide = pltpu.roll(padded, 0, 1, stride=1, stride_axis=0).astype(jnp.bfloat16)
    grad_raw = grad_raw.astype(jnp.bfloat16)
    from_content = dot_nn(grad_raw, keys[...])
    from_position = dot_nn(grad_wide, table[pl.ds(start, wide_len), :])
    from_position = flip_rows(from_position)
    grad_query[...] = (from_content + from_position).astype(jnp.bfloat16)
    grad_bias[0:1, :] += jnp.sum(from_content, axis=0, keepdims=True)
    grad_bias[1:2, :] += jnp.sum(from_position, axis=0, keepdims=True)
    key_sum[...] += dot_tn(content[...], grad_raw)
    value_sum[...] += dot_tn(grad_out, soft)
    table_sum[:, pl.ds(start, wide_len)] += dot_tn(flip_rows(position[...].astype(jnp.float32)).astype(jnp.bfloat16), grad_wide)
    @pl.when(step == pl.num_programs(1) - 1)
    def _():
        grad_keys[...] = key_sum[...].T.astype(jnp.bfloat16)
        grad_values[...] = value_sum[...].T.astype(jnp.bfloat16)
        grad_table[...] = table_sum[...].T.astype(jnp.bfloat16)

def attend_back(probs, grad_context, content, position, keys, values, table, head, block):
    frames, width = content.shape
    heads = width // head
    rows = pl.BlockSpec((block, head), lambda h, i: (i, h))
    whole = pl.BlockSpec((frames, head), lambda h, i: (0, h))
    both = pl.BlockSpec((2 * frames, head), lambda h, i: (0, h))
    out = functools.partial(jax.ShapeDtypeStruct, dtype=jnp.bfloat16)
    return pl.pallas_call(
        functools.partial(attend_back_kernel, frames, block),
        out_shape=(out((frames, width)), out((frames, width)), out((frames, width)), out((2 * frames, width)), jax.ShapeDtypeStruct((8, width), jnp.float32)),
        grid=(heads, frames // block),
        in_specs=[pl.BlockSpec((1, block, frames), lambda h, i: (h, i, 0)), rows, rows, rows, whole, whole, both],
        out_specs=[rows, whole, whole, both, pl.BlockSpec((8, head), lambda h, i: (0, h))],
        scratch_shapes=[pltpu.VMEM((head, frames), jnp.float32), pltpu.VMEM((head, frames), jnp.float32), pltpu.VMEM((head, 2 * frames), jnp.float32)],
        name="attend_back",
    )(probs, grad_context, content, position, keys, values, table)


def ffn_forward(residual, norm_gain, norm_shift, weight_up, weight_down):
    normed, scaled, inv_std = norm_forward(residual, norm_gain, norm_shift)
    act_own = normed.astype(jnp.bfloat16)
    act_peer = swap(act_own)

    def hidden_of(act):
        pre_act = jnp.dot(act, weight_up, preferred_element_type=jnp.float32)
        gate_sig = jax.nn.sigmoid(pre_act)
        slope = gate_sig * (1.0 + pre_act * (1.0 - gate_sig))
        return ((pre_act * gate_sig).astype(jnp.bfloat16), slope.astype(jnp.bfloat16))

    hidden_own, slope_own = hidden_of(act_own)
    hidden_peer, slope_peer = hidden_of(act_peer)
    out_peer = jnp.dot(hidden_peer, weight_down, preferred_element_type=jnp.float32)
    out_own = jnp.dot(hidden_own, weight_down, preferred_element_type=jnp.float32)
    saved = (scaled, inv_std, act_own, act_peer, hidden_own, hidden_peer, slope_own, slope_peer)
    return (narrow(out_own, out_peer), saved)


def ffn_backward(grad_after, saved, norm_gain, weight_up, weight_down):
    scaled, inv_std, act_own, act_peer, hidden_own, hidden_peer, slope_own, slope_peer = saved
    grad_own = grad_after.astype(jnp.bfloat16)
    grad_peer = swap(grad_own)
    pre_own = (times_transposed(grad_own, weight_down) * slope_own.astype(jnp.float32)).astype(jnp.bfloat16)
    pre_peer = (times_transposed(grad_peer, weight_down) * slope_peer.astype(jnp.float32)).astype(jnp.bfloat16)
    back_peer = times_transposed(pre_peer, weight_up)
    back_own = times_transposed(pre_own, weight_up)

    def grad_down(tie, begin=0, end=None):
        own, peer = hidden_own, hidden_peer
        if tie is not None:
            own, peer = after((own, peer), tie)
        return (contract_rows(grad_own, own[:, begin:end]) + contract_rows(grad_peer, peer[:, begin:end])).astype(jnp.bfloat16)

    def grad_up(tie, begin=0, end=None):
        own, peer = act_own, act_peer
        if tie is not None:
            own, peer = after((own, peer), tie)
        return (contract_rows(own, pre_own[:, begin:end]) + contract_rows(peer, pre_peer[:, begin:end])).astype(jnp.bfloat16)

    grad_resid, grad_gain, grad_shift = norm_backward(
        narrow(back_own, back_peer), scaled, inv_std, norm_gain
    )
    return (grad_resid, grad_gain, grad_shift, grad_up, grad_down)


def attn_forward(
    residual,
    norm_gain,
    norm_shift,
    attention_in,
    position_proj,
    position_bias,
    attention_out,
    lengths,
):
    normed, scaled, inv_std = norm_forward(residual, norm_gain, norm_shift)
    own = normed.astype(jnp.bfloat16)
    flat_act = in_order(own, swap(own))
    slot_frames, model_width = flat_act.shape
    head_count, head_size = (position_bias.shape[1], position_bias.shape[2])
    local_width = head_count * head_size
    projected = [
        jnp.dot(flat_act, attention_in[at], preferred_element_type=jnp.float32) for at in range(3)
    ]
    biases = position_bias.astype(jnp.float32).reshape(2, 1, local_width)
    query_content = (projected[0] + biases[0]).astype(jnp.bfloat16)
    query_position = (projected[0] + biases[1]).astype(jnp.bfloat16)
    key_all = projected[1].astype(jnp.bfloat16)
    value_all = projected[2].astype(jnp.bfloat16)
    table_in = relative_table(slot_frames, model_width)
    table = jnp.dot(table_in, position_proj, preferred_element_type=jnp.float32).astype(jnp.bfloat16)
    context, probs = attend(
        lengths, query_content, query_position, key_all, value_all, table, head_size, min(256, slot_frames)
    )
    context_own, context_peer = split_own(context)
    out_peer = jnp.dot(context_peer, attention_out, preferred_element_type=jnp.float32)
    out_own = jnp.dot(context_own, attention_out, preferred_element_type=jnp.float32)
    saved = (
        scaled,
        inv_std,
        flat_act,
        query_content,
        query_position,
        key_all,
        value_all,
        table_in,
        table,
        context,
        probs,
    )
    return (narrow(out_own, out_peer), saved)


def attn_backward(grad_after, saved, norm_gain, attention_in, attention_out, head_count, head_size):
    (
        scaled,
        inv_std,
        flat_act,
        query_content,
        query_position,
        key_all,
        value_all,
        table_in,
        table,
        context,
        probs,
    ) = saved
    grad_own = grad_after.astype(jnp.bfloat16)
    grad_flat = in_order(grad_own, swap(grad_own))
    slot_frames = grad_flat.shape[0]
    grad_back_proj = contract_rows(grad_flat, context)
    grad_context = times_transposed(grad_flat, attention_out).astype(jnp.bfloat16)
    grad_query, grad_keys, grad_values, grad_table, grad_bias = attend_back(
        probs,
        grad_context,
        query_content,
        query_position,
        key_all,
        value_all,
        table,
        head_size,
        min(256, slot_frames),
    )
    grad_bias = grad_bias[:2].reshape(2, head_count, head_size)
    grad_proj = (grad_query, grad_keys, grad_values)
    halves = [split_own(part) for part in grad_proj]
    back_own, back_peer = (
        sum(times_transposed(half[side], attention_in[at]) for at, half in enumerate(halves))
        for side in (0, 1)
    )
    grad_in_proj = [contract_rows(flat_act, part).astype(jnp.bfloat16) for part in grad_proj]
    grad_table_proj = contract_rows(table_in, grad_table)
    grad_resid, grad_gain, grad_shift = norm_backward(
        narrow(back_own, back_peer), scaled, inv_std, norm_gain
    )
    return (
        grad_resid,
        grad_gain,
        grad_shift,
        grad_in_proj,
        grad_table_proj,
        grad_bias,
        grad_back_proj,
    )


def conv_forward(
    residual,
    norm_gain,
    norm_shift,
    pointwise_in,
    depthwise,
    batch_gain,
    batch_shift,
    pointwise_out,
    slot_count,
    live_full,
):
    normed, scaled, inv_std = norm_forward(residual, norm_gain, norm_shift)
    own = normed.astype(jnp.bfloat16)
    flat_act = in_order(own, swap(own))
    slot_frames = flat_act.shape[0]
    both_halves = [
        jnp.dot(flat_act, pointwise_in[:, at], preferred_element_type=jnp.float32) for at in range(2)
    ]
    gate_sig = jax.nn.sigmoid(both_halves[1])
    gated = both_halves[0] * gate_sig * live_full
    channels = gated.shape[1]
    kernel = depthwise.astype(jnp.float32)
    tap_count = kernel.shape[0]
    half_taps = tap_count // 2
    padded = jnp.pad(gated, ((half_taps, half_taps), (0, 0)))
    mixed_conv = padded[0:slot_frames] * kernel[0]
    for tap_index in range(1, tap_count):
        mixed_conv = mixed_conv + padded[tap_index : tap_index + slot_frames] * kernel[tap_index]
    totals, _ = exchange(
        jnp.stack(
            [
                jnp.sum(mixed_conv * live_full, axis=0),
                jnp.sum(mixed_conv * mixed_conv * live_full, axis=0),
                jnp.broadcast_to(slot_count, (channels,)),
            ]
        ),
        "batch",
    )
    frame_count = totals[2, 0]
    batch_mean = totals[0] / frame_count
    batch_inv = lax.rsqrt(totals[1] / frame_count - batch_mean * batch_mean + eps_batch)
    centered = (mixed_conv - batch_mean) * batch_inv
    normed_batch = centered * batch_gain.astype(jnp.float32) + batch_shift.astype(jnp.float32)
    batch_sig = jax.nn.sigmoid(normed_batch)
    swished = (normed_batch * batch_sig).astype(jnp.bfloat16)
    swished_own, swished_peer = split_own(swished)
    out_peer = jnp.dot(swished_peer, pointwise_out, preferred_element_type=jnp.float32)
    out_own = jnp.dot(swished_own, pointwise_out, preferred_element_type=jnp.float32)
    saved = (
        scaled,
        inv_std,
        flat_act,
        both_halves,
        gate_sig,
        padded,
        centered,
        batch_inv,
        frame_count,
        normed_batch,
        batch_sig,
        swished,
    )
    return (narrow(out_own, out_peer), saved)


def conv_backward(
    grad_after, saved, norm_gain, pointwise_in, depthwise, batch_gain, pointwise_out, live_full, fillers
):
    (
        scaled,
        inv_std,
        flat_act,
        both_halves,
        gate_sig,
        padded,
        centered,
        batch_inv,
        frame_count,
        normed_batch,
        batch_sig,
        swished,
    ) = saved
    grad_own = grad_after.astype(jnp.bfloat16)
    grad_flat = in_order(grad_own, swap(grad_own))
    slot_frames = grad_flat.shape[0]
    grad_point_out = contract_rows(grad_flat, swished)
    grad_swished = times_transposed(grad_flat, pointwise_out)
    grad_normed = grad_swished * batch_sig * (1.0 + normed_batch * (1.0 - batch_sig))
    sums, filled = exchange(
        jnp.stack([jnp.sum(grad_normed, axis=0), jnp.sum(grad_normed * centered, axis=0)]), "batch", fillers
    )
    gamma = batch_gain.astype(jnp.float32)
    grad_mixed = batch_inv * (
        grad_normed * gamma
        - live_full * (gamma * sums[0] + centered * gamma * sums[1]) / frame_count
    )
    channels = grad_mixed.shape[1]
    kernel = depthwise.astype(jnp.float32)
    tap_count = kernel.shape[0]
    half_taps = tap_count // 2
    grad_kernel = jnp.stack(
        [
            jnp.sum(grad_mixed * padded[tap_index : tap_index + slot_frames], axis=0)
            for tap_index in range(tap_count)
        ]
    )
    spread = jnp.pad(grad_mixed, ((half_taps, half_taps), (0, 0)))
    grad_gated = spread[2 * half_taps : 2 * half_taps + slot_frames] * kernel[0]
    for tap_index in range(1, tap_count):
        begin = 2 * half_taps - tap_index
        grad_gated = grad_gated + spread[begin : begin + slot_frames] * kernel[tap_index]
    grad_gated = grad_gated * live_full
    grad_halves = [
        (grad_gated * gate_sig).astype(jnp.bfloat16),
        (grad_gated * both_halves[0] * gate_sig * (1.0 - gate_sig)).astype(jnp.bfloat16),
    ]
    grad_point_in = [contract_rows(flat_act, part) for part in grad_halves]
    halves = [split_own(part) for part in grad_halves]
    back_own, back_peer = (
        sum(times_transposed(half[side], pointwise_in[:, at]) for at, half in enumerate(halves))
        for side in (0, 1)
    )
    grad_resid, grad_gain, grad_shift = norm_backward(
        narrow(back_own, back_peer), scaled, inv_std, norm_gain
    )
    return (grad_resid, grad_gain, grad_shift, grad_point_in, grad_point_out, grad_kernel, sums, filled)


def per_device(
    features,
    lengths,
    norm_gains,
    norm_shifts,
    first_up,
    first_down,
    attention_in,
    position_proj,
    position_bias,
    attention_out,
    pointwise_in,
    depthwise,
    batch_gain,
    batch_shift,
    pointwise_out,
    second_up,
    second_down,
    cotangent,
):
    slot_count, half_frames, model_width = features.shape
    slot_frames = half_frames * lax.axis_size("tensor")
    positions = lax.broadcasted_iota(jnp.int32, (half_frames, 1), 0) + lax.axis_index("tensor") * half_frames
    live_half = (positions < lengths[0]).astype(jnp.float32)
    full_positions = lax.broadcasted_iota(jnp.int32, (slot_frames, 1), 0)
    live_full = (full_positions < lengths[0]).astype(jnp.float32)
    gain_rows = norm_gains.astype(jnp.float32)
    shift_rows = norm_shifts.astype(jnp.float32)
    stream_zero = features[0].astype(jnp.float32)
    branch_one, saved_one = ffn_forward(
        stream_zero, gain_rows[0], shift_rows[0], first_up, first_down
    )
    stream_one = stream_zero + 0.5 * branch_one
    branch_two, saved_two = attn_forward(
        stream_one,
        gain_rows[1],
        shift_rows[1],
        attention_in,
        position_proj,
        position_bias,
        attention_out,
        lengths,
    )
    stream_two = stream_one + branch_two
    branch_three, saved_three = conv_forward(
        stream_two,
        gain_rows[2],
        shift_rows[2],
        pointwise_in,
        depthwise,
        batch_gain,
        batch_shift,
        pointwise_out,
        lengths[0].astype(jnp.float32),
        live_full,
    )
    stream_three = stream_two + branch_three
    branch_four, saved_four = ffn_forward(
        stream_three, gain_rows[3], shift_rows[3], second_up, second_down
    )
    stream_four = stream_three + 0.5 * branch_four
    final_norm, scaled_final, inv_final = norm_forward(stream_four, gain_rows[4], shift_rows[4])
    output = (final_norm * live_half).astype(jnp.bfloat16)
    grad_final = cotangent[0].astype(jnp.float32) * live_half
    grad_stream, gain_five, shift_five = norm_backward(
        grad_final, scaled_final, inv_final, gain_rows[4]
    )
    grad_branch, gain_four, shift_four, up_two, down_two = ffn_backward(
        0.5 * grad_stream, saved_four, gain_rows[3], second_up, second_down
    )
    grad_stream = grad_stream + grad_branch
    early = second_up.shape[1] // 2
    (
        grad_branch,
        gain_three,
        shift_three,
        point_in_grad,
        point_out_grad,
        kernel_grad,
        batch_sums,
        (down_two, (up_two, up_rest)),
    ) = conv_backward(
        grad_stream,
        saved_three,
        gain_rows[2],
        pointwise_in,
        depthwise,
        batch_gain,
        pointwise_out,
        live_full,
        [down_two, lambda tie: (up_two(tie, 0, early), up_two(tie, early))],
    )
    down_two, up_two = scatter_batch(down_two).T, scatter_batch(up_two)
    points = [part.astype(jnp.bfloat16) for part in (*point_in_grad, point_out_grad)]
    grad_stream = grad_stream + grad_branch
    grad_branch, gain_two, shift_two, heads_grad, table_grad, bias_grad, back_grad = attn_backward(
        grad_stream,
        saved_two,
        gain_rows[1],
        attention_in,
        attention_out,
        position_bias.shape[1],
        position_bias.shape[2],
    )
    grad_stream = grad_stream + grad_branch
    grad_branch, gain_one, shift_one, up_one, down_one = ffn_backward(
        0.5 * grad_stream, saved_one, gain_rows[0], first_up, first_down
    )
    grad_stream = grad_stream + grad_branch
    up_one, down_one = up_one(None), down_one(None)
    gain_grads = jnp.stack([gain_one, gain_two, gain_three, gain_four, gain_five])
    shift_grads = jnp.stack([shift_one, shift_two, shift_three, shift_four, shift_five])
    norms, channels = gain_grads.shape[0], kernel_grad.shape[1]
    packed = jnp.concatenate([kernel_grad, bias_grad.reshape(2, channels)]).reshape(-1)
    packed = jnp.pad(packed, (0, -packed.shape[0] % (8 * model_width))).reshape(-1, model_width)
    pair_rows = 2 * norms + -2 * norms % 8
    norm_grads = jnp.pad(jnp.concatenate([gain_grads, shift_grads]), ((0, pair_rows - 2 * norms), (0, 0)))
    sums, small = finish_sums(
        [
            *points,
            up_rest,
            *heads_grad,
            table_grad.astype(jnp.bfloat16),
            back_grad.astype(jnp.bfloat16),
            up_one,
            down_one,
        ],
        jnp.concatenate([norm_grads, packed]),
        pair_rows,
    )
    gain_grads, shift_grads = small[:norms], small[norms : 2 * norms]
    packed = small[pair_rows:].reshape(-1)
    kernel_grad = packed[: kernel_grad.size].reshape(kernel_grad.shape)
    bias_grad = packed[kernel_grad.size : kernel_grad.size + bias_grad.size].reshape(bias_grad.shape)
    def take(part):
        nonlocal sums
        taken, sums = sums[:, : part.shape[1]], sums[:, part.shape[1] :]
        return taken

    value_point, gate_point, point_out_grad = [take(part) for part in points]
    point_in_grad = jnp.stack([value_point, gate_point], axis=1)
    point_out_grad = point_out_grad.T
    up_two = jnp.concatenate([up_two, take(up_rest)], axis=1)
    heads_grad = jnp.stack([take(part) for part in heads_grad])
    table_grad, back_grad = take(table_grad), take(back_grad).T
    up_one, down_one = take(up_one), take(down_one).T
    return (
        output[None],
        grad_stream[None],
        gain_grads,
        shift_grads,
        up_one,
        down_one,
        heads_grad,
        table_grad,
        bias_grad,
        back_grad,
        point_in_grad,
        kernel_grad,
        batch_sums[1],
        batch_sums[0],
        point_out_grad,
        up_two,
        down_two,
    )


def solution(mesh):
    in_specs = (
        P("batch", "tensor", None),
        P("batch"),
        P(),
        P(),
        P(None, "tensor"),
        P("tensor", None),
        P(None, None, "tensor"),
        P(None, "tensor"),
        P(None, "tensor", None),
        P("tensor", None),
        P(None, None, "tensor"),
        P(None, "tensor"),
        P("tensor"),
        P("tensor"),
        P("tensor", None),
        P(None, "tensor"),
        P("tensor", None),
        P("batch", "tensor", None),
    )
    out_specs = (
        P("batch", "tensor", None),
        P("batch", "tensor", None),
        P(),
        P(),
        P("batch", "tensor"),
        P("tensor", "batch"),
        P(None, "batch", "tensor"),
        P("batch", "tensor"),
        P(None, "tensor", None),
        P("tensor", "batch"),
        P("batch", None, "tensor"),
        P(None, "tensor"),
        P("tensor"),
        P("tensor"),
        P("tensor", "batch"),
        P("batch", "tensor"),
        P("tensor", "batch"),
    )
    return jax.shard_map(
        per_device, mesh=mesh, in_specs=in_specs, out_specs=out_specs, check_vma=False
    )
```

```python
import functools
import math

import jax
import jax.numpy as jnp
import numpy as np
from jax import lax
from jax.experimental import pallas as pl
from jax.experimental.pallas import tpu as pltpu
from jax.sharding import PartitionSpec as P

eps_norm = 1e-05
eps_batch = 1e-05


def contract_rows(left, right):
    return lax.dot_general(
        left, right, (((0,), (0,)), ((), ())), preferred_element_type=jnp.float32
    )


def times_transposed(left, right):
    return lax.dot_general(
        left, right, (((1,), (1,)), ((), ())), preferred_element_type=jnp.float32
    )


def norm_forward(values, norm_gain, norm_shift):
    center = values - jnp.mean(values, axis=-1, keepdims=True)
    inv_std = lax.rsqrt(jnp.mean(center * center, axis=-1, keepdims=True) + eps_norm)
    scaled = center * inv_std
    return (scaled * norm_gain + norm_shift, scaled, inv_std)


def norm_backward(grad_out, scaled, inv_std, norm_gain):
    grad_scaled = grad_out * norm_gain
    grad_in = inv_std * (
        grad_scaled
        - jnp.mean(grad_scaled, axis=-1, keepdims=True)
        - scaled * jnp.mean(grad_scaled * scaled, axis=-1, keepdims=True)
    )
    return (grad_in, jnp.sum(grad_out * scaled, axis=0), jnp.sum(grad_out, axis=0))


def swap(half):
    return lax.ppermute(half, "tensor", [(0, 1), (1, 0)])


def in_order(own, peer):
    first = lax.axis_index("tensor") == 0
    return jnp.concatenate([jnp.where(first, own, peer), jnp.where(first, peer, own)], axis=0)


def split_own(whole):
    half = whole.shape[0] // 2
    side = lax.axis_index("tensor")
    return (
        lax.dynamic_slice_in_dim(whole, side * half, half, 0),
        lax.dynamic_slice_in_dim(whole, (1 - side) * half, half, 0),
    )


def narrow(own, peer):
    return own + swap(peer.astype(jnp.bfloat16)).astype(jnp.float32)


def exchange(values, axis):
    size = lax.axis_size(axis)
    reach = 1
    while reach < size:
        radix = 4 if size % (reach * 4) == 0 else 2
        got = [
            lax.ppermute(values, axis, [(at, at ^ (reach * other)) for at in range(size)])
            for other in range(1, radix)
        ]
        values = sum(got, values)
        reach *= radix
    return values


def scatter_batch(grad):
    return lax.psum_scatter(
        grad.astype(jnp.bfloat16), "batch", scatter_dimension=0, tiled=True
    ).astype(jnp.float32)


chunk_width = 512
block_rows = 256


def reduce_plan(size, ready, made):
    bits = list(range(size.bit_length() - 1))
    kinds = (bits, [1, 0] + bits[2:], bits[2:] + bits[:2])
    chunk_count = ready + made
    few = max(1, round(chunk_count * 2 / 9))
    orders, turn = [], 0
    for at in range(chunk_count):
        if at % 4 == 3 and sum(order is kinds[2] for order in orders) < few:
            orders.append(kinds[2])
        else:
            orders.append(kinds[turn % 2])
            turn += 1
    free, arrivals, events = {}, [], []

    def issue(chunk, stage, now):
        bit = orders[chunk][stage]
        link = min(bit, 2)
        cost = 2.0 ** -(stage + 1) * (2 if bit >= 3 else 1)
        free[link] = max(free.get(link, 0.0), now) + cost
        arrivals.append((free[link] + 0.05, chunk, stage))

    def issue_small(stage, now):
        link = min(stage, 2) if stage < len(bits) else 3
        free[link] = max(free.get(link, 0.0), now) + 0.03
        arrivals.append((free[link] + 0.1, -1, stage))

    issue_small(0, 0.0)
    for chunk in range(ready):
        issue(chunk, 0, 0.0)
    for chunk in range(ready, chunk_count):
        arrivals.append((0.1 * (chunk - ready + 1), chunk, -1))
    while arrivals:
        arrivals.sort()
        now, chunk, stage = arrivals.pop(0)
        events.append((chunk, stage + 1))
        if chunk < 0 and stage < len(bits):
            issue_small(stage + 1, now)
        elif chunk >= 0 and stage + 1 < len(bits):
            issue(chunk, stage + 1, now)
    return orders, events


def reduce_kernel(size, ready, pieces, pair_rows, count, *refs):
    stages = size.bit_length() - 1
    chunks = ready + len(pieces)
    orders, events = reduce_plan(size, ready, len(pieces))
    sources, refs = refs[:count], refs[count:]
    given, small, out, small_out = refs[:ready], refs[ready], refs[ready + 1], refs[ready + 2]
    refs = refs[ready + 3 :]
    grads, left_buffer, right_buffer = refs[:3]
    landed = refs[3 : 3 + stages]
    small_sum, small_landed, sent, arrived, small_sent, small_arrived, left_sem, right_sem = refs[3 + stages :]
    rows = out.shape[0]
    me = lax.axis_index("batch")
    mine = [lax.rem(me // 2**bit, 2) for bit in range(stages)]

    def shard(block):
        return sum(2**bit * lax.rem(mine[bit] + (block >> bit) % 2, 2) for bit in range(stages))

    def fetches(at):
        left, right, begin, group = pieces[at]
        copies, first = [], 0
        for part, source in enumerate(right):
            length = sources[source].shape[0]
            copies.append(
                pltpu.make_async_copy(
                    sources[source].at[:, pl.ds(begin, chunk_width)],
                    right_buffer.at[at % 2, pl.ds(first, length)],
                    right_sem.at[at % 2, part],
                )
            )
            first += length
        if at == 0 or pieces[at - 1][3] != group:
            first = 0
            for part, source in enumerate(left):
                length = sources[source].shape[0]
                copies.append(
                    pltpu.make_async_copy(
                        sources[source], left_buffer.at[group % 2, pl.ds(first, length)], left_sem.at[group % 2, part]
                    )
                )
                first += length
        return copies

    for fetch in fetches(0):
        fetch.start()
    peer = {"tensor": 1 - lax.axis_index("tensor")}
    barrier = pltpu.get_barrier_semaphore()
    for device in [{"batch": shard(2**bit)} for bit in range(stages)] + [peer]:
        pl.semaphore_signal(barrier, inc=1, device_id=device, device_id_type=pl.DeviceIdType.MESH)
    pl.semaphore_wait(barrier, stages + 1)

    def blocks(chunk, stage):
        order = orders[chunk]
        leaving = [
            block
            for block in range(size)
            if (block >> order[stage]) % 2 and not any((block >> bit) % 2 for bit in order[:stage])
        ]
        return sorted(leaving, key=lambda block: [-((block >> bit) % 2) for bit in order[stage + 1 :]])

    def copy(chunk, stage, source, target):
        return pltpu.make_async_remote_copy(
            src_ref=source,
            dst_ref=target,
            send_sem=sent.at[chunk, stage],
            recv_sem=arrived.at[chunk, stage],
            device_id={"batch": shard(2 ** orders[chunk][stage])},
            device_id_type=pl.DeviceIdType.MESH,
        )

    def grad(chunk):
        return given[chunk] if chunk < ready else grads.at[chunk - ready]

    def start(chunk):
        for at, block in enumerate(blocks(chunk, 0)):
            copy(chunk, 0, grad(chunk).at[shard(block)], landed[0].at[chunk, at]).start()

    def make(at):
        for fetch in fetches(at):
            fetch.wait()
        if at + 1 < len(pieces):
            for fetch in fetches(at + 1):
                fetch.start()
        group = pieces[at][3]
        per = block_rows // rows

        def product(index, carry):
            columns = pl.ds(pl.multiple_of(index * block_rows, block_rows), block_rows)
            result = dot_tn(left_buffer[group % 2, :, columns], right_buffer[at % 2])
            grads[at, pl.ds(index * per, per)] = result.astype(jnp.bfloat16).reshape(per, rows, chunk_width)
            return carry

        lax.fori_loop(0, size // per, product, 0)

    def summed(chunk, block, stage, tile):
        total = grad(chunk)[shard(block), tile, :].astype(jnp.float32)
        for past in range(stage):
            at = blocks(chunk, past).index(block | (1 << orders[chunk][past]))
            total = total + landed[past][chunk, at, tile, :].astype(jnp.float32)
        return total

    def whole(chunk, stage):
        return copy(chunk, stage, landed[stage].at[chunk], landed[stage].at[chunk])

    def small_copy(stage):
        rows = pl.ds(0, small.shape[0] if stage < stages else pair_rows)
        return pltpu.make_async_remote_copy(
            src_ref=(small if stage == 0 else small_sum.at[stage]).at[rows],
            dst_ref=small_landed.at[stage, rows],
            send_sem=small_sent.at[stage],
            recv_sem=small_arrived.at[stage],
            device_id={"batch": shard(2**stage)} if stage < stages else peer,
            device_id_type=pl.DeviceIdType.MESH,
        )

    small_copy(0).start()
    for chunk in range(ready):
        start(chunk)

    step = min(16, rows)
    for chunk, stage in events:
        if chunk < 0:
            small_copy(stage - 1).wait_recv()
            held = small[...] if stage == 1 else small_sum[stage - 1]
            if stage <= stages:
                small_sum[stage] = held + small_landed[stage - 1]
                small_copy(stage).start()
            else:
                small_out[:pair_rows, :] = held[:pair_rows] + small_landed[stages, :pair_rows, :]
                small_out[pair_rows:, :] = held[pair_rows:]
            continue
        if stage == 0:
            make(chunk - ready)
            start(chunk)
            continue
        whole(chunk, stage - 1).wait_recv()

        def work(tile_index, carry, chunk=chunk, stage=stage):
            tile = pl.ds(pl.multiple_of(tile_index * step, step), step)
            if stage < stages:
                for at, block in enumerate(blocks(chunk, stage)):
                    landed[stage - 1][chunk, at, tile, :] = summed(chunk, block, stage, tile).astype(jnp.bfloat16)
            else:
                out[tile, pl.ds(chunk * chunk_width, chunk_width)] = summed(chunk, 0, stage, tile)
            return carry

        lax.fori_loop(0, rows // step, work, 0)
        if stage < stages:
            half = size >> (stage + 1)
            copy(chunk, stage, landed[stage - 1].at[chunk, pl.ds(0, half)], landed[stage].at[chunk]).start()
    for stage in range(stages + 1):
        small_copy(stage).wait_send()
    for chunk in range(chunks):
        for stage in range(stages):
            whole(chunk, stage).wait_send()


def reduce_rows(products, given, small, pair_rows):
    size = lax.axis_size("batch")
    stages = size.bit_length() - 1
    rows = given[0].shape[0] // size
    sources, pieces = [], []
    for group, (left, rights) in enumerate(products):
        left_at = tuple(range(len(sources), len(sources) + len(left)))
        sources.extend(left)
        for right, first in rights:
            right_at = tuple(range(len(sources), len(sources) + len(right)))
            sources.extend(right)
            pieces += [(left_at, right_at, begin, group) for begin in range(first, right[0].shape[1], chunk_width)]
    frames = sum(part.shape[0] for part in products[0][0])
    chunks = len(given) + len(pieces)
    landings = [pltpu.VMEM((chunks, size >> (stage + 1), rows, chunk_width), jnp.bfloat16) for stage in range(stages)]
    vmem = pl.BlockSpec(memory_space=pltpu.VMEM)
    return pl.pallas_call(
        functools.partial(reduce_kernel, size, len(given), pieces, pair_rows, len(sources)),
        out_shape=(
            jax.ShapeDtypeStruct((rows, chunks * chunk_width), jnp.float32),
            jax.ShapeDtypeStruct(small.shape, jnp.float32),
        ),
        in_specs=[pl.BlockSpec(memory_space=pl.ANY)] * len(sources) + [vmem] * (len(given) + 1),
        out_specs=(vmem, vmem),
        scratch_shapes=[
            pltpu.VMEM((len(pieces), size, rows, chunk_width), jnp.bfloat16),
            pltpu.VMEM((2, frames, given[0].shape[0]), jnp.bfloat16),
            pltpu.VMEM((2, frames, chunk_width), jnp.bfloat16),
        ]
        + landings
        + [pltpu.VMEM((stages + 1,) + small.shape, jnp.float32)] * 2
        + [pltpu.SemaphoreType.DMA((chunks, stages))] * 2
        + [pltpu.SemaphoreType.DMA((stages + 1,))] * 2
        + [pltpu.SemaphoreType.DMA((2, 2))] * 2,
        compiler_params=pltpu.CompilerParams(
            collective_id=1, has_side_effects=True, vmem_limit_bytes=60 * 1024 * 1024
        ),
        name="reduce_rows",
    )(*sources, *[grad.reshape(size, rows, grad.shape[1]) for grad in given], small)


def finish_sums(products, given, small, pair_rows):
    if given[0].shape[0] // lax.axis_size("batch") % 16 == 0:
        return reduce_rows(products, given, small, pair_rows)
    grads = list(given)
    for left, rights in products:
        for right, first in rights:
            part = sum(contract_rows(at, other[:, first:]) for at, other in zip(left, right))
            grads.append(part.astype(jnp.bfloat16))
    small = exchange(small, "batch")
    paired = exchange(small[:pair_rows], "tensor")
    return scatter_batch(jnp.concatenate(grads, axis=1)), jnp.concatenate([paired, small[pair_rows:]])


def relative_table(slot_frames, model_width):
    step = min(32, slot_frames)
    column = np.arange(model_width)
    freqs = np.exp((column // 2) * (-2.0 * math.log(10000.0) / model_width))
    coarse = (slot_frames - 1 - step * np.arange(2 * slot_frames // step))[:, None] * freqs + (column % 2) * (
        np.pi / 2
    )
    fine = np.arange(step)[:, None] * freqs
    parts = [jnp.asarray(part, jnp.float32) for part in (np.sin(coarse), np.cos(coarse), np.cos(fine), np.sin(fine))]
    table = parts[0][:, None, :] * parts[2][None] - parts[1][:, None, :] * parts[3][None]
    return table.reshape(2 * slot_frames, model_width).astype(jnp.bfloat16)


def dot_nn(a, b):
    return lax.dot_general(a, b, (((1,), (0,)), ((), ())), preferred_element_type=jnp.float32)
def dot_nt(a, b):
    return lax.dot_general(a, b, (((1,), (1,)), ((), ())), preferred_element_type=jnp.float32)
def dot_tn(a, b):
    return lax.dot_general(a, b, (((0,), (0,)), ((), ())), preferred_element_type=jnp.float32)

def flip_rows(x):
    order = 7 - lax.broadcasted_iota(jnp.int32, (8, x.shape[1]), 0)
    return jnp.concatenate(
        [jnp.take_along_axis(x[at : at + 8], order, axis=0) for at in range(x.shape[0] - 8, -8, -8)], axis=0)

def attend_kernel(frames, block, lengths, content, position, keys, values, table, context, probs):
    wide_len = frames + block
    start = pl.multiple_of(frames - block - pl.program_id(1) * block, block)
    window = table[pl.ds(start, wide_len), :]
    wide = dot_nt(position[...], window)
    skewed = pltpu.roll(wide, frames + 1, 1, stride=1, stride_axis=0)[:, :frames]
    raw = (dot_nt(content[...], keys[...]) + skewed) * (content.shape[1] ** -0.5)
    live = lax.broadcasted_iota(jnp.int32, (1, frames), 1) < lengths[0]
    scores = jnp.where(live, raw, -jnp.inf)
    weight = jnp.exp(scores - jnp.max(scores, axis=1, keepdims=True))
    soft = (weight / jnp.sum(weight, axis=1, keepdims=True)).astype(jnp.bfloat16)
    probs[0] = soft
    context[...] = dot_nn(soft, values[...]).astype(jnp.bfloat16)

def attend(lengths, content, position, keys, values, table, head, block):
    frames, width = content.shape
    heads = width // head
    rows = pl.BlockSpec((block, head), lambda h, i, *_: (i, h))
    whole = pl.BlockSpec((frames, head), lambda h, i, *_: (0, h))
    return pl.pallas_call(
        functools.partial(attend_kernel, frames, block),
        out_shape=(jax.ShapeDtypeStruct((frames, width), jnp.bfloat16), jax.ShapeDtypeStruct((heads, frames, frames), jnp.bfloat16)),
        grid_spec=pltpu.PrefetchScalarGridSpec(
            num_scalar_prefetch=1, grid=(heads, frames // block),
            in_specs=[rows, rows, whole, whole, pl.BlockSpec((2 * frames, head), lambda h, i, *_: (0, h))],
            out_specs=[rows, pl.BlockSpec((1, block, frames), lambda h, i, *_: (h, i, 0))]),
        name="attend",
    )(lengths, content, position, keys, values, table)

def attend_back_kernel(frames, block, probs, grad_context, content, position, keys, values, table, grad_query, grad_keys, grad_values, grad_table, grad_bias, key_sum, value_sum, table_sum):
    wide_len = frames + block
    step = pl.program_id(1)
    start = pl.multiple_of(frames - block - step * block, block)
    @pl.when(step == 0)
    def _():
        key_sum[...] = jnp.zeros_like(key_sum)
        value_sum[...] = jnp.zeros_like(value_sum)
        table_sum[...] = jnp.zeros_like(table_sum)
        grad_bias[...] = jnp.zeros_like(grad_bias)
    soft = probs[0]
    grad_out = grad_context[...]
    grad_probs = dot_nt(grad_out, values[...])
    wide_soft = soft.astype(jnp.float32)
    delta = jnp.sum(wide_soft * grad_probs, axis=1, keepdims=True)
    grad_raw = wide_soft * (grad_probs - delta) * (content.shape[1] ** -0.5)
    padded = jnp.concatenate([flip_rows(grad_raw), jnp.zeros((block, block), jnp.float32)], axis=1)
    grad_wide = pltpu.roll(padded, 0, 1, stride=1, stride_axis=0).astype(jnp.bfloat16)
    grad_raw = grad_raw.astype(jnp.bfloat16)
    from_content = dot_nn(grad_raw, keys[...])
    from_position = dot_nn(grad_wide, table[pl.ds(start, wide_len), :])
    from_position = flip_rows(from_position)
    grad_query[...] = (from_content + from_position).astype(jnp.bfloat16)
    grad_bias[0:1, :] += jnp.sum(from_content, axis=0, keepdims=True)
    grad_bias[1:2, :] += jnp.sum(from_position, axis=0, keepdims=True)
    key_sum[...] += dot_tn(content[...], grad_raw)
    value_sum[...] += dot_tn(grad_out, soft)
    table_sum[:, pl.ds(start, wide_len)] += dot_tn(flip_rows(position[...].astype(jnp.float32)).astype(jnp.bfloat16), grad_wide)
    @pl.when(step == pl.num_programs(1) - 1)
    def _():
        grad_keys[...] = key_sum[...].T.astype(jnp.bfloat16)
        grad_values[...] = value_sum[...].T.astype(jnp.bfloat16)
        grad_table[...] = table_sum[...].T.astype(jnp.bfloat16)

def attend_back(probs, grad_context, content, position, keys, values, table, head, block):
    frames, width = content.shape
    heads = width // head
    rows = pl.BlockSpec((block, head), lambda h, i: (i, h))
    whole = pl.BlockSpec((frames, head), lambda h, i: (0, h))
    both = pl.BlockSpec((2 * frames, head), lambda h, i: (0, h))
    out = functools.partial(jax.ShapeDtypeStruct, dtype=jnp.bfloat16)
    return pl.pallas_call(
        functools.partial(attend_back_kernel, frames, block),
        out_shape=(out((frames, width)), out((frames, width)), out((frames, width)), out((2 * frames, width)), jax.ShapeDtypeStruct((8, width), jnp.float32)),
        grid=(heads, frames // block),
        in_specs=[pl.BlockSpec((1, block, frames), lambda h, i: (h, i, 0)), rows, rows, rows, whole, whole, both],
        out_specs=[rows, whole, whole, both, pl.BlockSpec((8, head), lambda h, i: (0, h))],
        scratch_shapes=[pltpu.VMEM((head, frames), jnp.float32), pltpu.VMEM((head, frames), jnp.float32), pltpu.VMEM((head, 2 * frames), jnp.float32)],
        name="attend_back",
    )(probs, grad_context, content, position, keys, values, table)


def ffn_forward(residual, norm_gain, norm_shift, weight_up, weight_down):
    normed, scaled, inv_std = norm_forward(residual, norm_gain, norm_shift)
    act_own = normed.astype(jnp.bfloat16)
    act_peer = swap(act_own)

    def hidden_of(act):
        pre_act = jnp.dot(act, weight_up, preferred_element_type=jnp.float32)
        gate_sig = jax.nn.sigmoid(pre_act)
        slope = gate_sig * (1.0 + pre_act * (1.0 - gate_sig))
        return ((pre_act * gate_sig).astype(jnp.bfloat16), slope.astype(jnp.bfloat16))

    hidden_own, slope_own = hidden_of(act_own)
    hidden_peer, slope_peer = hidden_of(act_peer)
    out_peer = jnp.dot(hidden_peer, weight_down, preferred_element_type=jnp.float32)
    out_own = jnp.dot(hidden_own, weight_down, preferred_element_type=jnp.float32)
    saved = (scaled, inv_std, act_own, act_peer, hidden_own, hidden_peer, slope_own, slope_peer)
    return (narrow(out_own, out_peer), saved)


def ffn_backward(grad_after, saved, norm_gain, weight_up, weight_down):
    scaled, inv_std, act_own, act_peer, hidden_own, hidden_peer, slope_own, slope_peer = saved
    grad_own = grad_after.astype(jnp.bfloat16)
    grad_peer = swap(grad_own)
    pre_own = (times_transposed(grad_own, weight_down) * slope_own.astype(jnp.float32)).astype(jnp.bfloat16)
    pre_peer = (times_transposed(grad_peer, weight_down) * slope_peer.astype(jnp.float32)).astype(jnp.bfloat16)
    back_peer = times_transposed(pre_peer, weight_up)
    back_own = times_transposed(pre_own, weight_up)

    grad_resid, grad_gain, grad_shift = norm_backward(
        narrow(back_own, back_peer), scaled, inv_std, norm_gain
    )
    operands = (
        ((act_own, act_peer), (pre_own, pre_peer)),
        ((grad_own, grad_peer), (hidden_own, hidden_peer)),
    )
    return (grad_resid, grad_gain, grad_shift, operands)


def attn_forward(
    residual,
    norm_gain,
    norm_shift,
    attention_in,
    position_proj,
    position_bias,
    attention_out,
    lengths,
):
    normed, scaled, inv_std = norm_forward(residual, norm_gain, norm_shift)
    own = normed.astype(jnp.bfloat16)
    flat_act = in_order(own, swap(own))
    slot_frames, model_width = flat_act.shape
    head_count, head_size = (position_bias.shape[1], position_bias.shape[2])
    local_width = head_count * head_size
    projected = [
        jnp.dot(flat_act, attention_in[at], preferred_element_type=jnp.float32) for at in range(3)
    ]
    biases = position_bias.astype(jnp.float32).reshape(2, 1, local_width)
    query_content = (projected[0] + biases[0]).astype(jnp.bfloat16)
    query_position = (projected[0] + biases[1]).astype(jnp.bfloat16)
    key_all = projected[1].astype(jnp.bfloat16)
    value_all = projected[2].astype(jnp.bfloat16)
    table_in = relative_table(slot_frames, model_width)
    table = jnp.dot(table_in, position_proj, preferred_element_type=jnp.float32).astype(jnp.bfloat16)
    context, probs = attend(
        lengths, query_content, query_position, key_all, value_all, table, head_size, min(256, slot_frames)
    )
    context_own, context_peer = split_own(context)
    out_peer = jnp.dot(context_peer, attention_out, preferred_element_type=jnp.float32)
    out_own = jnp.dot(context_own, attention_out, preferred_element_type=jnp.float32)
    saved = (
        scaled,
        inv_std,
        flat_act,
        query_content,
        query_position,
        key_all,
        value_all,
        table_in,
        table,
        context,
        probs,
    )
    return (narrow(out_own, out_peer), saved)


def attn_backward(grad_after, saved, norm_gain, attention_in, attention_out, head_count, head_size):
    (
        scaled,
        inv_std,
        flat_act,
        query_content,
        query_position,
        key_all,
        value_all,
        table_in,
        table,
        context,
        probs,
    ) = saved
    grad_own = grad_after.astype(jnp.bfloat16)
    grad_flat = in_order(grad_own, swap(grad_own))
    slot_frames = grad_flat.shape[0]
    back_product = ((grad_flat,), [((context,), 0)])
    grad_context = times_transposed(grad_flat, attention_out).astype(jnp.bfloat16)
    grad_query, grad_keys, grad_values, grad_table, grad_bias = attend_back(
        probs,
        grad_context,
        query_content,
        query_position,
        key_all,
        value_all,
        table,
        head_size,
        min(256, slot_frames),
    )
    grad_bias = grad_bias[:2].reshape(2, head_count, head_size)
    grad_proj = (grad_query, grad_keys, grad_values)
    halves = [split_own(part) for part in grad_proj]
    back_own, back_peer = (
        sum(times_transposed(half[side], attention_in[at]) for at, half in enumerate(halves))
        for side in (0, 1)
    )
    in_product = ((flat_act,), [((part,), 0) for part in grad_proj])
    grad_table_proj = contract_rows(table_in, grad_table)
    grad_resid, grad_gain, grad_shift = norm_backward(
        narrow(back_own, back_peer), scaled, inv_std, norm_gain
    )
    return (
        grad_resid,
        grad_gain,
        grad_shift,
        in_product,
        grad_table_proj,
        grad_bias,
        back_product,
    )


def conv_forward(
    residual,
    norm_gain,
    norm_shift,
    pointwise_in,
    depthwise,
    batch_gain,
    batch_shift,
    pointwise_out,
    slot_count,
    live_full,
):
    normed, scaled, inv_std = norm_forward(residual, norm_gain, norm_shift)
    own = normed.astype(jnp.bfloat16)
    flat_act = in_order(own, swap(own))
    slot_frames = flat_act.shape[0]
    both_halves = [
        jnp.dot(flat_act, pointwise_in[:, at], preferred_element_type=jnp.float32) for at in range(2)
    ]
    gate_sig = jax.nn.sigmoid(both_halves[1])
    gated = both_halves[0] * gate_sig * live_full
    channels = gated.shape[1]
    kernel = depthwise.astype(jnp.float32)
    tap_count = kernel.shape[0]
    half_taps = tap_count // 2
    padded = jnp.pad(gated, ((half_taps, half_taps), (0, 0)))
    mixed_conv = padded[0:slot_frames] * kernel[0]
    for tap_index in range(1, tap_count):
        mixed_conv = mixed_conv + padded[tap_index : tap_index + slot_frames] * kernel[tap_index]
    totals = exchange(
        jnp.stack(
            [
                jnp.sum(mixed_conv * live_full, axis=0),
                jnp.sum(mixed_conv * mixed_conv * live_full, axis=0),
                jnp.broadcast_to(slot_count, (channels,)),
            ]
        ),
        "batch",
    )
    frame_count = totals[2, 0]
    batch_mean = totals[0] / frame_count
    batch_inv = lax.rsqrt(totals[1] / frame_count - batch_mean * batch_mean + eps_batch)
    centered = (mixed_conv - batch_mean) * batch_inv
    normed_batch = centered * batch_gain.astype(jnp.float32) + batch_shift.astype(jnp.float32)
    batch_sig = jax.nn.sigmoid(normed_batch)
    swished = (normed_batch * batch_sig).astype(jnp.bfloat16)
    swished_own, swished_peer = split_own(swished)
    out_peer = jnp.dot(swished_peer, pointwise_out, preferred_element_type=jnp.float32)
    out_own = jnp.dot(swished_own, pointwise_out, preferred_element_type=jnp.float32)
    saved = (
        scaled,
        inv_std,
        flat_act,
        both_halves,
        gate_sig,
        padded,
        centered,
        batch_inv,
        frame_count,
        normed_batch,
        batch_sig,
        swished,
    )
    return (narrow(out_own, out_peer), saved)


def conv_backward(
    grad_after, saved, norm_gain, pointwise_in, depthwise, batch_gain, pointwise_out, live_full
):
    (
        scaled,
        inv_std,
        flat_act,
        both_halves,
        gate_sig,
        padded,
        centered,
        batch_inv,
        frame_count,
        normed_batch,
        batch_sig,
        swished,
    ) = saved
    grad_own = grad_after.astype(jnp.bfloat16)
    grad_flat = in_order(grad_own, swap(grad_own))
    slot_frames = grad_flat.shape[0]
    out_product = ((grad_flat,), [((swished,), 0)])
    grad_swished = times_transposed(grad_flat, pointwise_out)
    grad_normed = grad_swished * batch_sig * (1.0 + normed_batch * (1.0 - batch_sig))
    sums = exchange(
        jnp.stack([jnp.sum(grad_normed, axis=0), jnp.sum(grad_normed * centered, axis=0)]), "batch"
    )
    gamma = batch_gain.astype(jnp.float32)
    grad_mixed = batch_inv * (
        grad_normed * gamma
        - live_full * (gamma * sums[0] + centered * gamma * sums[1]) / frame_count
    )
    channels = grad_mixed.shape[1]
    kernel = depthwise.astype(jnp.float32)
    tap_count = kernel.shape[0]
    half_taps = tap_count // 2
    grad_kernel = jnp.stack(
        [
            jnp.sum(grad_mixed * padded[tap_index : tap_index + slot_frames], axis=0)
            for tap_index in range(tap_count)
        ]
    )
    spread = jnp.pad(grad_mixed, ((half_taps, half_taps), (0, 0)))
    grad_gated = spread[2 * half_taps : 2 * half_taps + slot_frames] * kernel[0]
    for tap_index in range(1, tap_count):
        begin = 2 * half_taps - tap_index
        grad_gated = grad_gated + spread[begin : begin + slot_frames] * kernel[tap_index]
    grad_gated = grad_gated * live_full
    grad_halves = [
        (grad_gated * gate_sig).astype(jnp.bfloat16),
        (grad_gated * both_halves[0] * gate_sig * (1.0 - gate_sig)).astype(jnp.bfloat16),
    ]
    in_product = ((flat_act,), [((part,), 0) for part in grad_halves])
    halves = [split_own(part) for part in grad_halves]
    back_own, back_peer = (
        sum(times_transposed(half[side], pointwise_in[:, at]) for at, half in enumerate(halves))
        for side in (0, 1)
    )
    grad_resid, grad_gain, grad_shift = norm_backward(
        narrow(back_own, back_peer), scaled, inv_std, norm_gain
    )
    return (grad_resid, grad_gain, grad_shift, in_product, out_product, grad_kernel, sums)


def per_device(
    features,
    lengths,
    norm_gains,
    norm_shifts,
    first_up,
    first_down,
    attention_in,
    position_proj,
    position_bias,
    attention_out,
    pointwise_in,
    depthwise,
    batch_gain,
    batch_shift,
    pointwise_out,
    second_up,
    second_down,
    cotangent,
):
    slot_count, half_frames, model_width = features.shape
    slot_frames = half_frames * lax.axis_size("tensor")
    positions = lax.broadcasted_iota(jnp.int32, (half_frames, 1), 0) + lax.axis_index("tensor") * half_frames
    live_half = (positions < lengths[0]).astype(jnp.float32)
    full_positions = lax.broadcasted_iota(jnp.int32, (slot_frames, 1), 0)
    live_full = (full_positions < lengths[0]).astype(jnp.float32)
    gain_rows = norm_gains.astype(jnp.float32)
    shift_rows = norm_shifts.astype(jnp.float32)
    stream_zero = features[0].astype(jnp.float32)
    branch_one, saved_one = ffn_forward(
        stream_zero, gain_rows[0], shift_rows[0], first_up, first_down
    )
    stream_one = stream_zero + 0.5 * branch_one
    branch_two, saved_two = attn_forward(
        stream_one,
        gain_rows[1],
        shift_rows[1],
        attention_in,
        position_proj,
        position_bias,
        attention_out,
        lengths,
    )
    stream_two = stream_one + branch_two
    branch_three, saved_three = conv_forward(
        stream_two,
        gain_rows[2],
        shift_rows[2],
        pointwise_in,
        depthwise,
        batch_gain,
        batch_shift,
        pointwise_out,
        lengths[0].astype(jnp.float32),
        live_full,
    )
    stream_three = stream_two + branch_three
    branch_four, saved_four = ffn_forward(
        stream_three, gain_rows[3], shift_rows[3], second_up, second_down
    )
    stream_four = stream_three + 0.5 * branch_four
    final_norm, scaled_final, inv_final = norm_forward(stream_four, gain_rows[4], shift_rows[4])
    output = (final_norm * live_half).astype(jnp.bfloat16)
    grad_final = cotangent[0].astype(jnp.float32) * live_half
    grad_stream, gain_five, shift_five = norm_backward(
        grad_final, scaled_final, inv_final, gain_rows[4]
    )
    grad_branch, gain_four, shift_four, operands_two = ffn_backward(
        0.5 * grad_stream, saved_four, gain_rows[3], second_up, second_down
    )
    grad_stream = grad_stream + grad_branch
    (
        grad_branch,
        gain_three,
        shift_three,
        points_product,
        point_out_product,
        kernel_grad,
        batch_sums,
    ) = conv_backward(
        grad_stream,
        saved_three,
        gain_rows[2],
        pointwise_in,
        depthwise,
        batch_gain,
        pointwise_out,
        live_full,
    )
    grad_stream = grad_stream + grad_branch
    grad_branch, gain_two, shift_two, heads_product, table_grad, bias_grad, back_product = attn_backward(
        grad_stream,
        saved_two,
        gain_rows[1],
        attention_in,
        attention_out,
        position_bias.shape[1],
        position_bias.shape[2],
    )
    grad_stream = grad_stream + grad_branch
    grad_branch, gain_one, shift_one, operands_one = ffn_backward(
        0.5 * grad_stream, saved_one, gain_rows[0], first_up, first_down
    )
    grad_stream = grad_stream + grad_branch
    gain_grads = jnp.stack([gain_one, gain_two, gain_three, gain_four, gain_five])
    shift_grads = jnp.stack([shift_one, shift_two, shift_three, shift_four, shift_five])
    norms, channels = gain_grads.shape[0], kernel_grad.shape[1]
    packed = jnp.concatenate([kernel_grad, bias_grad.reshape(2, channels)]).reshape(-1)
    packed = jnp.pad(packed, (0, -packed.shape[0] % (8 * model_width))).reshape(-1, model_width)
    pair_rows = 2 * norms + -2 * norms % 8
    norm_grads = jnp.pad(jnp.concatenate([gain_grads, shift_grads]), ((0, pair_rows - 2 * norms), (0, 0)))
    sums, small = finish_sums(
        [
            (operands_two[0][0], [(operands_two[0][1], 0)]),
            (operands_two[1][0], [(operands_two[1][1], 0)]),
            points_product,
            point_out_product,
            heads_product,
            back_product,
            (operands_one[0][0], [(operands_one[0][1], 0)]),
            (operands_one[1][0], [(operands_one[1][1], 0)]),
        ],
        [table_grad.astype(jnp.bfloat16)],
        jnp.concatenate([norm_grads, packed]),
        pair_rows,
    )
    gain_grads, shift_grads = small[:norms], small[norms : 2 * norms]
    packed = small[pair_rows:].reshape(-1)
    kernel_grad = packed[: kernel_grad.size].reshape(kernel_grad.shape)
    bias_grad = packed[kernel_grad.size : kernel_grad.size + bias_grad.size].reshape(bias_grad.shape)
    def take(width):
        nonlocal sums
        taken, sums = sums[:, :width], sums[:, width:]
        return taken

    hidden = first_up.shape[1]
    table_grad = take(channels)
    up_two, down_two = take(hidden), take(hidden).T
    point_in_grad = jnp.stack([take(channels) for _ in range(2)], axis=1)
    point_out_grad = take(channels).T
    heads_grad = jnp.stack([take(channels) for _ in range(3)])
    back_grad = take(channels).T
    up_one, down_one = take(hidden), take(hidden).T
    return (
        output[None],
        grad_stream[None],
        gain_grads,
        shift_grads,
        up_one,
        down_one,
        heads_grad,
        table_grad,
        bias_grad,
        back_grad,
        point_in_grad,
        kernel_grad,
        batch_sums[1],
        batch_sums[0],
        point_out_grad,
        up_two,
        down_two,
    )


def solution(mesh):
    in_specs = (
        P("batch", "tensor", None),
        P("batch"),
        P(),
        P(),
        P(None, "tensor"),
        P("tensor", None),
        P(None, None, "tensor"),
        P(None, "tensor"),
        P(None, "tensor", None),
        P("tensor", None),
        P(None, None, "tensor"),
        P(None, "tensor"),
        P("tensor"),
        P("tensor"),
        P("tensor", None),
        P(None, "tensor"),
        P("tensor", None),
        P("batch", "tensor", None),
    )
    out_specs = (
        P("batch", "tensor", None),
        P("batch", "tensor", None),
        P(),
        P(),
        P("batch", "tensor"),
        P("tensor", "batch"),
        P(None, "batch", "tensor"),
        P("batch", "tensor"),
        P(None, "tensor", None),
        P("tensor", "batch"),
        P("batch", None, "tensor"),
        P(None, "tensor"),
        P("tensor"),
        P("tensor"),
        P("tensor", "batch"),
        P("batch", "tensor"),
        P("tensor", "batch"),
    )
    return jax.shard_map(
        per_device, mesh=mesh, in_specs=in_specs, out_specs=out_specs, check_vma=False
    )
```

```python
import functools
import math

import jax
import jax.numpy as jnp
import numpy as np
from jax import lax
from jax.experimental import pallas as pl
from jax.experimental.pallas import tpu as pltpu
from jax.sharding import PartitionSpec as P

eps_norm = 1e-05
eps_batch = 1e-05


def contract_rows(left, right):
    return lax.dot_general(
        left, right, (((0,), (0,)), ((), ())), preferred_element_type=jnp.float32
    )


def times_transposed(left, right):
    return lax.dot_general(
        left, right, (((1,), (1,)), ((), ())), preferred_element_type=jnp.float32
    )


def norm_forward(values, norm_gain, norm_shift):
    center = values - jnp.mean(values, axis=-1, keepdims=True)
    inv_std = lax.rsqrt(jnp.mean(center * center, axis=-1, keepdims=True) + eps_norm)
    scaled = center * inv_std
    return (scaled * norm_gain + norm_shift, scaled, inv_std)


def norm_backward(grad_out, scaled, inv_std, norm_gain):
    grad_scaled = grad_out * norm_gain
    grad_in = inv_std * (
        grad_scaled
        - jnp.mean(grad_scaled, axis=-1, keepdims=True)
        - scaled * jnp.mean(grad_scaled * scaled, axis=-1, keepdims=True)
    )
    return (grad_in, jnp.sum(grad_out * scaled, axis=0), jnp.sum(grad_out, axis=0))


def swap(half):
    return lax.ppermute(half, "tensor", [(0, 1), (1, 0)])


def in_order(own, peer):
    first = lax.axis_index("tensor") == 0
    return jnp.concatenate([jnp.where(first, own, peer), jnp.where(first, peer, own)], axis=0)


def split_own(whole):
    half = whole.shape[0] // 2
    side = lax.axis_index("tensor")
    return (
        lax.dynamic_slice_in_dim(whole, side * half, half, 0),
        lax.dynamic_slice_in_dim(whole, (1 - side) * half, half, 0),
    )


def narrow(own, peer):
    return lax.optimization_barrier(own) + swap(peer.astype(jnp.bfloat16)).astype(jnp.float32)


def exchange(values, axis):
    size = lax.axis_size(axis)
    reach = 1
    while reach < size:
        radix = 4 if size % (reach * 4) == 0 else 2
        got = [
            lax.ppermute(values, axis, [(at, at ^ (reach * other)) for at in range(size)])
            for other in range(1, radix)
        ]
        values = sum(got, values)
        reach *= radix
    return values


def share_kernel(size, own, out, landed, sent, arrived):
    me = lax.axis_index("batch")
    barrier = pltpu.get_barrier_semaphore()
    for step in range(1, size):
        other = {"batch": lax.rem(me + step, size)}
        pl.semaphore_signal(barrier, inc=1, device_id=other, device_id_type=pl.DeviceIdType.MESH)
    pl.semaphore_wait(barrier, size - 1)

    def copy(step):
        return pltpu.make_async_remote_copy(
            src_ref=own,
            dst_ref=landed.at[me],
            send_sem=sent.at[step],
            recv_sem=arrived.at[step],
            device_id={"batch": lax.rem(me + step, size)},
            device_id_type=pl.DeviceIdType.MESH,
        )

    for step in range(1, size):
        copy(step).start()
    landed[me] = own[...]
    for step in range(1, size):
        copy(step).wait_recv()
    total = landed[0]
    for at in range(1, size):
        total = total + landed[at]
    out[...] = total
    for step in range(1, size):
        copy(step).wait_send()


def share(values):
    size = lax.axis_size("batch")
    if size > 16:
        return exchange(values, "batch")
    shape = values.shape
    values = jnp.pad(values.reshape(-1), (0, -values.size % 2048)).reshape(-1, 128)
    vmem = pl.BlockSpec(memory_space=pltpu.VMEM)
    return pl.pallas_call(
        functools.partial(share_kernel, size),
        out_shape=jax.ShapeDtypeStruct(values.shape, jnp.float32),
        in_specs=[vmem],
        out_specs=vmem,
        scratch_shapes=[pltpu.VMEM((size,) + values.shape, jnp.float32)] + [pltpu.SemaphoreType.DMA((size,))] * 2,
        compiler_params=pltpu.CompilerParams(
            collective_id=2, has_side_effects=True, vmem_limit_bytes=2 * 1024 * 1024
        ),
        name="share",
    )(values).reshape(-1)[: shape[0] * shape[1]].reshape(shape)


def scatter_batch(grad):
    return lax.psum_scatter(
        grad.astype(jnp.bfloat16), "batch", scatter_dimension=0, tiled=True
    ).astype(jnp.float32)


chunk_width = 512
block_rows = 256


def reduce_plan(size, ready, made):
    bits = list(range(size.bit_length() - 1))
    kinds = (bits, [1, 0] + bits[2:], bits[2:] + bits[:2])
    chunk_count = ready + made
    few = max(1, round(chunk_count * 2 / 9))
    orders, turn = [], 0
    for at in range(chunk_count):
        if at % 4 == 3 and sum(order is kinds[2] for order in orders) < few:
            orders.append(kinds[2])
        else:
            orders.append(kinds[turn % 2])
            turn += 1
    free, arrivals, events = {}, [], []

    def issue(chunk, stage, now):
        bit = orders[chunk][stage]
        link = min(bit, 2)
        cost = 2.0 ** -(stage + 1) * (2 if bit >= 3 else 1)
        free[link] = max(free.get(link, 0.0), now) + cost
        arrivals.append((free[link] + 0.05, chunk, stage))

    def issue_small(stage, now):
        link = min(stage, 2) if stage < len(bits) else 3
        free[link] = max(free.get(link, 0.0), now) + 0.03
        arrivals.append((free[link] + 0.1, -1, stage))

    issue_small(0, 0.0)
    for chunk in range(ready):
        issue(chunk, 0, 0.0)
    for chunk in range(ready, chunk_count):
        arrivals.append((0.1 * (chunk - ready + 1), chunk, -1))
    while arrivals:
        arrivals.sort()
        now, chunk, stage = arrivals.pop(0)
        events.append((chunk, stage + 1))
        if chunk < 0 and stage < len(bits):
            issue_small(stage + 1, now)
        elif chunk >= 0 and stage + 1 < len(bits):
            issue(chunk, stage + 1, now)
    return orders, events


def reduce_kernel(size, ready, pieces, pair_rows, count, *refs):
    stages = size.bit_length() - 1
    chunks = ready + len(pieces)
    orders, events = reduce_plan(size, ready, len(pieces))
    sources, refs = refs[:count], refs[count:]
    given, small, out, small_out = refs[:ready], refs[ready], refs[ready + 1], refs[ready + 2]
    refs = refs[ready + 3 :]
    grads, left_buffer, right_buffer = refs[:3]
    landed = refs[3 : 3 + stages]
    small_sum, small_landed, sent, arrived, small_sent, small_arrived, left_sem, right_sem = refs[3 + stages :]
    rows = out.shape[0]
    me = lax.axis_index("batch")
    mine = [lax.rem(me // 2**bit, 2) for bit in range(stages)]

    def shard(block):
        return sum(2**bit * lax.rem(mine[bit] + (block >> bit) % 2, 2) for bit in range(stages))

    def fetches(at):
        left, right, begin, group = pieces[at]
        copies, first = [], 0
        halves = len(left) // len(right)
        for part, source in enumerate(right * halves):
            length = sources[source].shape[0] // halves
            offset = 0
            if halves > 1:
                offset = pl.multiple_of(lax.rem(lax.axis_index("tensor") + part, 2) * length, length)
            copies.append(
                pltpu.make_async_copy(
                    sources[source].at[pl.ds(offset, length), pl.ds(begin, chunk_width)],
                    right_buffer.at[at % 2, pl.ds(first, length)],
                    right_sem.at[at % 2, part],
                )
            )
            first += length
        if at == 0 or pieces[at - 1][3] != group:
            first = 0
            for part, source in enumerate(left):
                length = sources[source].shape[0]
                copies.append(
                    pltpu.make_async_copy(
                        sources[source], left_buffer.at[group % 2, pl.ds(first, length)], left_sem.at[group % 2, part]
                    )
                )
                first += length
        return copies

    for fetch in fetches(0):
        fetch.start()
    peer = {"tensor": 1 - lax.axis_index("tensor")}
    barrier = pltpu.get_barrier_semaphore()
    for device in [{"batch": shard(2**bit)} for bit in range(stages)] + [peer]:
        pl.semaphore_signal(barrier, inc=1, device_id=device, device_id_type=pl.DeviceIdType.MESH)
    pl.semaphore_wait(barrier, stages + 1)

    def blocks(chunk, stage):
        order = orders[chunk]
        leaving = [
            block
            for block in range(size)
            if (block >> order[stage]) % 2 and not any((block >> bit) % 2 for bit in order[:stage])
        ]
        return sorted(leaving, key=lambda block: [-((block >> bit) % 2) for bit in order[stage + 1 :]])

    def copy(chunk, stage, source, target):
        return pltpu.make_async_remote_copy(
            src_ref=source,
            dst_ref=target,
            send_sem=sent.at[chunk, stage],
            recv_sem=arrived.at[chunk, stage],
            device_id={"batch": shard(2 ** orders[chunk][stage])},
            device_id_type=pl.DeviceIdType.MESH,
        )

    def grad(chunk):
        return given[chunk] if chunk < ready else grads.at[chunk - ready]

    def start(chunk):
        for at, block in enumerate(blocks(chunk, 0)):
            copy(chunk, 0, grad(chunk).at[shard(block)], landed[0].at[chunk, at]).start()

    def make(at):
        for fetch in fetches(at):
            fetch.wait()
        if at + 1 < len(pieces):
            for fetch in fetches(at + 1):
                fetch.start()
        group = pieces[at][3]
        per = block_rows // rows

        def product(index, carry):
            columns = pl.ds(pl.multiple_of(index * block_rows, block_rows), block_rows)
            result = dot_tn(left_buffer[group % 2, :, columns], right_buffer[at % 2])
            grads[at, pl.ds(index * per, per)] = result.astype(jnp.bfloat16).reshape(per, rows, chunk_width)
            return carry

        lax.fori_loop(0, size // per, product, 0)

    def summed(chunk, block, stage, tile):
        total = grad(chunk)[shard(block), tile, :].astype(jnp.float32)
        for past in range(stage):
            at = blocks(chunk, past).index(block | (1 << orders[chunk][past]))
            total = total + landed[past][chunk, at, tile, :].astype(jnp.float32)
        return total

    def whole(chunk, stage):
        return copy(chunk, stage, landed[stage].at[chunk], landed[stage].at[chunk])

    def small_copy(stage):
        rows = pl.ds(0, small.shape[0] if stage < stages else pair_rows)
        return pltpu.make_async_remote_copy(
            src_ref=(small if stage == 0 else small_sum.at[stage]).at[rows],
            dst_ref=small_landed.at[stage, rows],
            send_sem=small_sent.at[stage],
            recv_sem=small_arrived.at[stage],
            device_id={"batch": shard(2**stage)} if stage < stages else peer,
            device_id_type=pl.DeviceIdType.MESH,
        )

    small_copy(0).start()
    for chunk in range(ready):
        start(chunk)

    step = min(16, rows)
    for chunk, stage in events:
        if chunk < 0:
            small_copy(stage - 1).wait_recv()
            held = small[...] if stage == 1 else small_sum[stage - 1]
            if stage <= stages:
                small_sum[stage] = held + small_landed[stage - 1]
                small_copy(stage).start()
            else:
                small_out[:pair_rows, :] = held[:pair_rows] + small_landed[stages, :pair_rows, :]
                small_out[pair_rows:, :] = held[pair_rows:]
            continue
        if stage == 0:
            make(chunk - ready)
            start(chunk)
            continue
        whole(chunk, stage - 1).wait_recv()

        def work(tile_index, carry, chunk=chunk, stage=stage):
            tile = pl.ds(pl.multiple_of(tile_index * step, step), step)
            if stage < stages:
                for at, block in enumerate(blocks(chunk, stage)):
                    landed[stage - 1][chunk, at, tile, :] = summed(chunk, block, stage, tile).astype(jnp.bfloat16)
            else:
                out[tile, pl.ds(chunk * chunk_width, chunk_width)] = summed(chunk, 0, stage, tile)
            return carry

        lax.fori_loop(0, rows // step, work, 0)
        if stage < stages:
            half = size >> (stage + 1)
            copy(chunk, stage, landed[stage - 1].at[chunk, pl.ds(0, half)], landed[stage].at[chunk]).start()
    for stage in range(stages + 1):
        small_copy(stage).wait_send()
    for chunk in range(chunks):
        for stage in range(stages):
            whole(chunk, stage).wait_send()


def reduce_rows(products, given, small, pair_rows):
    size = lax.axis_size("batch")
    stages = size.bit_length() - 1
    rows = given[0].shape[0] // size
    sources, pieces = [], []
    for group, (left, rights) in enumerate(products):
        left_at = tuple(range(len(sources), len(sources) + len(left)))
        sources.extend(left)
        for right, first in rights:
            right_at = tuple(range(len(sources), len(sources) + len(right)))
            sources.extend(right)
            pieces += [(left_at, right_at, begin, group) for begin in range(first, right[0].shape[1], chunk_width)]
    frames = sum(part.shape[0] for part in products[0][0])
    chunks = len(given) + len(pieces)
    landings = [pltpu.VMEM((chunks, size >> (stage + 1), rows, chunk_width), jnp.bfloat16) for stage in range(stages)]
    vmem = pl.BlockSpec(memory_space=pltpu.VMEM)
    return pl.pallas_call(
        functools.partial(reduce_kernel, size, len(given), pieces, pair_rows, len(sources)),
        out_shape=(
            jax.ShapeDtypeStruct((rows, chunks * chunk_width), jnp.float32),
            jax.ShapeDtypeStruct(small.shape, jnp.float32),
        ),
        in_specs=[pl.BlockSpec(memory_space=pl.ANY)] * len(sources) + [vmem] * (len(given) + 1),
        out_specs=(vmem, vmem),
        scratch_shapes=[
            pltpu.VMEM((len(pieces), size, rows, chunk_width), jnp.bfloat16),
            pltpu.VMEM((2, frames, given[0].shape[0]), jnp.bfloat16),
            pltpu.VMEM((2, frames, chunk_width), jnp.bfloat16),
        ]
        + landings
        + [pltpu.VMEM((stages + 1,) + small.shape, jnp.float32)] * 2
        + [pltpu.SemaphoreType.DMA((chunks, stages))] * 2
        + [pltpu.SemaphoreType.DMA((stages + 1,))] * 2
        + [pltpu.SemaphoreType.DMA((2, 2))] * 2,
        compiler_params=pltpu.CompilerParams(
            collective_id=1, has_side_effects=True, vmem_limit_bytes=60 * 1024 * 1024
        ),
        name="reduce_rows",
    )(*sources, *[grad.reshape(size, rows, grad.shape[1]) for grad in given], small)


def finish_sums(products, given, small, pair_rows):
    if given[0].shape[0] // lax.axis_size("batch") % 16 == 0:
        return reduce_rows(products, given, small, pair_rows)
    grads = list(given)
    for left, rights in products:
        for right, first in rights:
            if len(right) < len(left):
                right = split_own(right[0])
            part = sum(contract_rows(at, other[:, first:]) for at, other in zip(left, right))
            grads.append(part.astype(jnp.bfloat16))
    small = exchange(small, "batch")
    paired = exchange(small[:pair_rows], "tensor")
    return scatter_batch(jnp.concatenate(grads, axis=1)), jnp.concatenate([paired, small[pair_rows:]])


def relative_table(slot_frames, model_width):
    step = min(32, slot_frames)
    column = np.arange(model_width)
    freqs = np.exp((column // 2) * (-2.0 * math.log(10000.0) / model_width))
    coarse = (slot_frames - 1 - step * np.arange(2 * slot_frames // step))[:, None] * freqs + (column % 2) * (
        np.pi / 2
    )
    fine = np.arange(step)[:, None] * freqs
    parts = [jnp.asarray(part, jnp.float32) for part in (np.sin(coarse), np.cos(coarse), np.cos(fine), np.sin(fine))]
    table = parts[0][:, None, :] * parts[2][None] - parts[1][:, None, :] * parts[3][None]
    return table.reshape(2 * slot_frames, model_width).astype(jnp.bfloat16)


def dot_nn(a, b):
    return lax.dot_general(a, b, (((1,), (0,)), ((), ())), preferred_element_type=jnp.float32)
def dot_nt(a, b):
    return lax.dot_general(a, b, (((1,), (1,)), ((), ())), preferred_element_type=jnp.float32)
def dot_tn(a, b):
    return lax.dot_general(a, b, (((0,), (0,)), ((), ())), preferred_element_type=jnp.float32)

def flip_rows(x):
    order = 7 - lax.broadcasted_iota(jnp.int32, (8, x.shape[1]), 0)
    return jnp.concatenate(
        [jnp.take_along_axis(x[at : at + 8], order, axis=0) for at in range(x.shape[0] - 8, -8, -8)], axis=0)

def attend_kernel(frames, block, lengths, content, position, keys, values, table, context, probs):
    wide_len = frames + block
    start = pl.multiple_of(frames - block - pl.program_id(1) * block, block)
    window = table[pl.ds(start, wide_len), :]
    wide = dot_nt(position[...], window)
    skewed = pltpu.roll(wide, frames + 1, 1, stride=1, stride_axis=0)[:, :frames]
    raw = (dot_nt(content[...], keys[...]) + skewed) * (content.shape[1] ** -0.5)
    live = lax.broadcasted_iota(jnp.int32, (1, frames), 1) < lengths[0]
    scores = jnp.where(live, raw, -jnp.inf)
    weight = jnp.exp(scores - jnp.max(scores, axis=1, keepdims=True))
    soft = (weight / jnp.sum(weight, axis=1, keepdims=True)).astype(jnp.bfloat16)
    probs[0] = soft
    context[...] = dot_nn(soft, values[...]).astype(jnp.bfloat16)

def attend(lengths, content, position, keys, values, table, head, block):
    frames, width = content.shape
    heads = width // head
    rows = pl.BlockSpec((block, head), lambda h, i, *_: (i, h))
    whole = pl.BlockSpec((frames, head), lambda h, i, *_: (0, h))
    return pl.pallas_call(
        functools.partial(attend_kernel, frames, block),
        out_shape=(jax.ShapeDtypeStruct((frames, width), jnp.bfloat16), jax.ShapeDtypeStruct((heads, frames, frames), jnp.bfloat16)),
        grid_spec=pltpu.PrefetchScalarGridSpec(
            num_scalar_prefetch=1, grid=(heads, frames // block),
            in_specs=[rows, rows, whole, whole, pl.BlockSpec((2 * frames, head), lambda h, i, *_: (0, h))],
            out_specs=[rows, pl.BlockSpec((1, block, frames), lambda h, i, *_: (h, i, 0))]),
        compiler_params=pltpu.CompilerParams(vmem_limit_bytes=24 * 1024 * 1024),
        name="attend",
    )(lengths, content, position, keys, values, table)

def attend_back_kernel(frames, block, probs, grad_context, content, position, keys, values, table, grad_query, grad_keys, grad_values, grad_table, grad_bias, key_sum, value_sum, table_sum):
    wide_len = frames + block
    step = pl.program_id(1)
    start = pl.multiple_of(frames - block - step * block, block)
    @pl.when(step == 0)
    def _():
        key_sum[...] = jnp.zeros_like(key_sum)
        value_sum[...] = jnp.zeros_like(value_sum)
        table_sum[...] = jnp.zeros_like(table_sum)
        grad_bias[...] = jnp.zeros_like(grad_bias)
    soft = probs[0]
    grad_out = grad_context[...]
    grad_probs = dot_nt(grad_out, values[...])
    wide_soft = soft.astype(jnp.float32)
    delta = jnp.sum(wide_soft * grad_probs, axis=1, keepdims=True)
    grad_raw = wide_soft * (grad_probs - delta) * (content.shape[1] ** -0.5)
    padded = jnp.concatenate([flip_rows(grad_raw), jnp.zeros((block, block), jnp.float32)], axis=1)
    grad_wide = pltpu.roll(padded, 0, 1, stride=1, stride_axis=0).astype(jnp.bfloat16)
    grad_raw = grad_raw.astype(jnp.bfloat16)
    from_content = dot_nn(grad_raw, keys[...])
    from_position = dot_nn(grad_wide, table[pl.ds(start, wide_len), :])
    from_position = flip_rows(from_position)
    grad_query[...] = (from_content + from_position).astype(jnp.bfloat16)
    grad_bias[0:1, :] += jnp.sum(from_content, axis=0, keepdims=True)
    grad_bias[1:2, :] += jnp.sum(from_position, axis=0, keepdims=True)
    key_sum[...] += dot_tn(content[...], grad_raw)
    value_sum[...] += dot_tn(grad_out, soft)
    table_sum[:, pl.ds(start, wide_len)] += dot_tn(flip_rows(position[...].astype(jnp.float32)).astype(jnp.bfloat16), grad_wide)
    @pl.when(step == pl.num_programs(1) - 1)
    def _():
        grad_keys[...] = key_sum[...].T.astype(jnp.bfloat16)
        grad_values[...] = value_sum[...].T.astype(jnp.bfloat16)
        grad_table[...] = table_sum[...].T.astype(jnp.bfloat16)

def attend_back(probs, grad_context, content, position, keys, values, table, head, block):
    frames, width = content.shape
    heads = width // head
    rows = pl.BlockSpec((block, head), lambda h, i: (i, h))
    whole = pl.BlockSpec((frames, head), lambda h, i: (0, h))
    both = pl.BlockSpec((2 * frames, head), lambda h, i: (0, h))
    out = functools.partial(jax.ShapeDtypeStruct, dtype=jnp.bfloat16)
    return pl.pallas_call(
        functools.partial(attend_back_kernel, frames, block),
        out_shape=(out((frames, width)), out((frames, width)), out((frames, width)), out((2 * frames, width)), jax.ShapeDtypeStruct((8, width), jnp.float32)),
        grid=(heads, frames // block),
        in_specs=[pl.BlockSpec((1, block, frames), lambda h, i: (h, i, 0)), rows, rows, rows, whole, whole, both],
        out_specs=[rows, whole, whole, both, pl.BlockSpec((8, head), lambda h, i: (0, h))],
        scratch_shapes=[pltpu.VMEM((head, frames), jnp.float32), pltpu.VMEM((head, frames), jnp.float32), pltpu.VMEM((head, 2 * frames), jnp.float32)],
        compiler_params=pltpu.CompilerParams(vmem_limit_bytes=28 * 1024 * 1024),
        name="attend_back",
    )(probs, grad_context, content, position, keys, values, table)


def ffn_forward(residual, norm_gain, norm_shift, weight_up, weight_down):
    normed, scaled, inv_std = norm_forward(residual, norm_gain, norm_shift)
    act_own = normed.astype(jnp.bfloat16)
    act_peer = swap(act_own)

    def hidden_of(act):
        pre_act = jnp.dot(act, weight_up, preferred_element_type=jnp.float32)
        gate_sig = jax.nn.sigmoid(pre_act)
        slope = gate_sig * (1.0 + pre_act * (1.0 - gate_sig))
        return ((pre_act * gate_sig).astype(jnp.bfloat16), slope.astype(jnp.bfloat16))

    hidden_own, slope_own = hidden_of(act_own)
    hidden_peer, slope_peer = hidden_of(act_peer)
    out_peer = jnp.dot(hidden_peer, weight_down, preferred_element_type=jnp.float32)
    out_own = jnp.dot(hidden_own, weight_down, preferred_element_type=jnp.float32)
    saved = (scaled, inv_std, act_own, act_peer, hidden_own, hidden_peer, slope_own, slope_peer)
    return (narrow(out_own, out_peer), saved)


def ffn_backward(grad_after, saved, norm_gain, weight_up, weight_down):
    scaled, inv_std, act_own, act_peer, hidden_own, hidden_peer, slope_own, slope_peer = saved
    grad_own = grad_after.astype(jnp.bfloat16)
    grad_peer = swap(grad_own)
    pre_own = (times_transposed(grad_own, weight_down) * slope_own.astype(jnp.float32)).astype(jnp.bfloat16)
    pre_peer = (times_transposed(grad_peer, weight_down) * slope_peer.astype(jnp.float32)).astype(jnp.bfloat16)
    back_peer = times_transposed(pre_peer, weight_up)
    back_own = times_transposed(pre_own, weight_up)

    grad_resid, grad_gain, grad_shift = norm_backward(
        narrow(back_own, back_peer), scaled, inv_std, norm_gain
    )
    operands = (
        ((act_own, act_peer), (pre_own, pre_peer)),
        ((grad_own, grad_peer), (hidden_own, hidden_peer)),
    )
    return (grad_resid, grad_gain, grad_shift, operands)


def attn_forward(
    residual,
    norm_gain,
    norm_shift,
    attention_in,
    position_proj,
    position_bias,
    attention_out,
    lengths,
):
    normed, scaled, inv_std = norm_forward(residual, norm_gain, norm_shift)
    own = normed.astype(jnp.bfloat16)
    peer = swap(own)
    flat_act = in_order(own, peer)
    slot_frames, model_width = flat_act.shape
    head_count, head_size = (position_bias.shape[1], position_bias.shape[2])
    local_width = head_count * head_size
    projected = [
        jnp.dot(flat_act, attention_in[at], preferred_element_type=jnp.float32) for at in range(3)
    ]
    biases = position_bias.astype(jnp.float32).reshape(2, 1, local_width)
    query_content = (projected[0] + biases[0]).astype(jnp.bfloat16)
    query_position = (projected[0] + biases[1]).astype(jnp.bfloat16)
    key_all = projected[1].astype(jnp.bfloat16)
    value_all = projected[2].astype(jnp.bfloat16)
    table_in = relative_table(slot_frames, model_width)
    table = jnp.dot(table_in, position_proj, preferred_element_type=jnp.float32).astype(jnp.bfloat16)
    context, probs = attend(
        lengths, query_content, query_position, key_all, value_all, table, head_size, min(512, slot_frames)
    )
    context_own, context_peer = split_own(context)
    out_peer = jnp.dot(context_peer, attention_out, preferred_element_type=jnp.float32)
    out_own = jnp.dot(context_own, attention_out, preferred_element_type=jnp.float32)
    saved = (
        scaled,
        inv_std,
        (own, peer),
        query_content,
        query_position,
        key_all,
        value_all,
        table_in,
        table,
        context,
        probs,
    )
    return (narrow(out_own, out_peer), saved)


def attn_backward(grad_after, saved, norm_gain, attention_in, attention_out, head_count, head_size):
    (
        scaled,
        inv_std,
        flat_act,
        query_content,
        query_position,
        key_all,
        value_all,
        table_in,
        table,
        context,
        probs,
    ) = saved
    grad_own = grad_after.astype(jnp.bfloat16)
    grad_peer = swap(grad_own)
    grad_flat = in_order(grad_own, grad_peer)
    slot_frames = grad_flat.shape[0]
    back_product = ((grad_own, grad_peer), [((context,), 0)])
    grad_context = times_transposed(grad_flat, attention_out).astype(jnp.bfloat16)
    grad_query, grad_keys, grad_values, grad_table, grad_bias = attend_back(
        probs,
        grad_context,
        query_content,
        query_position,
        key_all,
        value_all,
        table,
        head_size,
        min(512, slot_frames),
    )
    grad_bias = grad_bias[:2].reshape(2, head_count, head_size)
    grad_proj = (grad_query, grad_keys, grad_values)
    halves = [split_own(part) for part in grad_proj]
    back_own, back_peer = (
        sum(times_transposed(half[side], attention_in[at]) for at, half in enumerate(halves))
        for side in (0, 1)
    )
    in_product = (flat_act, [((part,), 0) for part in grad_proj])
    grad_table_proj = contract_rows(table_in, grad_table)
    grad_resid, grad_gain, grad_shift = norm_backward(
        narrow(back_own, back_peer), scaled, inv_std, norm_gain
    )
    return (
        grad_resid,
        grad_gain,
        grad_shift,
        in_product,
        grad_table_proj,
        grad_bias,
        back_product,
    )


def conv_forward(
    residual,
    norm_gain,
    norm_shift,
    pointwise_in,
    depthwise,
    batch_gain,
    batch_shift,
    pointwise_out,
    slot_count,
    live_full,
):
    normed, scaled, inv_std = norm_forward(residual, norm_gain, norm_shift)
    own = normed.astype(jnp.bfloat16)
    peer = swap(own)
    flat_act = in_order(own, peer)
    slot_frames = flat_act.shape[0]
    both_halves = [
        jnp.dot(flat_act, pointwise_in[:, at], preferred_element_type=jnp.float32) for at in range(2)
    ]
    gate_sig = jax.nn.sigmoid(both_halves[1])
    gated = both_halves[0] * gate_sig * live_full
    channels = gated.shape[1]
    kernel = depthwise.astype(jnp.float32)
    tap_count = kernel.shape[0]
    half_taps = tap_count // 2
    padded = jnp.pad(gated, ((half_taps, half_taps), (0, 0)))
    mixed_conv = padded[0:slot_frames] * kernel[0]
    for tap_index in range(1, tap_count):
        mixed_conv = mixed_conv + padded[tap_index : tap_index + slot_frames] * kernel[tap_index]
    totals = share(
        jnp.stack(
            [
                jnp.sum(mixed_conv * live_full, axis=0),
                jnp.sum(mixed_conv * mixed_conv * live_full, axis=0),
                jnp.broadcast_to(slot_count, (channels,)),
            ]
        )
    )
    frame_count = totals[2, 0]
    batch_mean = totals[0] / frame_count
    batch_inv = lax.rsqrt(totals[1] / frame_count - batch_mean * batch_mean + eps_batch)
    centered = (mixed_conv - batch_mean) * batch_inv
    normed_batch = centered * batch_gain.astype(jnp.float32) + batch_shift.astype(jnp.float32)
    batch_sig = jax.nn.sigmoid(normed_batch)
    swished = (normed_batch * batch_sig).astype(jnp.bfloat16)
    swished_own, swished_peer = split_own(swished)
    out_peer = jnp.dot(swished_peer, pointwise_out, preferred_element_type=jnp.float32)
    out_own = jnp.dot(swished_own, pointwise_out, preferred_element_type=jnp.float32)
    saved = (
        scaled,
        inv_std,
        (own, peer),
        both_halves,
        gate_sig,
        padded,
        centered,
        batch_inv,
        frame_count,
        normed_batch,
        batch_sig,
        swished,
    )
    return (narrow(out_own, out_peer), saved)


def conv_backward(
    grad_after, saved, norm_gain, pointwise_in, depthwise, batch_gain, pointwise_out, live_full
):
    (
        scaled,
        inv_std,
        flat_act,
        both_halves,
        gate_sig,
        padded,
        centered,
        batch_inv,
        frame_count,
        normed_batch,
        batch_sig,
        swished,
    ) = saved
    grad_own = grad_after.astype(jnp.bfloat16)
    grad_peer = swap(grad_own)
    grad_flat = in_order(grad_own, grad_peer)
    slot_frames = grad_flat.shape[0]
    out_product = ((grad_own, grad_peer), [((swished,), 0)])
    grad_swished = times_transposed(grad_flat, pointwise_out)
    grad_normed = grad_swished * batch_sig * (1.0 + normed_batch * (1.0 - batch_sig))
    sums = share(jnp.stack([jnp.sum(grad_normed, axis=0), jnp.sum(grad_normed * centered, axis=0)]))
    gamma = batch_gain.astype(jnp.float32)
    grad_mixed = batch_inv * (
        grad_normed * gamma
        - live_full * (gamma * sums[0] + centered * gamma * sums[1]) / frame_count
    )
    channels = grad_mixed.shape[1]
    kernel = depthwise.astype(jnp.float32)
    tap_count = kernel.shape[0]
    half_taps = tap_count // 2
    grad_kernel = jnp.stack(
        [
            jnp.sum(grad_mixed * padded[tap_index : tap_index + slot_frames], axis=0)
            for tap_index in range(tap_count)
        ]
    )
    spread = jnp.pad(grad_mixed, ((half_taps, half_taps), (0, 0)))
    grad_gated = spread[2 * half_taps : 2 * half_taps + slot_frames] * kernel[0]
    for tap_index in range(1, tap_count):
        begin = 2 * half_taps - tap_index
        grad_gated = grad_gated + spread[begin : begin + slot_frames] * kernel[tap_index]
    grad_gated = grad_gated * live_full
    grad_halves = [
        (grad_gated * gate_sig).astype(jnp.bfloat16),
        (grad_gated * both_halves[0] * gate_sig * (1.0 - gate_sig)).astype(jnp.bfloat16),
    ]
    in_product = (flat_act, [((part,), 0) for part in grad_halves])
    halves = [split_own(part) for part in grad_halves]
    back_own, back_peer = (
        sum(times_transposed(half[side], pointwise_in[:, at]) for at, half in enumerate(halves))
        for side in (0, 1)
    )
    grad_resid, grad_gain, grad_shift = norm_backward(
        narrow(back_own, back_peer), scaled, inv_std, norm_gain
    )
    return (grad_resid, grad_gain, grad_shift, in_product, out_product, grad_kernel, sums)


def per_device(
    features,
    lengths,
    norm_gains,
    norm_shifts,
    first_up,
    first_down,
    attention_in,
    position_proj,
    position_bias,
    attention_out,
    pointwise_in,
    depthwise,
    batch_gain,
    batch_shift,
    pointwise_out,
    second_up,
    second_down,
    cotangent,
):
    slot_count, half_frames, model_width = features.shape
    slot_frames = half_frames * lax.axis_size("tensor")
    positions = lax.broadcasted_iota(jnp.int32, (half_frames, 1), 0) + lax.axis_index("tensor") * half_frames
    live_half = (positions < lengths[0]).astype(jnp.float32)
    full_positions = lax.broadcasted_iota(jnp.int32, (slot_frames, 1), 0)
    live_full = (full_positions < lengths[0]).astype(jnp.float32)
    gain_rows = norm_gains.astype(jnp.float32)
    shift_rows = norm_shifts.astype(jnp.float32)
    stream_zero = features[0].astype(jnp.float32)
    branch_one, saved_one = ffn_forward(
        stream_zero, gain_rows[0], shift_rows[0], first_up, first_down
    )
    stream_one = stream_zero + 0.5 * branch_one
    branch_two, saved_two = attn_forward(
        stream_one,
        gain_rows[1],
        shift_rows[1],
        attention_in,
        position_proj,
        position_bias,
        attention_out,
        lengths,
    )
    stream_two = stream_one + branch_two
    branch_three, saved_three = conv_forward(
        stream_two,
        gain_rows[2],
        shift_rows[2],
        pointwise_in,
        depthwise,
        batch_gain,
        batch_shift,
        pointwise_out,
        lengths[0].astype(jnp.float32),
        live_full,
    )
    stream_three = stream_two + branch_three
    branch_four, saved_four = ffn_forward(
        stream_three, gain_rows[3], shift_rows[3], second_up, second_down
    )
    stream_four = stream_three + 0.5 * branch_four
    final_norm, scaled_final, inv_final = norm_forward(stream_four, gain_rows[4], shift_rows[4])
    output = (final_norm * live_half).astype(jnp.bfloat16)
    grad_final = cotangent[0].astype(jnp.float32) * live_half
    grad_stream, gain_five, shift_five = norm_backward(
        grad_final, scaled_final, inv_final, gain_rows[4]
    )
    grad_branch, gain_four, shift_four, operands_two = ffn_backward(
        0.5 * grad_stream, saved_four, gain_rows[3], second_up, second_down
    )
    grad_stream = grad_stream + grad_branch
    (
        grad_branch,
        gain_three,
        shift_three,
        points_product,
        point_out_product,
        kernel_grad,
        batch_sums,
    ) = conv_backward(
        grad_stream,
        saved_three,
        gain_rows[2],
        pointwise_in,
        depthwise,
        batch_gain,
        pointwise_out,
        live_full,
    )
    grad_stream = grad_stream + grad_branch
    grad_branch, gain_two, shift_two, heads_product, table_grad, bias_grad, back_product = attn_backward(
        grad_stream,
        saved_two,
        gain_rows[1],
        attention_in,
        attention_out,
        position_bias.shape[1],
        position_bias.shape[2],
    )
    grad_stream = grad_stream + grad_branch
    grad_branch, gain_one, shift_one, operands_one = ffn_backward(
        0.5 * grad_stream, saved_one, gain_rows[0], first_up, first_down
    )
    grad_stream = grad_stream + grad_branch
    gain_grads = jnp.stack([gain_one, gain_two, gain_three, gain_four, gain_five])
    shift_grads = jnp.stack([shift_one, shift_two, shift_three, shift_four, shift_five])
    norms, channels = gain_grads.shape[0], kernel_grad.shape[1]
    packed = jnp.concatenate([kernel_grad, bias_grad.reshape(2, channels)]).reshape(-1)
    packed = jnp.pad(packed, (0, -packed.shape[0] % (8 * model_width))).reshape(-1, model_width)
    pair_rows = 2 * norms + -2 * norms % 8
    norm_grads = jnp.pad(jnp.concatenate([gain_grads, shift_grads]), ((0, pair_rows - 2 * norms), (0, 0)))
    sums, small = finish_sums(
        [
            (operands_two[0][0], [(operands_two[0][1], 0)]),
            (operands_two[1][0], [(operands_two[1][1], 0)]),
            points_product,
            point_out_product,
            heads_product,
            back_product,
            (operands_one[0][0], [(operands_one[0][1], 0)]),
            (operands_one[1][0], [(operands_one[1][1], 0)]),
        ],
        [table_grad.astype(jnp.bfloat16)],
        jnp.concatenate([norm_grads, packed]),
        pair_rows,
    )
    gain_grads, shift_grads = small[:norms], small[norms : 2 * norms]
    packed = small[pair_rows:].reshape(-1)
    kernel_grad = packed[: kernel_grad.size].reshape(kernel_grad.shape)
    bias_grad = packed[kernel_grad.size : kernel_grad.size + bias_grad.size].reshape(bias_grad.shape)
    def take(width):
        nonlocal sums
        taken, sums = sums[:, :width], sums[:, width:]
        return taken

    hidden = first_up.shape[1]
    table_grad = take(channels)
    up_two, down_two = take(hidden), take(hidden).T
    point_in_grad = jnp.stack([take(channels) for _ in range(2)], axis=1)
    point_out_grad = take(channels).T
    heads_grad = jnp.stack([take(channels) for _ in range(3)])
    back_grad = take(channels).T
    up_one, down_one = take(hidden), take(hidden).T
    return (
        output[None],
        grad_stream[None],
        gain_grads,
        shift_grads,
        up_one,
        down_one,
        heads_grad,
        table_grad,
        bias_grad,
        back_grad,
        point_in_grad,
        kernel_grad,
        batch_sums[1],
        batch_sums[0],
        point_out_grad,
        up_two,
        down_two,
    )


def solution(mesh):
    in_specs = (
        P("batch", "tensor", None),
        P("batch"),
        P(),
        P(),
        P(None, "tensor"),
        P("tensor", None),
        P(None, None, "tensor"),
        P(None, "tensor"),
        P(None, "tensor", None),
        P("tensor", None),
        P(None, None, "tensor"),
        P(None, "tensor"),
        P("tensor"),
        P("tensor"),
        P("tensor", None),
        P(None, "tensor"),
        P("tensor", None),
        P("batch", "tensor", None),
    )
    out_specs = (
        P("batch", "tensor", None),
        P("batch", "tensor", None),
        P(),
        P(),
        P("batch", "tensor"),
        P("tensor", "batch"),
        P(None, "batch", "tensor"),
        P("batch", "tensor"),
        P(None, "tensor", None),
        P("tensor", "batch"),
        P("batch", None, "tensor"),
        P(None, "tensor"),
        P("tensor"),
        P("tensor"),
        P("tensor", "batch"),
        P("batch", "tensor"),
        P("tensor", "batch"),
    )
    return jax.shard_map(
        per_device, mesh=mesh, in_specs=in_specs, out_specs=out_specs, check_vma=False
    )
```

```python
import functools
import math

import jax
import jax.numpy as jnp
import numpy as np
from jax import lax
from jax.experimental import pallas as pl
from jax.experimental.pallas import tpu as pltpu
from jax.sharding import PartitionSpec as P

eps_norm = 1e-05
eps_batch = 1e-05


def contract_rows(left, right):
    return lax.dot_general(
        left, right, (((0,), (0,)), ((), ())), preferred_element_type=jnp.float32
    )


def times_transposed(left, right):
    return lax.dot_general(
        left, right, (((1,), (1,)), ((), ())), preferred_element_type=jnp.float32
    )


def norm_forward(values, norm_gain, norm_shift):
    center = values - jnp.mean(values, axis=-1, keepdims=True)
    inv_std = lax.rsqrt(jnp.mean(center * center, axis=-1, keepdims=True) + eps_norm)
    scaled = center * inv_std
    return (scaled * norm_gain + norm_shift, scaled, inv_std)


def norm_backward(grad_out, scaled, inv_std, norm_gain):
    grad_scaled = grad_out * norm_gain
    grad_in = inv_std * (
        grad_scaled
        - jnp.mean(grad_scaled, axis=-1, keepdims=True)
        - scaled * jnp.mean(grad_scaled * scaled, axis=-1, keepdims=True)
    )
    return (grad_in, jnp.sum(grad_out * scaled, axis=0), jnp.sum(grad_out, axis=0))


def swap(half):
    return lax.ppermute(half, "tensor", [(0, 1), (1, 0)])


def in_order(own, peer):
    first = lax.axis_index("tensor") == 0
    return jnp.concatenate([jnp.where(first, own, peer), jnp.where(first, peer, own)], axis=0)


def split_own(whole):
    half = whole.shape[0] // 2
    side = lax.axis_index("tensor")
    return (
        lax.dynamic_slice_in_dim(whole, side * half, half, 0),
        lax.dynamic_slice_in_dim(whole, (1 - side) * half, half, 0),
    )


def narrow(own, peer):
    return lax.optimization_barrier(own) + swap(peer.astype(jnp.bfloat16)).astype(jnp.float32)


def exchange(values, axis):
    size = lax.axis_size(axis)
    reach = 1
    while reach < size:
        radix = 4 if size % (reach * 4) == 0 else 2
        got = [
            lax.ppermute(values, axis, [(at, at ^ (reach * other)) for at in range(size)])
            for other in range(1, radix)
        ]
        values = sum(got, values)
        reach *= radix
    return values


def share_kernel(size, own, out, landed, sent, arrived):
    me = lax.axis_index("batch")
    barrier = pltpu.get_barrier_semaphore()
    for step in range(1, size):
        other = {"batch": lax.rem(me + step, size)}
        pl.semaphore_signal(barrier, inc=1, device_id=other, device_id_type=pl.DeviceIdType.MESH)
    pl.semaphore_wait(barrier, size - 1)

    def copy(step):
        return pltpu.make_async_remote_copy(
            src_ref=own,
            dst_ref=landed.at[me],
            send_sem=sent.at[step],
            recv_sem=arrived.at[step],
            device_id={"batch": lax.rem(me + step, size)},
            device_id_type=pl.DeviceIdType.MESH,
        )

    for step in range(1, size):
        copy(step).start()
    landed[me] = own[...]
    for step in range(1, size):
        copy(step).wait_recv()
    total = landed[0]
    for at in range(1, size):
        total = total + landed[at]
    out[...] = total
    for step in range(1, size):
        copy(step).wait_send()


def share(values):
    size = lax.axis_size("batch")
    if size > 16:
        return exchange(values, "batch")
    shape = values.shape
    values = jnp.pad(values.reshape(-1), (0, -values.size % 2048)).reshape(-1, 128)
    vmem = pl.BlockSpec(memory_space=pltpu.VMEM)
    return pl.pallas_call(
        functools.partial(share_kernel, size),
        out_shape=jax.ShapeDtypeStruct(values.shape, jnp.float32),
        in_specs=[vmem],
        out_specs=vmem,
        scratch_shapes=[pltpu.VMEM((size,) + values.shape, jnp.float32)] + [pltpu.SemaphoreType.DMA((size,))] * 2,
        compiler_params=pltpu.CompilerParams(
            collective_id=2, has_side_effects=True, vmem_limit_bytes=2 * 1024 * 1024
        ),
        name="share",
    )(values).reshape(-1)[: shape[0] * shape[1]].reshape(shape)


def scatter_batch(grad):
    return lax.psum_scatter(
        grad.astype(jnp.bfloat16), "batch", scatter_dimension=0, tiled=True
    ).astype(jnp.float32)


chunk_width = 512
block_rows = 256


def reduce_plan(size, ready, made):
    bits = list(range(size.bit_length() - 1))
    kinds = (bits, [1, 0] + bits[2:], bits[2:] + bits[:2])
    chunk_count = ready + made
    few = max(1, round(chunk_count * 2 / 9))
    orders, turn = [], 0
    for at in range(chunk_count):
        if at % 4 == 3 and sum(order is kinds[2] for order in orders) < few:
            orders.append(kinds[2])
        else:
            orders.append(kinds[turn % 2])
            turn += 1
    free, arrivals, events = {}, [], []

    def issue(chunk, stage, now):
        bit = orders[chunk][stage]
        link = min(bit, 2)
        cost = 2.0 ** -(stage + 1) * (2 if bit >= 3 else 1)
        free[link] = max(free.get(link, 0.0), now) + cost
        arrivals.append((free[link] + 0.05, chunk, stage))

    def issue_small(stage, now):
        link = min(stage, 2) if stage < len(bits) else 3
        free[link] = max(free.get(link, 0.0), now) + 0.03
        arrivals.append((free[link] + 0.1, -1, stage))

    issue_small(0, 0.0)
    for chunk in range(ready):
        issue(chunk, 0, 0.0)
    for chunk in range(ready, chunk_count):
        arrivals.append((0.1 * (chunk - ready + 1), chunk, -1))
    while arrivals:
        arrivals.sort()
        now, chunk, stage = arrivals.pop(0)
        events.append((chunk, stage + 1))
        if chunk < 0 and stage < len(bits):
            issue_small(stage + 1, now)
        elif chunk >= 0 and stage + 1 < len(bits):
            issue(chunk, stage + 1, now)
    return orders, events


def reduce_kernel(size, ready, pieces, pair_rows, count, *refs):
    stages = size.bit_length() - 1
    chunks = ready + len(pieces)
    orders, events = reduce_plan(size, ready, len(pieces))
    sources, refs = refs[:count], refs[count:]
    given, small, out, small_out = refs[:ready], refs[ready], refs[ready + 1], refs[ready + 2]
    refs = refs[ready + 3 :]
    grads, left_buffer, right_buffer = refs[:3]
    landed = refs[3 : 3 + stages]
    small_sum, small_landed, sent, arrived, small_sent, small_arrived, left_sem, right_sem = refs[3 + stages :]
    rows = out.shape[0]
    me = lax.axis_index("batch")
    mine = [lax.rem(me // 2**bit, 2) for bit in range(stages)]

    def shard(block):
        return sum(2**bit * lax.rem(mine[bit] + (block >> bit) % 2, 2) for bit in range(stages))

    def fetches(at):
        left, right, begin, group = pieces[at]
        copies, first = [], 0
        halves = len(left) // len(right)
        for part, source in enumerate(right * halves):
            length = sources[source].shape[0] // halves
            offset = 0
            if halves > 1:
                offset = pl.multiple_of(lax.rem(lax.axis_index("tensor") + part, 2) * length, length)
            copies.append(
                pltpu.make_async_copy(
                    sources[source].at[pl.ds(offset, length), pl.ds(begin, chunk_width)],
                    right_buffer.at[at % 2, pl.ds(first, length)],
                    right_sem.at[at % 2, part],
                )
            )
            first += length
        if at == 0 or pieces[at - 1][3] != group:
            first = 0
            for part, source in enumerate(left):
                length = sources[source].shape[0]
                copies.append(
                    pltpu.make_async_copy(
                        sources[source], left_buffer.at[group % 2, pl.ds(first, length)], left_sem.at[group % 2, part]
                    )
                )
                first += length
        return copies

    for fetch in fetches(0):
        fetch.start()
    peer = {"tensor": 1 - lax.axis_index("tensor")}
    barrier = pltpu.get_barrier_semaphore()
    for device in [{"batch": shard(2**bit)} for bit in range(stages)] + [peer]:
        pl.semaphore_signal(barrier, inc=1, device_id=device, device_id_type=pl.DeviceIdType.MESH)
    pl.semaphore_wait(barrier, stages + 1)

    def blocks(chunk, stage):
        order = orders[chunk]
        leaving = [
            block
            for block in range(size)
            if (block >> order[stage]) % 2 and not any((block >> bit) % 2 for bit in order[:stage])
        ]
        return sorted(leaving, key=lambda block: [-((block >> bit) % 2) for bit in order[stage + 1 :]])

    def copy(chunk, stage, source, target):
        return pltpu.make_async_remote_copy(
            src_ref=source,
            dst_ref=target,
            send_sem=sent.at[chunk, stage],
            recv_sem=arrived.at[chunk, stage],
            device_id={"batch": shard(2 ** orders[chunk][stage])},
            device_id_type=pl.DeviceIdType.MESH,
        )

    def grad(chunk):
        return given[chunk] if chunk < ready else grads.at[chunk - ready]

    def start(chunk):
        for at, block in enumerate(blocks(chunk, 0)):
            copy(chunk, 0, grad(chunk).at[shard(block)], landed[0].at[chunk, at]).start()

    def make(at):
        for fetch in fetches(at):
            fetch.wait()
        if at + 1 < len(pieces):
            for fetch in fetches(at + 1):
                fetch.start()
        group = pieces[at][3]
        per = block_rows // rows

        def product(index, carry):
            columns = pl.ds(pl.multiple_of(index * block_rows, block_rows), block_rows)
            result = dot_tn(left_buffer[group % 2, :, columns], right_buffer[at % 2])
            grads[at, pl.ds(index * per, per)] = result.astype(jnp.bfloat16).reshape(per, rows, chunk_width)
            return carry

        lax.fori_loop(0, size // per, product, 0)

    def summed(chunk, block, stage, tile):
        total = grad(chunk)[shard(block), tile, :].astype(jnp.float32)
        for past in range(stage):
            at = blocks(chunk, past).index(block | (1 << orders[chunk][past]))
            total = total + landed[past][chunk, at, tile, :].astype(jnp.float32)
        return total

    def whole(chunk, stage):
        return copy(chunk, stage, landed[stage].at[chunk], landed[stage].at[chunk])

    def small_copy(stage):
        rows = pl.ds(0, small.shape[0] if stage < stages else pair_rows)
        return pltpu.make_async_remote_copy(
            src_ref=(small if stage == 0 else small_sum.at[stage]).at[rows],
            dst_ref=small_landed.at[stage, rows],
            send_sem=small_sent.at[stage],
            recv_sem=small_arrived.at[stage],
            device_id={"batch": shard(2**stage)} if stage < stages else peer,
            device_id_type=pl.DeviceIdType.MESH,
        )

    small_copy(0).start()
    for chunk in range(ready):
        start(chunk)

    step = min(16, rows)
    for chunk, stage in events:
        if chunk < 0:
            small_copy(stage - 1).wait_recv()
            held = small[...] if stage == 1 else small_sum[stage - 1]
            if stage <= stages:
                small_sum[stage] = held + small_landed[stage - 1]
                small_copy(stage).start()
            else:
                small_out[:pair_rows, :] = held[:pair_rows] + small_landed[stages, :pair_rows, :]
                small_out[pair_rows:, :] = held[pair_rows:]
            continue
        if stage == 0:
            make(chunk - ready)
            start(chunk)
            continue
        whole(chunk, stage - 1).wait_recv()

        def work(tile_index, carry, chunk=chunk, stage=stage):
            tile = pl.ds(pl.multiple_of(tile_index * step, step), step)
            if stage < stages:
                for at, block in enumerate(blocks(chunk, stage)):
                    landed[stage - 1][chunk, at, tile, :] = summed(chunk, block, stage, tile).astype(jnp.bfloat16)
            else:
                out[tile, pl.ds(chunk * chunk_width, chunk_width)] = summed(chunk, 0, stage, tile)
            return carry

        lax.fori_loop(0, rows // step, work, 0)
        if stage < stages:
            half = size >> (stage + 1)
            copy(chunk, stage, landed[stage - 1].at[chunk, pl.ds(0, half)], landed[stage].at[chunk]).start()
    for stage in range(stages + 1):
        small_copy(stage).wait_send()
    for chunk in range(chunks):
        for stage in range(stages):
            whole(chunk, stage).wait_send()


def reduce_rows(products, given, small, pair_rows):
    size = lax.axis_size("batch")
    stages = size.bit_length() - 1
    rows = given[0].shape[0] // size
    sources, pieces = [], []
    for group, (left, rights) in enumerate(products):
        left_at = tuple(range(len(sources), len(sources) + len(left)))
        sources.extend(left)
        for right, first in rights:
            right_at = tuple(range(len(sources), len(sources) + len(right)))
            sources.extend(right)
            pieces += [(left_at, right_at, begin, group) for begin in range(first, right[0].shape[1], chunk_width)]
    frames = sum(part.shape[0] for part in products[0][0])
    chunks = len(given) + len(pieces)
    landings = [pltpu.VMEM((chunks, size >> (stage + 1), rows, chunk_width), jnp.bfloat16) for stage in range(stages)]
    vmem = pl.BlockSpec(memory_space=pltpu.VMEM)
    return pl.pallas_call(
        functools.partial(reduce_kernel, size, len(given), pieces, pair_rows, len(sources)),
        out_shape=(
            jax.ShapeDtypeStruct((rows, chunks * chunk_width), jnp.float32),
            jax.ShapeDtypeStruct(small.shape, jnp.float32),
        ),
        in_specs=[pl.BlockSpec(memory_space=pl.ANY)] * len(sources) + [vmem] * (len(given) + 1),
        out_specs=(vmem, vmem),
        scratch_shapes=[
            pltpu.VMEM((len(pieces), size, rows, chunk_width), jnp.bfloat16),
            pltpu.VMEM((2, frames, given[0].shape[0]), jnp.bfloat16),
            pltpu.VMEM((2, frames, chunk_width), jnp.bfloat16),
        ]
        + landings
        + [pltpu.VMEM((stages + 1,) + small.shape, jnp.float32)] * 2
        + [pltpu.SemaphoreType.DMA((chunks, stages))] * 2
        + [pltpu.SemaphoreType.DMA((stages + 1,))] * 2
        + [pltpu.SemaphoreType.DMA((2, 2))] * 2,
        compiler_params=pltpu.CompilerParams(
            collective_id=1, has_side_effects=True, vmem_limit_bytes=60 * 1024 * 1024
        ),
        name="reduce_rows",
    )(*sources, *[grad.reshape(size, rows, grad.shape[1]) for grad in given], small)


def finish_sums(products, given, small, pair_rows):
    if given[0].shape[0] // lax.axis_size("batch") % 16 == 0:
        return reduce_rows(products, given, small, pair_rows)
    grads = list(given)
    for left, rights in products:
        for right, first in rights:
            if len(right) < len(left):
                right = split_own(right[0])
            part = sum(contract_rows(at, other[:, first:]) for at, other in zip(left, right))
            grads.append(part.astype(jnp.bfloat16))
    small = exchange(small, "batch")
    paired = exchange(small[:pair_rows], "tensor")
    return scatter_batch(jnp.concatenate(grads, axis=1)), jnp.concatenate([paired, small[pair_rows:]])


def relative_table(slot_frames, model_width):
    step = min(32, slot_frames)
    column = np.arange(model_width)
    freqs = np.exp((column // 2) * (-2.0 * math.log(10000.0) / model_width))
    coarse = (slot_frames - 1 - step * np.arange(2 * slot_frames // step))[:, None] * freqs + (column % 2) * (
        np.pi / 2
    )
    fine = np.arange(step)[:, None] * freqs
    parts = [jnp.asarray(part, jnp.float32) for part in (np.sin(coarse), np.cos(coarse), np.cos(fine), np.sin(fine))]
    table = parts[0][:, None, :] * parts[2][None] - parts[1][:, None, :] * parts[3][None]
    return table.reshape(2 * slot_frames, model_width).astype(jnp.bfloat16)


def dot_nn(a, b):
    return lax.dot_general(a, b, (((1,), (0,)), ((), ())), preferred_element_type=jnp.float32)
def dot_nt(a, b):
    return lax.dot_general(a, b, (((1,), (1,)), ((), ())), preferred_element_type=jnp.float32)
def dot_tn(a, b):
    return lax.dot_general(a, b, (((0,), (0,)), ((), ())), preferred_element_type=jnp.float32)

def flip_rows(x):
    order = 7 - lax.broadcasted_iota(jnp.int32, (8, x.shape[1]), 0)
    return jnp.concatenate(
        [jnp.take_along_axis(x[at : at + 8], order, axis=0) for at in range(x.shape[0] - 8, -8, -8)], axis=0)

def attend_kernel(frames, block, lengths, content, position, keys, values, table, context, probs):
    wide_len = frames + block
    start = pl.multiple_of(frames - block - pl.program_id(1) * block, block)
    window = table[pl.ds(start, wide_len), :]
    wide = dot_nt(position[...], window)
    skewed = pltpu.roll(wide, frames + 1, 1, stride=1, stride_axis=0)[:, :frames]
    raw = (dot_nt(content[...], keys[...]) + skewed) * (content.shape[1] ** -0.5)
    live = lax.broadcasted_iota(jnp.int32, (1, frames), 1) < lengths[0]
    scores = jnp.where(live, raw, -jnp.inf)
    weight = jnp.exp(scores - jnp.max(scores, axis=1, keepdims=True))
    soft = (weight / jnp.sum(weight, axis=1, keepdims=True)).astype(jnp.bfloat16)
    probs[0] = soft
    context[...] = dot_nn(soft, values[...]).astype(jnp.bfloat16)

def attend(lengths, content, position, keys, values, table, head, block):
    frames, width = content.shape
    heads = width // head
    rows = pl.BlockSpec((block, head), lambda h, i, *_: (i, h))
    whole = pl.BlockSpec((frames, head), lambda h, i, *_: (0, h))
    return pl.pallas_call(
        functools.partial(attend_kernel, frames, block),
        out_shape=(jax.ShapeDtypeStruct((frames, width), jnp.bfloat16), jax.ShapeDtypeStruct((heads, frames, frames), jnp.bfloat16)),
        grid_spec=pltpu.PrefetchScalarGridSpec(
            num_scalar_prefetch=1, grid=(heads, frames // block),
            in_specs=[rows, rows, whole, whole, pl.BlockSpec((2 * frames, head), lambda h, i, *_: (0, h))],
            out_specs=[rows, pl.BlockSpec((1, block, frames), lambda h, i, *_: (h, i, 0))]),
        compiler_params=pltpu.CompilerParams(vmem_limit_bytes=24 * 1024 * 1024),
        name="attend",
    )(lengths, content, position, keys, values, table)

def attend_back_kernel(frames, block, probs, grad_context, content, position, keys, values, table, grad_query, grad_keys, grad_values, grad_table, grad_bias, key_sum, value_sum, table_sum):
    wide_len = frames + block
    step = pl.program_id(1)
    start = pl.multiple_of(frames - block - step * block, block)
    @pl.when(step == 0)
    def _():
        key_sum[...] = jnp.zeros_like(key_sum)
        value_sum[...] = jnp.zeros_like(value_sum)
        table_sum[...] = jnp.zeros_like(table_sum)
        grad_bias[...] = jnp.zeros_like(grad_bias)
    soft = probs[0]
    grad_out = grad_context[...]
    grad_probs = dot_nt(grad_out, values[...])
    wide_soft = soft.astype(jnp.float32)
    delta = jnp.sum(wide_soft * grad_probs, axis=1, keepdims=True)
    grad_raw = wide_soft * (grad_probs - delta) * (content.shape[1] ** -0.5)
    padded = jnp.concatenate([flip_rows(grad_raw), jnp.zeros((block, block), jnp.float32)], axis=1)
    grad_wide = pltpu.roll(padded, 0, 1, stride=1, stride_axis=0).astype(jnp.bfloat16)
    grad_raw = grad_raw.astype(jnp.bfloat16)
    from_content = dot_nn(grad_raw, keys[...])
    from_position = dot_nn(grad_wide, table[pl.ds(start, wide_len), :])
    from_position = flip_rows(from_position)
    grad_query[...] = (from_content + from_position).astype(jnp.bfloat16)
    grad_bias[0:1, :] += jnp.sum(from_content, axis=0, keepdims=True)
    grad_bias[1:2, :] += jnp.sum(from_position, axis=0, keepdims=True)
    key_sum[...] += dot_tn(content[...], grad_raw)
    value_sum[...] += dot_tn(grad_out, soft)
    table_sum[:, pl.ds(start, wide_len)] += dot_tn(flip_rows(position[...].astype(jnp.float32)).astype(jnp.bfloat16), grad_wide)
    @pl.when(step == pl.num_programs(1) - 1)
    def _():
        grad_keys[...] = key_sum[...].T.astype(jnp.bfloat16)
        grad_values[...] = value_sum[...].T.astype(jnp.bfloat16)
        grad_table[...] = table_sum[...].T.astype(jnp.bfloat16)

def attend_back(probs, grad_context, content, position, keys, values, table, head, block):
    frames, width = content.shape
    heads = width // head
    rows = pl.BlockSpec((block, head), lambda h, i: (i, h))
    whole = pl.BlockSpec((frames, head), lambda h, i: (0, h))
    both = pl.BlockSpec((2 * frames, head), lambda h, i: (0, h))
    out = functools.partial(jax.ShapeDtypeStruct, dtype=jnp.bfloat16)
    return pl.pallas_call(
        functools.partial(attend_back_kernel, frames, block),
        out_shape=(out((frames, width)), out((frames, width)), out((frames, width)), out((2 * frames, width)), jax.ShapeDtypeStruct((8, width), jnp.float32)),
        grid=(heads, frames // block),
        in_specs=[pl.BlockSpec((1, block, frames), lambda h, i: (h, i, 0)), rows, rows, rows, whole, whole, both],
        out_specs=[rows, whole, whole, both, pl.BlockSpec((8, head), lambda h, i: (0, h))],
        scratch_shapes=[pltpu.VMEM((head, frames), jnp.float32), pltpu.VMEM((head, frames), jnp.float32), pltpu.VMEM((head, 2 * frames), jnp.float32)],
        compiler_params=pltpu.CompilerParams(vmem_limit_bytes=28 * 1024 * 1024),
        name="attend_back",
    )(probs, grad_context, content, position, keys, values, table)


def ffn_forward(residual, norm_gain, norm_shift, weight_up, weight_down):
    normed, scaled, inv_std = norm_forward(residual, norm_gain, norm_shift)
    act_own = normed.astype(jnp.bfloat16)
    act_peer = swap(act_own)

    def hidden_of(act):
        pre_act = jnp.dot(act, weight_up, preferred_element_type=jnp.float32)
        gate_sig = jax.nn.sigmoid(pre_act)
        slope = gate_sig * (1.0 + pre_act * (1.0 - gate_sig))
        return ((pre_act * gate_sig).astype(jnp.bfloat16), slope.astype(jnp.bfloat16))

    hidden_own, slope_own = hidden_of(act_own)
    hidden_peer, slope_peer = hidden_of(act_peer)
    out_peer = jnp.dot(hidden_peer, weight_down, preferred_element_type=jnp.float32)
    out_own = jnp.dot(hidden_own, weight_down, preferred_element_type=jnp.float32)
    saved = (scaled, inv_std, act_own, act_peer, hidden_own, hidden_peer, slope_own, slope_peer)
    return (narrow(out_own, out_peer), saved)


def ffn_backward(grad_after, saved, norm_gain, weight_up, weight_down):
    scaled, inv_std, act_own, act_peer, hidden_own, hidden_peer, slope_own, slope_peer = saved
    grad_own = grad_after.astype(jnp.bfloat16)
    grad_peer = swap(grad_own)
    pre_own = (times_transposed(grad_own, weight_down) * slope_own.astype(jnp.float32)).astype(jnp.bfloat16)
    pre_peer = (times_transposed(grad_peer, weight_down) * slope_peer.astype(jnp.float32)).astype(jnp.bfloat16)
    back_peer = times_transposed(pre_peer, weight_up)
    back_own = times_transposed(pre_own, weight_up)

    grad_resid, grad_gain, grad_shift = norm_backward(
        narrow(back_own, back_peer), scaled, inv_std, norm_gain
    )
    operands = (
        ((act_own, act_peer), (pre_own, pre_peer)),
        ((grad_own, grad_peer), (hidden_own, hidden_peer)),
    )
    return (grad_resid, grad_gain, grad_shift, operands)


def attn_forward(
    residual,
    norm_gain,
    norm_shift,
    attention_in,
    position_proj,
    position_bias,
    attention_out,
    lengths,
):
    normed, scaled, inv_std = norm_forward(residual, norm_gain, norm_shift)
    own = normed.astype(jnp.bfloat16)
    peer = swap(own)
    flat_act = in_order(own, peer)
    slot_frames, model_width = flat_act.shape
    head_count, head_size = (position_bias.shape[1], position_bias.shape[2])
    local_width = head_count * head_size
    projected = [
        jnp.dot(flat_act, attention_in[at], preferred_element_type=jnp.float32) for at in range(3)
    ]
    biases = position_bias.astype(jnp.float32).reshape(2, 1, local_width)
    query_content = (projected[0] + biases[0]).astype(jnp.bfloat16)
    query_position = (projected[0] + biases[1]).astype(jnp.bfloat16)
    key_all = projected[1].astype(jnp.bfloat16)
    value_all = projected[2].astype(jnp.bfloat16)
    table_in = relative_table(slot_frames, model_width)
    table = jnp.dot(table_in, position_proj, preferred_element_type=jnp.float32).astype(jnp.bfloat16)
    context, probs = attend(
        lengths, query_content, query_position, key_all, value_all, table, head_size, min(512, slot_frames)
    )
    context_own, context_peer = split_own(context)
    out_peer = jnp.dot(context_peer, attention_out, preferred_element_type=jnp.float32)
    out_own = jnp.dot(context_own, attention_out, preferred_element_type=jnp.float32)
    saved = (
        scaled,
        inv_std,
        (own, peer),
        query_content,
        query_position,
        key_all,
        value_all,
        table_in,
        table,
        context,
        probs,
    )
    return (narrow(out_own, out_peer), saved)


def attn_backward(grad_after, saved, norm_gain, attention_in, attention_out, head_count, head_size):
    (
        scaled,
        inv_std,
        flat_act,
        query_content,
        query_position,
        key_all,
        value_all,
        table_in,
        table,
        context,
        probs,
    ) = saved
    grad_own = grad_after.astype(jnp.bfloat16)
    grad_peer = swap(grad_own)
    grad_flat = in_order(grad_own, grad_peer)
    slot_frames = grad_flat.shape[0]
    back_product = ((grad_own, grad_peer), [((context,), 0)])
    grad_context = times_transposed(grad_flat, attention_out).astype(jnp.bfloat16)
    grad_query, grad_keys, grad_values, grad_table, grad_bias = attend_back(
        probs,
        grad_context,
        query_content,
        query_position,
        key_all,
        value_all,
        table,
        head_size,
        min(512, slot_frames),
    )
    grad_bias = grad_bias[:2].reshape(2, head_count, head_size)
    grad_proj = (grad_query, grad_keys, grad_values)
    halves = [split_own(part) for part in grad_proj]
    back_own, back_peer = (
        sum(times_transposed(half[side], attention_in[at]) for at, half in enumerate(halves))
        for side in (0, 1)
    )
    in_product = (flat_act, [((part,), 0) for part in grad_proj])
    grad_table_proj = contract_rows(table_in, grad_table)
    grad_resid, grad_gain, grad_shift = norm_backward(
        narrow(back_own, back_peer), scaled, inv_std, norm_gain
    )
    return (
        grad_resid,
        grad_gain,
        grad_shift,
        in_product,
        grad_table_proj,
        grad_bias,
        back_product,
    )


def conv_forward(
    residual,
    norm_gain,
    norm_shift,
    pointwise_in,
    depthwise,
    batch_gain,
    batch_shift,
    pointwise_out,
    slot_count,
    live_full,
):
    normed, scaled, inv_std = norm_forward(residual, norm_gain, norm_shift)
    own = normed.astype(jnp.bfloat16)
    peer = swap(own)
    flat_act = in_order(own, peer)
    slot_frames = flat_act.shape[0]
    joined = pointwise_in.reshape(pointwise_in.shape[0], -1)
    both_halves = jnp.split(jnp.dot(flat_act, joined, preferred_element_type=jnp.float32), 2, axis=1)
    gate_sig = jax.nn.sigmoid(both_halves[1])
    gated = both_halves[0] * gate_sig * live_full
    channels = gated.shape[1]
    kernel = depthwise.astype(jnp.float32)
    tap_count = kernel.shape[0]
    half_taps = tap_count // 2
    padded = jnp.pad(gated, ((half_taps, half_taps), (0, 0)))
    mixed_conv = padded[0:slot_frames] * kernel[0]
    for tap_index in range(1, tap_count):
        mixed_conv = mixed_conv + padded[tap_index : tap_index + slot_frames] * kernel[tap_index]
    totals = share(
        jnp.stack(
            [
                jnp.sum(mixed_conv * live_full, axis=0),
                jnp.sum(mixed_conv * mixed_conv * live_full, axis=0),
                jnp.broadcast_to(slot_count, (channels,)),
            ]
        )
    )
    frame_count = totals[2, 0]
    batch_mean = totals[0] / frame_count
    batch_inv = lax.rsqrt(totals[1] / frame_count - batch_mean * batch_mean + eps_batch)
    centered = (mixed_conv - batch_mean) * batch_inv
    normed_batch = centered * batch_gain.astype(jnp.float32) + batch_shift.astype(jnp.float32)
    batch_sig = jax.nn.sigmoid(normed_batch)
    swished = (normed_batch * batch_sig).astype(jnp.bfloat16)
    swished_own, swished_peer = split_own(swished)
    out_peer = jnp.dot(swished_peer, pointwise_out, preferred_element_type=jnp.float32)
    out_own = jnp.dot(swished_own, pointwise_out, preferred_element_type=jnp.float32)
    saved = (
        scaled,
        inv_std,
        (own, peer),
        both_halves,
        gate_sig,
        padded,
        centered,
        batch_inv,
        frame_count,
        normed_batch,
        batch_sig,
        swished,
    )
    return (narrow(out_own, out_peer), saved)


def conv_backward(
    grad_after, saved, norm_gain, pointwise_in, depthwise, batch_gain, pointwise_out, live_full
):
    (
        scaled,
        inv_std,
        flat_act,
        both_halves,
        gate_sig,
        padded,
        centered,
        batch_inv,
        frame_count,
        normed_batch,
        batch_sig,
        swished,
    ) = saved
    grad_own = grad_after.astype(jnp.bfloat16)
    grad_peer = swap(grad_own)
    grad_flat = in_order(grad_own, grad_peer)
    slot_frames = grad_flat.shape[0]
    out_product = ((grad_own, grad_peer), [((swished,), 0)])
    grad_swished = times_transposed(grad_flat, pointwise_out)
    grad_normed = grad_swished * batch_sig * (1.0 + normed_batch * (1.0 - batch_sig))
    sums = share(jnp.stack([jnp.sum(grad_normed, axis=0), jnp.sum(grad_normed * centered, axis=0)]))
    gamma = batch_gain.astype(jnp.float32)
    grad_mixed = batch_inv * (
        grad_normed * gamma
        - live_full * (gamma * sums[0] + centered * gamma * sums[1]) / frame_count
    )
    channels = grad_mixed.shape[1]
    kernel = depthwise.astype(jnp.float32)
    tap_count = kernel.shape[0]
    half_taps = tap_count // 2
    grad_kernel = jnp.stack(
        [
            jnp.sum(grad_mixed * padded[tap_index : tap_index + slot_frames], axis=0)
            for tap_index in range(tap_count)
        ]
    )
    spread = jnp.pad(grad_mixed, ((half_taps, half_taps), (0, 0)))
    grad_gated = spread[2 * half_taps : 2 * half_taps + slot_frames] * kernel[0]
    for tap_index in range(1, tap_count):
        begin = 2 * half_taps - tap_index
        grad_gated = grad_gated + spread[begin : begin + slot_frames] * kernel[tap_index]
    grad_gated = grad_gated * live_full
    grad_halves = [
        (grad_gated * gate_sig).astype(jnp.bfloat16),
        (grad_gated * both_halves[0] * gate_sig * (1.0 - gate_sig)).astype(jnp.bfloat16),
    ]
    in_product = (flat_act, [((part,), 0) for part in grad_halves])
    joined = jnp.split(pointwise_in.reshape(pointwise_in.shape[0], -1), 2, axis=1)
    halves = [split_own(part) for part in grad_halves]
    back_own, back_peer = (
        sum(times_transposed(half[side], joined[at]) for at, half in enumerate(halves))
        for side in (0, 1)
    )
    grad_resid, grad_gain, grad_shift = norm_backward(
        narrow(back_own, back_peer), scaled, inv_std, norm_gain
    )
    return (grad_resid, grad_gain, grad_shift, in_product, out_product, grad_kernel, sums)


def per_device(
    features,
    lengths,
    norm_gains,
    norm_shifts,
    first_up,
    first_down,
    attention_in,
    position_proj,
    position_bias,
    attention_out,
    pointwise_in,
    depthwise,
    batch_gain,
    batch_shift,
    pointwise_out,
    second_up,
    second_down,
    cotangent,
):
    slot_count, half_frames, model_width = features.shape
    slot_frames = half_frames * lax.axis_size("tensor")
    positions = lax.broadcasted_iota(jnp.int32, (half_frames, 1), 0) + lax.axis_index("tensor") * half_frames
    live_half = (positions < lengths[0]).astype(jnp.float32)
    full_positions = lax.broadcasted_iota(jnp.int32, (slot_frames, 1), 0)
    live_full = (full_positions < lengths[0]).astype(jnp.float32)
    gain_rows = norm_gains.astype(jnp.float32)
    shift_rows = norm_shifts.astype(jnp.float32)
    stream_zero = features[0].astype(jnp.float32)
    branch_one, saved_one = ffn_forward(
        stream_zero, gain_rows[0], shift_rows[0], first_up, first_down
    )
    stream_one = stream_zero + 0.5 * branch_one
    branch_two, saved_two = attn_forward(
        stream_one,
        gain_rows[1],
        shift_rows[1],
        attention_in,
        position_proj,
        position_bias,
        attention_out,
        lengths,
    )
    stream_two = stream_one + branch_two
    branch_three, saved_three = conv_forward(
        stream_two,
        gain_rows[2],
        shift_rows[2],
        pointwise_in,
        depthwise,
        batch_gain,
        batch_shift,
        pointwise_out,
        lengths[0].astype(jnp.float32),
        live_full,
    )
    stream_three = stream_two + branch_three
    branch_four, saved_four = ffn_forward(
        stream_three, gain_rows[3], shift_rows[3], second_up, second_down
    )
    stream_four = stream_three + 0.5 * branch_four
    final_norm, scaled_final, inv_final = norm_forward(stream_four, gain_rows[4], shift_rows[4])
    output = (final_norm * live_half).astype(jnp.bfloat16)
    grad_final = cotangent[0].astype(jnp.float32) * live_half
    grad_stream, gain_five, shift_five = norm_backward(
        grad_final, scaled_final, inv_final, gain_rows[4]
    )
    grad_branch, gain_four, shift_four, operands_two = ffn_backward(
        0.5 * grad_stream, saved_four, gain_rows[3], second_up, second_down
    )
    grad_stream = grad_stream + grad_branch
    (
        grad_branch,
        gain_three,
        shift_three,
        points_product,
        point_out_product,
        kernel_grad,
        batch_sums,
    ) = conv_backward(
        grad_stream,
        saved_three,
        gain_rows[2],
        pointwise_in,
        depthwise,
        batch_gain,
        pointwise_out,
        live_full,
    )
    grad_stream = grad_stream + grad_branch
    grad_branch, gain_two, shift_two, heads_product, table_grad, bias_grad, back_product = attn_backward(
        grad_stream,
        saved_two,
        gain_rows[1],
        attention_in,
        attention_out,
        position_bias.shape[1],
        position_bias.shape[2],
    )
    grad_stream = grad_stream + grad_branch
    grad_branch, gain_one, shift_one, operands_one = ffn_backward(
        0.5 * grad_stream, saved_one, gain_rows[0], first_up, first_down
    )
    grad_stream = grad_stream + grad_branch
    gain_grads = jnp.stack([gain_one, gain_two, gain_three, gain_four, gain_five])
    shift_grads = jnp.stack([shift_one, shift_two, shift_three, shift_four, shift_five])
    norms, channels = gain_grads.shape[0], kernel_grad.shape[1]
    packed = jnp.concatenate([kernel_grad, bias_grad.reshape(2, channels)]).reshape(-1)
    packed = jnp.pad(packed, (0, -packed.shape[0] % (8 * model_width))).reshape(-1, model_width)
    pair_rows = 2 * norms + -2 * norms % 8
    norm_grads = jnp.pad(jnp.concatenate([gain_grads, shift_grads]), ((0, pair_rows - 2 * norms), (0, 0)))
    sums, small = finish_sums(
        [
            (operands_two[0][0], [(operands_two[0][1], 0)]),
            (operands_two[1][0], [(operands_two[1][1], 0)]),
            points_product,
            point_out_product,
            heads_product,
            back_product,
            (operands_one[0][0], [(operands_one[0][1], 0)]),
            (operands_one[1][0], [(operands_one[1][1], 0)]),
        ],
        [table_grad.astype(jnp.bfloat16)],
        jnp.concatenate([norm_grads, packed]),
        pair_rows,
    )
    gain_grads, shift_grads = small[:norms], small[norms : 2 * norms]
    packed = small[pair_rows:].reshape(-1)
    kernel_grad = packed[: kernel_grad.size].reshape(kernel_grad.shape)
    bias_grad = packed[kernel_grad.size : kernel_grad.size + bias_grad.size].reshape(bias_grad.shape)
    def take(width):
        nonlocal sums
        taken, sums = sums[:, :width], sums[:, width:]
        return taken

    hidden = first_up.shape[1]
    table_grad = take(channels)
    up_two, down_two = take(hidden), take(hidden).T
    point_in_grad = jnp.stack([take(channels) for _ in range(2)], axis=1)
    point_out_grad = take(channels).T
    heads_grad = jnp.stack([take(channels) for _ in range(3)])
    back_grad = take(channels).T
    up_one, down_one = take(hidden), take(hidden).T
    return (
        output[None],
        grad_stream[None],
        gain_grads,
        shift_grads,
        up_one,
        down_one,
        heads_grad,
        table_grad,
        bias_grad,
        back_grad,
        point_in_grad,
        kernel_grad,
        batch_sums[1],
        batch_sums[0],
        point_out_grad,
        up_two,
        down_two,
    )


def solution(mesh):
    in_specs = (
        P("batch", "tensor", None),
        P("batch"),
        P(),
        P(),
        P(None, "tensor"),
        P("tensor", None),
        P(None, None, "tensor"),
        P(None, "tensor"),
        P(None, "tensor", None),
        P("tensor", None),
        P(None, None, "tensor"),
        P(None, "tensor"),
        P("tensor"),
        P("tensor"),
        P("tensor", None),
        P(None, "tensor"),
        P("tensor", None),
        P("batch", "tensor", None),
    )
    out_specs = (
        P("batch", "tensor", None),
        P("batch", "tensor", None),
        P(),
        P(),
        P("batch", "tensor"),
        P("tensor", "batch"),
        P(None, "batch", "tensor"),
        P("batch", "tensor"),
        P(None, "tensor", None),
        P("tensor", "batch"),
        P("batch", None, "tensor"),
        P(None, "tensor"),
        P("tensor"),
        P("tensor"),
        P("tensor", "batch"),
        P("batch", "tensor"),
        P("tensor", "batch"),
    )
    return jax.shard_map(
        per_device, mesh=mesh, in_specs=in_specs, out_specs=out_specs, check_vma=False
    )
```
